128 devices in a mesh: frame: 8 (over x_hi, z), pos: 16 (over y, x_lo, core).
Axes of the slice: x: 4 (x_hi: 2, x_lo: 2; x = x_hi * 2 + x_lo), y: 4, z: 4, core: 2. Of those that a mesh axis runs over, the one named last changes fastest.
Arguments:
- latents: bfloat16 [256, 1024, 256], P('frame', 'pos'), as said below
- gain_one: float32 [256], replicated, may hold values from 0.5 to 1.5
- query_one: bfloat16 [256, 256], replicated, as said below
- key_one: bfloat16 [256, 256], replicated, as said below
- value_one: bfloat16 [256, 256], replicated, may hold values from -0.375 to 0.375
- out_one: bfloat16 [256, 256], replicated, may hold values from -0.75 to 0.75
- gain_two: float32 [256], replicated, may hold values from 0.5 to 1.5
- query_two: bfloat16 [256, 256], replicated, as said below
- key_two: bfloat16 [256, 256], replicated, as said below
- value_two: bfloat16 [256, 256], replicated, may hold values from -0.375 to 0.375
- out_two: bfloat16 [256, 256], replicated, may hold values from -0.75 to 0.75
Outputs:
- decoded: bfloat16 [256, 1024, 256], P('frame', 'pos')
The draws below stay inside these ranges and needn't reach their ends.
Inputs may be any that keep to these rules, and one draw needn't show every extreme that they name: `latents`: latent features of the video. `query_one`: A projection of the spatial block. `key_one`: A projection of the spatial block. `query_two`: A projection of the temporal block. `key_two`: A projection of the temporal block.
All inputs are finite; a program needn't handle non-finite values.
Results may differ from the reference program's by a relative error of at most 0.015.
The reference program's roundings to bfloat16 on the way count: a program that leaves them out, or rounds other values in their place, can miss the bound.
Values may be sent and summed in bfloat16 or wider, within the bound.
A program may use at most 320 MiB of HBM per device.

```python
import math
import jax
import jax.numpy as jnp
from jax import lax

C = 256
HEADS = 4
HEAD_DIM = 64
FRAMES = 256
POSITIONS = 1024


def draw_latents(key, part):
    return jax.random.normal(jax.random.fold_in(key, 102), (FRAMES, POSITIONS, C), jnp.float32).astype(jnp.bfloat16)


def attention_weight(key, salt):
    noise = jax.random.normal(jax.random.fold_in(key, salt), (C, C), jnp.float32)
    return (noise * (1.5 / math.sqrt(C))).astype(jnp.bfloat16)


def draw_query_one(key, part):
    return attention_weight(key, 201)


def draw_key_one(key, part):
    return attention_weight(key, 202)


def draw_query_two(key, part):
    return attention_weight(key, 203)


def draw_key_two(key, part):
    return attention_weight(key, 204)


def bell_draw(key, shape, spread, limit, kind=jnp.bfloat16):
    entries = jax.random.normal(key, shape, jnp.float32) * spread
    return jnp.minimum(jnp.maximum(entries, -limit), limit).astype(kind)


def setup_inputs(seed: int = 0) -> dict:
    key_of = jax.random.split(jax.random.key(seed), 12)
    return {
        "latents": draw_latents(jax.random.fold_in(key_of[11], 71), 0),
        "gain_one": jnp.clip(1.0 + 0.1 * jax.random.normal(key_of[1], (C,), jnp.float32), 0.5, 1.5),
        "query_one": draw_query_one(jax.random.fold_in(key_of[11], 71), 0),
        "key_one": draw_key_one(jax.random.fold_in(key_of[11], 71), 0),
        "value_one": bell_draw(key_of[4], (C, C), C ** -0.5, 0.375),
        "out_one": bell_draw(key_of[5], (C, C), (C // 4) ** -0.5, 0.75),
        "gain_two": jnp.clip(1.0 + 0.1 * jax.random.normal(key_of[6], (C,), jnp.float32), 0.5, 1.5),
        "query_two": draw_query_two(jax.random.fold_in(key_of[11], 71), 0),
        "key_two": draw_key_two(jax.random.fold_in(key_of[11], 71), 0),
        "value_two": bell_draw(key_of[9], (C, C), C ** -0.5, 0.375),
        "out_two": bell_draw(key_of[10], (C, C), (C // 4) ** -0.5, 0.75),
    }


def normed(values, gain):
    wide = values.astype(jnp.float32)
    factor = lax.rsqrt(lax.optimization_barrier(jnp.mean(wide * wide, axis=-1, keepdims=True)) + 1e-06)
    return (wide * factor * gain).astype(jnp.bfloat16)

def project(values, weight):
    flat = values.reshape(-1, values.shape[-1])
    result = jnp.dot(flat, weight, preferred_element_type=jnp.float32).astype(jnp.bfloat16)
    return result.reshape(values.shape[:-1] + (weight.shape[1],))

def heads_of(values):
    return values.reshape(values.shape[:-1] + (HEADS, HEAD_DIM))

def rounded_weights(weights):
    return lax.optimization_barrier(weights.astype(jnp.bfloat16)).astype(jnp.float32)

def reference(latents, gain_one, query_one, key_one, value_one, out_one, gain_two, query_two, key_two, value_two, out_two):
    scale = HEAD_DIM ** (-0.5)
    normed_one = normed(latents, gain_one)
    q_one = heads_of(project(normed_one, query_one))
    k_one = heads_of(project(normed_one, key_one))
    v_one = heads_of(project(normed_one, value_one))

    def spatial(index):
        query = q_one[index].astype(jnp.float32)
        keys = jnp.concatenate([k_one[index], k_one[0]], axis=0).astype(jnp.float32)
        vals = jnp.concatenate([v_one[index], v_one[0]], axis=0).astype(jnp.float32)
        scores = jnp.einsum('phd,khd->hpk', query, keys) * scale
        weights = jnp.exp(scores - lax.optimization_barrier(jnp.max(scores, axis=-1, keepdims=True)))
        totals = lax.optimization_barrier(jnp.sum(weights, axis=-1))
        summed = jnp.einsum('hpk,khd->phd', rounded_weights(weights), vals)
        return (summed / totals.T[:, :, None]).reshape(POSITIONS, C).astype(jnp.bfloat16)
    attended_one = lax.map(spatial, jnp.arange(FRAMES, dtype=jnp.int32))
    mid = (latents.astype(jnp.float32) + jnp.dot(attended_one.reshape(-1, C), out_one, preferred_element_type=jnp.float32).reshape(FRAMES, POSITIONS, C)).astype(jnp.bfloat16)
    normed_two = normed(mid, gain_two)
    q_two = heads_of(project(normed_two, query_two)).transpose(1, 0, 2, 3)
    k_two = heads_of(project(normed_two, key_two)).transpose(1, 0, 2, 3)
    v_two = heads_of(project(normed_two, value_two)).transpose(1, 0, 2, 3)

    def temporal(operands):
        query, keys, vals = operands
        scores = jnp.einsum('fhd,khd->hfk', query.astype(jnp.float32), keys.astype(jnp.float32)) * scale
        weights = jnp.exp(scores - lax.optimization_barrier(jnp.max(scores, axis=-1, keepdims=True)))
        totals = lax.optimization_barrier(jnp.sum(weights, axis=-1))
        summed = jnp.einsum('hfk,khd->fhd', rounded_weights(weights), vals.astype(jnp.float32))
        return (summed / totals.T[:, :, None]).reshape(FRAMES, C).astype(jnp.bfloat16)
    attended_two = lax.map(temporal, (q_two, k_two, v_two)).transpose(1, 0, 2)
    mixed = jnp.dot(attended_two.reshape(-1, C), out_two, preferred_element_type=jnp.float32).reshape(FRAMES, POSITIONS, C)
    return (mid.astype(jnp.float32) + mixed).astype(jnp.bfloat16)
```

```python
import jax
import jax.numpy as jnp
from jax import lax
from jax.sharding import PartitionSpec as P

HEADS = 4


def normed(values, gain):
    wide = values.astype(jnp.float32)
    factor = lax.rsqrt(jnp.mean(wide * wide, axis=-1, keepdims=True) + 1e-06)
    return (wide * factor * gain).astype(jnp.bfloat16)


def project(values, weight):
    flat = values.reshape(-1, values.shape[-1])
    result = jnp.dot(flat, weight, preferred_element_type=jnp.float32).astype(jnp.bfloat16)
    return result.reshape(values.shape[:-1] + (weight.shape[1],))


def heads_of(values):
    return values.reshape(values.shape[:-1] + (HEADS, values.shape[-1] // HEADS))


def softmax_attend(query, keys, vals, score_form, value_form, total_form):
    scale = query.shape[-1] ** (-0.5)
    scores = jnp.einsum(score_form, query, keys, preferred_element_type=jnp.float32) * scale
    weights = jnp.exp(scores - jnp.max(scores, axis=-1, keepdims=True))
    totals = jnp.sum(weights, axis=-1)
    summed = jnp.einsum(
        value_form, weights.astype(jnp.bfloat16), vals, preferred_element_type=jnp.float32
    )
    return summed / jnp.einsum(total_form, totals)[..., None]


def shards(
    latents,
    gain_one,
    query_one,
    key_one,
    value_one,
    out_one,
    gain_two,
    query_two,
    key_two,
    value_two,
    out_two,
):
    frames, places, width = latents.shape
    n_pos = lax.axis_size("pos")
    n_frame = lax.axis_size("frame")
    per = frames // n_pos
    first = jnp.where(lax.axis_index("frame") == 0, latents[0], 0).astype(latents.dtype)
    first = lax.psum(first, "frame")
    sent = jnp.concatenate(
        [
            latents.reshape(n_pos, per, places, width),
            jnp.broadcast_to(first[None, None], (n_pos, 1, places, width)),
        ],
        axis=1,
    )
    got = lax.all_to_all(sent, "pos", 0, 0, tiled=True)
    xs = got[:, :per].transpose(1, 0, 2, 3).reshape(per, n_pos * places, width)
    x0 = got[:, per].reshape(n_pos * places, width)

    n_one = normed(xs, gain_one)
    q_one = heads_of(project(n_one, query_one))
    k_one = heads_of(project(n_one, key_one))
    v_one = heads_of(project(n_one, value_one))
    n_zero = normed(x0, gain_one)
    k_zero = heads_of(project(n_zero, key_one))
    v_zero = heads_of(project(n_zero, value_one))
    keys = jnp.concatenate([k_one, jnp.broadcast_to(k_zero[None], k_one.shape)], axis=1)
    vals = jnp.concatenate([v_one, jnp.broadcast_to(v_zero[None], v_one.shape)], axis=1)
    attended_one = softmax_attend(
        q_one, keys, vals, "fphd,fkhd->fhpk", "fhpk,fkhd->fphd", "fhp->fph"
    ).reshape(xs.shape).astype(jnp.bfloat16)
    mixed_one = jnp.dot(
        attended_one.reshape(-1, width), out_one, preferred_element_type=jnp.float32
    ).reshape(xs.shape)
    middle = (xs.astype(jnp.float32) + mixed_one).astype(jnp.bfloat16)

    all_places = n_pos * places
    run = all_places // (n_pos * n_frame)
    sent = (
        middle.reshape(per, n_pos, n_frame, run, width)
        .transpose(2, 1, 0, 3, 4)
        .reshape(n_frame * n_pos, per, run, width)
    )
    got = lax.all_to_all(sent, ("frame", "pos"), 0, 0, tiled=True)
    mid_t = got.reshape(n_frame * n_pos * per, run, width)

    n_two = normed(mid_t, gain_two)
    q_two = heads_of(project(n_two, query_two))
    k_two = heads_of(project(n_two, key_two))
    v_two = heads_of(project(n_two, value_two))
    attended_two = softmax_attend(
        q_two, k_two, v_two, "fphd,kphd->phfk", "phfk,kphd->fphd", "phf->fph"
    ).reshape(mid_t.shape).astype(jnp.bfloat16)
    mixed_two = jnp.dot(
        attended_two.reshape(-1, width), out_two, preferred_element_type=jnp.float32
    ).reshape(mid_t.shape)
    decoded = (mid_t.astype(jnp.float32) + mixed_two).astype(jnp.bfloat16)

    sent = decoded.reshape(n_frame, frames, run, width)
    got = lax.all_to_all(sent, "frame", 0, 0, tiled=True)
    return got.transpose(1, 0, 2, 3).reshape(frames, places, width)


def solution(mesh):
    return jax.shard_map(
        shards,
        mesh=mesh,
        in_specs=(P("frame", "pos", None), P(), P(), P(), P(), P(), P(), P(), P(), P(), P()),
        out_specs=P("frame", "pos", None),
        check_vma=False,
    )
```

```python
import jax
import jax.numpy as jnp
from jax import lax
from jax.experimental import pallas as pl
from jax.experimental.pallas import tpu as pltpu
from jax.sharding import PartitionSpec as P

HEADS = 4

MESH = pl.DeviceIdType.MESH


def exchange(x, names, sizes, cid):
    n = x.shape[0]

    def where(peer):
        if len(names) == 1:
            return {names[0]: peer}
        return {names[0]: peer // sizes[1], names[1]: peer % sizes[1]}

    def kernel(x_ref, o_ref, send_sem, recv_sem):
        me = lax.axis_index(names[0])
        if len(names) == 2:
            me = me * sizes[1] + lax.axis_index(names[1])
        barrier = pltpu.get_barrier_semaphore()
        for k in range(1, n):
            pl.semaphore_signal(barrier, inc=1, device_id=where((me + k) % n), device_id_type=MESH)
        pl.semaphore_wait(barrier, n - 1)
        copies = []
        for k in range(1, n):
            peer = (me + k) % n
            copy = pltpu.make_async_remote_copy(
                src_ref=x_ref.at[peer],
                dst_ref=o_ref.at[me],
                send_sem=send_sem.at[k],
                recv_sem=recv_sem.at[k],
                device_id=where(peer),
                device_id_type=MESH,
            )
            copy.start()
            copies.append(copy)
        o_ref[me] = x_ref[me]
        for copy in copies:
            copy.wait()

    return pl.pallas_call(
        kernel,
        out_shape=jax.ShapeDtypeStruct(x.shape, x.dtype),
        in_specs=[pl.BlockSpec(memory_space=pltpu.VMEM)],
        out_specs=pl.BlockSpec(memory_space=pltpu.VMEM),
        scratch_shapes=[pltpu.SemaphoreType.DMA((n,)), pltpu.SemaphoreType.DMA((n,))],
        compiler_params=pltpu.CompilerParams(collective_id=cid, has_side_effects=True),
    )(x)


def spatial_exchange(x, n_pos, n_frame, cid):
    _, per, places, width = x.shape

    def kernel(x_ref, o_ref, z_ref, send_sem, recv_sem, fsend_sem, frecv_sem, zsend_sem, zrecv_sem, local_sem):
        fi = lax.axis_index("frame")
        pi = lax.axis_index("pos")
        barrier = pltpu.get_barrier_semaphore()
        for k in range(1, n_pos):
            pl.semaphore_signal(barrier, inc=1, device_id={"pos": (pi + k) % n_pos}, device_id_type=MESH)
        for g in range(1, n_frame):
            pl.semaphore_signal(barrier, inc=1, device_id={"frame": (fi + g) % n_frame}, device_id_type=MESH)
        pl.semaphore_wait(barrier, n_pos - 1 + n_frame - 1)
        copies = []
        for k in range(1, n_pos):
            peer = (pi + k) % n_pos
            copy = pltpu.make_async_remote_copy(
                src_ref=x_ref.at[peer],
                dst_ref=o_ref.at[pi],
                send_sem=send_sem.at[k],
                recv_sem=recv_sem.at[k],
                device_id={"pos": peer},
                device_id_type=MESH,
            )
            copy.start()
            copies.append(copy)
        o_ref[pi] = x_ref[pi]

        def spread(g):
            return pltpu.make_async_remote_copy(
                src_ref=x_ref.at[0, 0],
                dst_ref=z_ref.at[pi],
                send_sem=fsend_sem.at[g],
                recv_sem=frecv_sem,
                device_id={"frame": g},
                device_id_type=MESH,
            )

        @pl.when(fi == 0)
        def _():
            local = pltpu.make_async_copy(x_ref.at[0, 0], z_ref.at[pi], local_sem)
            local.start()
            sends = [spread(g) for g in range(1, n_frame)]
            for send in sends:
                send.start()
            local.wait()
            for send in sends:
                send.wait_send()

        @pl.when(fi != 0)
        def _():
            spread(1).wait_recv()

        for k in range(1, n_pos):
            peer = (pi + k) % n_pos
            copy = pltpu.make_async_remote_copy(
                src_ref=z_ref.at[pi],
                dst_ref=z_ref.at[pi],
                send_sem=zsend_sem.at[k],
                recv_sem=zrecv_sem.at[k],
                device_id={"pos": peer},
                device_id_type=MESH,
            )
            copy.start()
            copies.append(copy)
        for copy in copies:
            copy.wait()

    return pl.pallas_call(
        kernel,
        out_shape=(
            jax.ShapeDtypeStruct(x.shape, x.dtype),
            jax.ShapeDtypeStruct((n_pos, places, width), x.dtype),
        ),
        in_specs=[pl.BlockSpec(memory_space=pltpu.VMEM)],
        out_specs=(pl.BlockSpec(memory_space=pltpu.VMEM), pl.BlockSpec(memory_space=pltpu.VMEM)),
        scratch_shapes=[
            pltpu.SemaphoreType.DMA((n_pos,)),
            pltpu.SemaphoreType.DMA((n_pos,)),
            pltpu.SemaphoreType.DMA((n_frame,)),
            pltpu.SemaphoreType.DMA,
            pltpu.SemaphoreType.DMA((n_pos,)),
            pltpu.SemaphoreType.DMA((n_pos,)),
            pltpu.SemaphoreType.DMA,
        ],
        compiler_params=pltpu.CompilerParams(collective_id=cid, has_side_effects=True),
    )(x)


def normed(values, gain):
    wide = values.astype(jnp.float32)
    factor = lax.rsqrt(jnp.mean(wide * wide, axis=-1, keepdims=True) + 1e-06)
    return (wide * factor * gain).astype(jnp.bfloat16)


def project(values, weight):
    flat = values.reshape(-1, values.shape[-1])
    result = jnp.dot(flat, weight, preferred_element_type=jnp.float32).astype(jnp.bfloat16)
    return result.reshape(values.shape[:-1] + (weight.shape[1],))


def heads_of(values):
    return values.reshape(values.shape[:-1] + (HEADS, values.shape[-1] // HEADS))


def softmax_attend(query, keys, vals, score_form, value_form, total_form):
    scale = query.shape[-1] ** (-0.5)
    scores = jnp.einsum(score_form, query, keys, preferred_element_type=jnp.float32) * scale
    weights = jnp.exp(scores - jnp.max(scores, axis=-1, keepdims=True))
    totals = jnp.sum(weights, axis=-1)
    summed = jnp.einsum(
        value_form, weights.astype(jnp.bfloat16), vals, preferred_element_type=jnp.float32
    )
    return summed / jnp.einsum(total_form, totals)[..., None]


def shards(
    latents,
    gain_one,
    query_one,
    key_one,
    value_one,
    out_one,
    gain_two,
    query_two,
    key_two,
    value_two,
    out_two,
):
    frames, places, width = latents.shape
    n_pos = lax.axis_size("pos")
    n_frame = lax.axis_size("frame")
    per = frames // n_pos
    got, zero = spatial_exchange(latents.reshape(n_pos, per, places, width), n_pos, n_frame, 1)
    xs = got.transpose(1, 0, 2, 3).reshape(per, n_pos * places, width)
    x0 = zero.reshape(n_pos * places, width)

    n_one = normed(xs, gain_one)
    q_one = heads_of(project(n_one, query_one))
    k_one = heads_of(project(n_one, key_one))
    v_one = heads_of(project(n_one, value_one))
    n_zero = normed(x0, gain_one)
    k_zero = heads_of(project(n_zero, key_one))
    v_zero = heads_of(project(n_zero, value_one))
    keys = jnp.concatenate([k_one, jnp.broadcast_to(k_zero[None], k_one.shape)], axis=1)
    vals = jnp.concatenate([v_one, jnp.broadcast_to(v_zero[None], v_one.shape)], axis=1)
    attended_one = softmax_attend(
        q_one, keys, vals, "fphd,fkhd->fhpk", "fhpk,fkhd->fphd", "fhp->fph"
    ).reshape(xs.shape).astype(jnp.bfloat16)
    mixed_one = jnp.dot(
        attended_one.reshape(-1, width), out_one, preferred_element_type=jnp.float32
    ).reshape(xs.shape)
    middle = (xs.astype(jnp.float32) + mixed_one).astype(jnp.bfloat16)

    all_places = n_pos * places
    run = all_places // (n_pos * n_frame)
    sent = (
        middle.reshape(per, n_pos, n_frame, run, width)
        .transpose(2, 1, 0, 3, 4)
        .reshape(n_frame * n_pos, per, run, width)
    )
    got = exchange(sent, ("frame", "pos"), (n_frame, n_pos), 2)
    mid_t = got.reshape(n_frame * n_pos * per, run, width)

    n_two = normed(mid_t, gain_two)
    q_two = heads_of(project(n_two, query_two))
    k_two = heads_of(project(n_two, key_two))
    v_two = heads_of(project(n_two, value_two))
    attended_two = softmax_attend(
        q_two, k_two, v_two, "fphd,kphd->phfk", "phfk,kphd->fphd", "phf->fph"
    ).reshape(mid_t.shape).astype(jnp.bfloat16)
    mixed_two = jnp.dot(
        attended_two.reshape(-1, width), out_two, preferred_element_type=jnp.float32
    ).reshape(mid_t.shape)
    decoded = (mid_t.astype(jnp.float32) + mixed_two).astype(jnp.bfloat16)

    sent = decoded.reshape(n_frame, frames, run, width)
    got = exchange(sent, ("frame",), (n_frame,), 3)
    return got.transpose(1, 0, 2, 3).reshape(frames, places, width)


def solution(mesh):
    return jax.shard_map(
        shards,
        mesh=mesh,
        in_specs=(P("frame", "pos", None), P(), P(), P(), P(), P(), P(), P(), P(), P(), P()),
        out_specs=P("frame", "pos", None),
        check_vma=False,
    )
```

```python
import jax
import jax.numpy as jnp
from jax import lax
from jax.experimental import pallas as pl
from jax.experimental.pallas import tpu as pltpu
from jax.sharding import PartitionSpec as P

HEADS = 4

MESH = pl.DeviceIdType.MESH


def exchange(x, names, sizes, cid):
    n = x.shape[0]

    def where(peer):
        if len(names) == 1:
            return {names[0]: peer}
        return {names[0]: peer // sizes[1], names[1]: peer % sizes[1]}

    def kernel(x_ref, o_ref, send_sem, recv_sem):
        me = lax.axis_index(names[0])
        if len(names) == 2:
            me = me * sizes[1] + lax.axis_index(names[1])
        barrier = pltpu.get_barrier_semaphore()
        for k in range(1, n):
            pl.semaphore_signal(barrier, inc=1, device_id=where((me + k) % n), device_id_type=MESH)
        pl.semaphore_wait(barrier, n - 1)
        copies = []
        for k in range(1, n):
            peer = (me + k) % n
            copy = pltpu.make_async_remote_copy(
                src_ref=x_ref.at[peer],
                dst_ref=o_ref.at[me],
                send_sem=send_sem.at[k],
                recv_sem=recv_sem.at[k],
                device_id=where(peer),
                device_id_type=MESH,
            )
            copy.start()
            copies.append(copy)
        o_ref[me] = x_ref[me]
        for copy in copies:
            copy.wait()

    return pl.pallas_call(
        kernel,
        out_shape=jax.ShapeDtypeStruct(x.shape, x.dtype),
        in_specs=[pl.BlockSpec(memory_space=pltpu.VMEM)],
        out_specs=pl.BlockSpec(memory_space=pltpu.VMEM),
        scratch_shapes=[pltpu.SemaphoreType.DMA((n,)), pltpu.SemaphoreType.DMA((n,))],
        compiler_params=pltpu.CompilerParams(collective_id=cid, has_side_effects=True),
    )(x)


def spatial_exchange(x, n_pos, n_frame, cid):
    _, per, places, width = x.shape

    def kernel(x_ref, o_ref, z_ref, send_sem, recv_sem, fsend_sem, frecv_sem, zsend_sem, zrecv_sem, local_sem):
        fi = lax.axis_index("frame")
        pi = lax.axis_index("pos")
        barrier = pltpu.get_barrier_semaphore()
        for k in range(1, n_pos):
            pl.semaphore_signal(barrier, inc=1, device_id={"pos": (pi + k) % n_pos}, device_id_type=MESH)
        for g in range(1, n_frame):
            pl.semaphore_signal(barrier, inc=1, device_id={"frame": (fi + g) % n_frame}, device_id_type=MESH)
        pl.semaphore_wait(barrier, n_pos - 1 + n_frame - 1)
        copies = []
        for k in range(1, n_pos):
            peer = (pi + k) % n_pos
            copy = pltpu.make_async_remote_copy(
                src_ref=x_ref.at[peer],
                dst_ref=o_ref.at[pi],
                send_sem=send_sem.at[k],
                recv_sem=recv_sem.at[k],
                device_id={"pos": peer},
                device_id_type=MESH,
            )
            copy.start()
            copies.append(copy)
        o_ref[pi] = x_ref[pi]

        def spread(g):
            return pltpu.make_async_remote_copy(
                src_ref=x_ref.at[0, 0],
                dst_ref=z_ref.at[pi],
                send_sem=fsend_sem.at[g],
                recv_sem=frecv_sem,
                device_id={"frame": g},
                device_id_type=MESH,
            )

        @pl.when(fi == 0)
        def _():
            local = pltpu.make_async_copy(x_ref.at[0, 0], z_ref.at[pi], local_sem)
            local.start()
            sends = [spread(g) for g in range(1, n_frame)]
            for send in sends:
                send.start()
            local.wait()
            for send in sends:
                send.wait_send()

        @pl.when(fi != 0)
        def _():
            spread(1).wait_recv()

        for k in range(1, n_pos):
            peer = (pi + k) % n_pos
            copy = pltpu.make_async_remote_copy(
                src_ref=z_ref.at[pi],
                dst_ref=z_ref.at[pi],
                send_sem=zsend_sem.at[k],
                recv_sem=zrecv_sem.at[k],
                device_id={"pos": peer},
                device_id_type=MESH,
            )
            copy.start()
            copies.append(copy)
        for copy in copies:
            copy.wait()

    return pl.pallas_call(
        kernel,
        out_shape=(
            jax.ShapeDtypeStruct(x.shape, x.dtype),
            jax.ShapeDtypeStruct((n_pos, places, width), x.dtype),
        ),
        in_specs=[pl.BlockSpec(memory_space=pltpu.VMEM)],
        out_specs=(pl.BlockSpec(memory_space=pltpu.VMEM), pl.BlockSpec(memory_space=pltpu.VMEM)),
        scratch_shapes=[
            pltpu.SemaphoreType.DMA((n_pos,)),
            pltpu.SemaphoreType.DMA((n_pos,)),
            pltpu.SemaphoreType.DMA((n_frame,)),
            pltpu.SemaphoreType.DMA,
            pltpu.SemaphoreType.DMA((n_pos,)),
            pltpu.SemaphoreType.DMA((n_pos,)),
            pltpu.SemaphoreType.DMA,
        ],
        compiler_params=pltpu.CompilerParams(collective_id=cid, has_side_effects=True),
    )(x)


def spatial_attend(x, q, kt, vt, k0t, v0t, out_w, rows):
    frames, places, width = x.shape
    depth = width // HEADS
    scale = depth ** (-0.5)

    def kernel(x_ref, q_ref, kt_ref, vt_ref, k0t_ref, v0t_ref, w_ref, o_ref):
        acc = x_ref[0].astype(jnp.float32)
        for h in range(HEADS):
            part = pl.ds(h * depth, depth)
            qh = q_ref[0, :, part]
            own = jnp.dot(qh, kt_ref[0, part, :], preferred_element_type=jnp.float32) * scale
            first = jnp.dot(qh, k0t_ref[part, :], preferred_element_type=jnp.float32) * scale
            high = jnp.maximum(jnp.max(own, axis=-1, keepdims=True), jnp.max(first, axis=-1, keepdims=True))
            own = jnp.exp(own - high)
            first = jnp.exp(first - high)
            totals = jnp.sum(own, axis=-1, keepdims=True) + jnp.sum(first, axis=-1, keepdims=True)
            contract = (((1,), (1,)), ((), ()))
            summed = lax.dot_general(
                own.astype(jnp.bfloat16), vt_ref[0, part, :], contract, preferred_element_type=jnp.float32
            ) + lax.dot_general(
                first.astype(jnp.bfloat16), v0t_ref[part, :], contract, preferred_element_type=jnp.float32
            )
            attended = (summed / totals).astype(jnp.bfloat16)
            acc = acc + jnp.dot(attended, w_ref[part, :], preferred_element_type=jnp.float32)
        o_ref[0] = acc.astype(o_ref.dtype)

    tile = lambda f, t: (f, t, 0)
    whole = lambda f, t: (f, 0, 0)
    fixed = lambda f, t: (0, 0)
    return pl.pallas_call(
        kernel,
        out_shape=jax.ShapeDtypeStruct(x.shape, x.dtype),
        grid=(frames, places // rows),
        in_specs=[
            pl.BlockSpec((1, rows, width), tile),
            pl.BlockSpec((1, rows, width), tile),
            pl.BlockSpec((1, width, places), whole),
            pl.BlockSpec((1, width, places), whole),
            pl.BlockSpec((width, places), fixed),
            pl.BlockSpec((width, places), fixed),
            pl.BlockSpec((width, width), fixed),
        ],
        out_specs=pl.BlockSpec((1, rows, width), tile),
    )(x, q, kt, vt, k0t, v0t, out_w)


def transposed(values, weight):
    result = jnp.einsum("...rc,cd->...dr", values, weight, preferred_element_type=jnp.float32)
    return result.astype(jnp.bfloat16)


def normed(values, gain):
    wide = values.astype(jnp.float32)
    factor = lax.rsqrt(jnp.mean(wide * wide, axis=-1, keepdims=True) + 1e-06)
    return (wide * factor * gain).astype(jnp.bfloat16)


def project(values, weight):
    flat = values.reshape(-1, values.shape[-1])
    result = jnp.dot(flat, weight, preferred_element_type=jnp.float32).astype(jnp.bfloat16)
    return result.reshape(values.shape[:-1] + (weight.shape[1],))


def heads_of(values):
    return values.reshape(values.shape[:-1] + (HEADS, values.shape[-1] // HEADS))


def softmax_attend(query, keys, vals, score_form, value_form, total_form):
    scale = query.shape[-1] ** (-0.5)
    scores = jnp.einsum(score_form, query, keys, preferred_element_type=jnp.float32) * scale
    weights = jnp.exp(scores - jnp.max(scores, axis=-1, keepdims=True))
    totals = jnp.sum(weights, axis=-1)
    summed = jnp.einsum(
        value_form, weights.astype(jnp.bfloat16), vals, preferred_element_type=jnp.float32
    )
    return summed / jnp.einsum(total_form, totals)[..., None]


def shards(
    latents,
    gain_one,
    query_one,
    key_one,
    value_one,
    out_one,
    gain_two,
    query_two,
    key_two,
    value_two,
    out_two,
):
    frames, places, width = latents.shape
    n_pos = lax.axis_size("pos")
    n_frame = lax.axis_size("frame")
    per = frames // n_pos
    got, zero = spatial_exchange(latents.reshape(n_pos, per, places, width), n_pos, n_frame, 1)
    xs = got.transpose(1, 0, 2, 3).reshape(per, n_pos * places, width)
    x0 = zero.reshape(n_pos * places, width)

    n_one = normed(xs, gain_one)
    q_one = project(n_one, query_one)
    n_zero = normed(x0, gain_one)
    middle = spatial_attend(
        xs,
        q_one,
        transposed(n_one, key_one),
        transposed(n_one, value_one),
        transposed(n_zero, key_one),
        transposed(n_zero, value_one),
        out_one,
        min(256, n_pos * places),
    )

    all_places = n_pos * places
    run = all_places // (n_pos * n_frame)
    sent = (
        middle.reshape(per, n_pos, n_frame, run, width)
        .transpose(2, 1, 0, 3, 4)
        .reshape(n_frame * n_pos, per, run, width)
    )
    got = exchange(sent, ("frame", "pos"), (n_frame, n_pos), 2)
    mid_t = got.reshape(n_frame * n_pos * per, run, width)

    n_two = normed(mid_t, gain_two)
    q_two = heads_of(project(n_two, query_two))
    k_two = heads_of(project(n_two, key_two))
    v_two = heads_of(project(n_two, value_two))
    attended_two = softmax_attend(
        q_two, k_two, v_two, "fphd,kphd->phfk", "phfk,kphd->fphd", "phf->fph"
    ).reshape(mid_t.shape).astype(jnp.bfloat16)
    mixed_two = jnp.dot(
        attended_two.reshape(-1, width), out_two, preferred_element_type=jnp.float32
    ).reshape(mid_t.shape)
    decoded = (mid_t.astype(jnp.float32) + mixed_two).astype(jnp.bfloat16)

    sent = decoded.reshape(n_frame, frames, run, width)
    got = exchange(sent, ("frame",), (n_frame,), 3)
    return got.transpose(1, 0, 2, 3).reshape(frames, places, width)


def solution(mesh):
    return jax.shard_map(
        shards,
        mesh=mesh,
        in_specs=(P("frame", "pos", None), P(), P(), P(), P(), P(), P(), P(), P(), P(), P()),
        out_specs=P("frame", "pos", None),
        check_vma=False,
    )
```

```python
import jax
import jax.numpy as jnp
from jax import lax
from jax.experimental import pallas as pl
from jax.experimental.pallas import tpu as pltpu
from jax.sharding import PartitionSpec as P

HEADS = 4

MESH = pl.DeviceIdType.MESH


def exchange(x, names, sizes, cid):
    n = x.shape[0]

    def where(peer):
        if len(names) == 1:
            return {names[0]: peer}
        return {names[0]: peer // sizes[1], names[1]: peer % sizes[1]}

    def kernel(x_ref, o_ref, send_sem, recv_sem):
        me = lax.axis_index(names[0])
        if len(names) == 2:
            me = me * sizes[1] + lax.axis_index(names[1])
        barrier = pltpu.get_barrier_semaphore()
        for k in range(1, n):
            pl.semaphore_signal(barrier, inc=1, device_id=where((me + k) % n), device_id_type=MESH)
        pl.semaphore_wait(barrier, n - 1)
        copies = []
        for k in range(1, n):
            peer = (me + k) % n
            copy = pltpu.make_async_remote_copy(
                src_ref=x_ref.at[peer],
                dst_ref=o_ref.at[me],
                send_sem=send_sem.at[k],
                recv_sem=recv_sem.at[k],
                device_id=where(peer),
                device_id_type=MESH,
            )
            copy.start()
            copies.append(copy)
        o_ref[me] = x_ref[me]
        for copy in copies:
            copy.wait()

    return pl.pallas_call(
        kernel,
        out_shape=jax.ShapeDtypeStruct(x.shape, x.dtype),
        in_specs=[pl.BlockSpec(memory_space=pltpu.VMEM)],
        out_specs=pl.BlockSpec(memory_space=pltpu.VMEM),
        scratch_shapes=[pltpu.SemaphoreType.DMA((n,)), pltpu.SemaphoreType.DMA((n,))],
        compiler_params=pltpu.CompilerParams(collective_id=cid, has_side_effects=True),
    )(x)


def spatial_exchange(x, n_pos, n_frame, cid):
    _, per, places, width = x.shape

    def kernel(x_ref, o_ref, z_ref, send_sem, recv_sem, fsend_sem, frecv_sem, zsend_sem, zrecv_sem, local_sem):
        fi = lax.axis_index("frame")
        pi = lax.axis_index("pos")
        barrier = pltpu.get_barrier_semaphore()
        for k in range(1, n_pos):
            pl.semaphore_signal(barrier, inc=1, device_id={"pos": (pi + k) % n_pos}, device_id_type=MESH)
        for g in range(1, n_frame):
            pl.semaphore_signal(barrier, inc=1, device_id={"frame": (fi + g) % n_frame}, device_id_type=MESH)
        pl.semaphore_wait(barrier, n_pos - 1 + n_frame - 1)
        copies = []
        for k in range(1, n_pos):
            peer = (pi + k) % n_pos
            copy = pltpu.make_async_remote_copy(
                src_ref=x_ref.at[peer],
                dst_ref=o_ref.at[pi],
                send_sem=send_sem.at[k],
                recv_sem=recv_sem.at[k],
                device_id={"pos": peer},
                device_id_type=MESH,
            )
            copy.start()
            copies.append(copy)
        o_ref[pi] = x_ref[pi]

        def spread(g):
            return pltpu.make_async_remote_copy(
                src_ref=x_ref.at[0, 0],
                dst_ref=z_ref.at[pi],
                send_sem=fsend_sem.at[g],
                recv_sem=frecv_sem,
                device_id={"frame": g},
                device_id_type=MESH,
            )

        @pl.when(fi == 0)
        def _():
            local = pltpu.make_async_copy(x_ref.at[0, 0], z_ref.at[pi], local_sem)
            local.start()
            sends = [spread(g) for g in range(1, n_frame)]
            for send in sends:
                send.start()
            local.wait()
            for send in sends:
                send.wait_send()

        @pl.when(fi != 0)
        def _():
            spread(1).wait_recv()

        for k in range(1, n_pos):
            peer = (pi + k) % n_pos
            copy = pltpu.make_async_remote_copy(
                src_ref=z_ref.at[pi],
                dst_ref=z_ref.at[pi],
                send_sem=zsend_sem.at[k],
                recv_sem=zrecv_sem.at[k],
                device_id={"pos": peer},
                device_id_type=MESH,
            )
            copy.start()
            copies.append(copy)
        for copy in copies:
            copy.wait()

    return pl.pallas_call(
        kernel,
        out_shape=(
            jax.ShapeDtypeStruct(x.shape, x.dtype),
            jax.ShapeDtypeStruct((n_pos, places, width), x.dtype),
        ),
        in_specs=[pl.BlockSpec(memory_space=pltpu.VMEM)],
        out_specs=(pl.BlockSpec(memory_space=pltpu.VMEM), pl.BlockSpec(memory_space=pltpu.VMEM)),
        scratch_shapes=[
            pltpu.SemaphoreType.DMA((n_pos,)),
            pltpu.SemaphoreType.DMA((n_pos,)),
            pltpu.SemaphoreType.DMA((n_frame,)),
            pltpu.SemaphoreType.DMA,
            pltpu.SemaphoreType.DMA((n_pos,)),
            pltpu.SemaphoreType.DMA((n_pos,)),
            pltpu.SemaphoreType.DMA,
        ],
        compiler_params=pltpu.CompilerParams(collective_id=cid, has_side_effects=True),
    )(x)


def spatial_attend(x, q, kt, vt, k0t, v0t, out_w, rows, n_frame, n_pos, cid):
    frames, places, width = x.shape
    depth = width // HEADS
    scale = depth ** (-0.5)
    n_dev = n_frame * n_pos
    run = places // n_dev
    chunks = rows // run

    def kernel(x_ref, q_ref, kt_ref, vt_ref, k0t_ref, v0t_ref, w_ref, o_ref, made, got, send_sem, recv_sem):
        f = pl.program_id(0)
        t = pl.program_id(1)
        fi = lax.axis_index("frame")
        pi = lax.axis_index("pos")
        me = fi * n_pos + pi

        @pl.when((f == 0) & (t == 0))
        def _():
            barrier = pltpu.get_barrier_semaphore()
            for k in range(1, n_dev):
                peer = (me + k) % n_dev
                pl.semaphore_signal(
                    barrier, inc=1, device_id={"frame": peer // n_pos, "pos": peer % n_pos}, device_id_type=MESH
                )
            pl.semaphore_wait(barrier, n_dev - 1)

        acc = x_ref[0].astype(jnp.float32)
        for h in range(HEADS):
            part = pl.ds(h * depth, depth)
            qh = q_ref[0, :, part]
            own = jnp.dot(qh, kt_ref[0, part, :], preferred_element_type=jnp.float32) * scale
            first = jnp.dot(qh, k0t_ref[part, :], preferred_element_type=jnp.float32) * scale
            high = jnp.maximum(jnp.max(own, axis=-1, keepdims=True), jnp.max(first, axis=-1, keepdims=True))
            own = jnp.exp(own - high)
            first = jnp.exp(first - high)
            totals = jnp.sum(own, axis=-1, keepdims=True) + jnp.sum(first, axis=-1, keepdims=True)
            contract = (((1,), (1,)), ((), ()))
            summed = lax.dot_general(
                own.astype(jnp.bfloat16), vt_ref[0, part, :], contract, preferred_element_type=jnp.float32
            ) + lax.dot_general(
                first.astype(jnp.bfloat16), v0t_ref[part, :], contract, preferred_element_type=jnp.float32
            )
            attended = (summed / totals).astype(jnp.bfloat16)
            acc = acc + jnp.dot(attended, w_ref[part, :], preferred_element_type=jnp.float32)
        base = t * chunks
        made[f, pl.ds(base, chunks)] = acc.reshape(chunks, run, width).astype(made.dtype)

        for i in range(chunks):
            gf = i % n_frame
            gp = (base + i) // n_frame

            @pl.when((gf == fi) & (gp == pi))
            def _():
                got[me, f] = made[f, base + i]

            @pl.when((gf != fi) | (gp != pi))
            def _():
                pltpu.make_async_remote_copy(
                    src_ref=made.at[f, base + i],
                    dst_ref=got.at[me, f],
                    send_sem=send_sem,
                    recv_sem=recv_sem,
                    device_id={"frame": gf, "pos": gp},
                    device_id_type=MESH,
                ).start()

        @pl.when((f == frames - 1) & (t == places // rows - 1))
        def _():
            others = pltpu.make_async_copy(got.at[pl.ds(0, n_dev - 1)], got.at[pl.ds(1, n_dev - 1)], recv_sem)
            others.wait()
            sent = pltpu.make_async_copy(got.at[pl.ds(0, n_dev - 1)], got.at[pl.ds(1, n_dev - 1)], send_sem)
            sent.wait()
            o_ref[...] = got[...]

    tile = lambda f, t: (f, t, 0)
    whole = lambda f, t: (f, 0, 0)
    fixed = lambda f, t: (0, 0)
    return pl.pallas_call(
        kernel,
        out_shape=jax.ShapeDtypeStruct((n_dev, frames, run, width), x.dtype),
        grid=(frames, places // rows),
        in_specs=[
            pl.BlockSpec((1, rows, width), tile),
            pl.BlockSpec((1, rows, width), tile),
            pl.BlockSpec((1, width, places), whole),
            pl.BlockSpec((1, width, places), whole),
            pl.BlockSpec((width, places), fixed),
            pl.BlockSpec((width, places), fixed),
            pl.BlockSpec((width, width), fixed),
        ],
        out_specs=pl.BlockSpec(memory_space=pltpu.VMEM),
        scratch_shapes=[
            pltpu.VMEM((frames, n_dev, run, width), x.dtype),
            pltpu.VMEM((n_dev, frames, run, width), x.dtype),
            pltpu.SemaphoreType.DMA,
            pltpu.SemaphoreType.DMA,
        ],
        compiler_params=pltpu.CompilerParams(collective_id=cid, has_side_effects=True),
    )(x, q, kt, vt, k0t, v0t, out_w)


def transposed(values, weight):
    result = jnp.einsum("...rc,cd->...dr", values, weight, preferred_element_type=jnp.float32)
    return result.astype(jnp.bfloat16)


def normed(values, gain):
    wide = values.astype(jnp.float32)
    factor = lax.rsqrt(jnp.mean(wide * wide, axis=-1, keepdims=True) + 1e-06)
    return (wide * factor * gain).astype(jnp.bfloat16)


def project(values, weight):
    flat = values.reshape(-1, values.shape[-1])
    result = jnp.dot(flat, weight, preferred_element_type=jnp.float32).astype(jnp.bfloat16)
    return result.reshape(values.shape[:-1] + (weight.shape[1],))


def heads_of(values):
    return values.reshape(values.shape[:-1] + (HEADS, values.shape[-1] // HEADS))


def softmax_attend(query, keys, vals, score_form, value_form, total_form):
    scale = query.shape[-1] ** (-0.5)
    scores = jnp.einsum(score_form, query, keys, preferred_element_type=jnp.float32) * scale
    weights = jnp.exp(scores - jnp.max(scores, axis=-1, keepdims=True))
    totals = jnp.sum(weights, axis=-1)
    summed = jnp.einsum(
        value_form, weights.astype(jnp.bfloat16), vals, preferred_element_type=jnp.float32
    )
    return summed / jnp.einsum(total_form, totals)[..., None]


def shards(
    latents,
    gain_one,
    query_one,
    key_one,
    value_one,
    out_one,
    gain_two,
    query_two,
    key_two,
    value_two,
    out_two,
):
    frames, places, width = latents.shape
    n_pos = lax.axis_size("pos")
    n_frame = lax.axis_size("frame")
    per = frames // n_pos
    got, zero = spatial_exchange(latents.reshape(n_pos, per, places, width), n_pos, n_frame, 1)
    xs = got.transpose(1, 0, 2, 3).reshape(per, n_pos * places, width)
    x0 = zero.reshape(n_pos * places, width)

    n_one = normed(xs, gain_one)
    q_one = project(n_one, query_one)
    n_zero = normed(x0, gain_one)
    got = spatial_attend(
        xs,
        q_one,
        transposed(n_one, key_one),
        transposed(n_one, value_one),
        transposed(n_zero, key_one),
        transposed(n_zero, value_one),
        out_one,
        min(256, n_pos * places),
        n_frame,
        n_pos,
        2,
    )
    all_places = n_pos * places
    run = all_places // (n_pos * n_frame)
    mid_t = got.reshape(n_frame * n_pos * per, run, width)

    n_two = normed(mid_t, gain_two)
    q_two = heads_of(project(n_two, query_two))
    k_two = heads_of(project(n_two, key_two))
    v_two = heads_of(project(n_two, value_two))
    attended_two = softmax_attend(
        q_two, k_two, v_two, "fphd,kphd->phfk", "phfk,kphd->fphd", "phf->fph"
    ).reshape(mid_t.shape).astype(jnp.bfloat16)
    mixed_two = jnp.dot(
        attended_two.reshape(-1, width), out_two, preferred_element_type=jnp.float32
    ).reshape(mid_t.shape)
    decoded = (mid_t.astype(jnp.float32) + mixed_two).astype(jnp.bfloat16)

    sent = decoded.reshape(n_frame, frames, run, width)
    got = exchange(sent, ("frame",), (n_frame,), 3)
    return got.transpose(1, 0, 2, 3).reshape(frames, places, width)


def solution(mesh):
    return jax.shard_map(
        shards,
        mesh=mesh,
        in_specs=(P("frame", "pos", None), P(), P(), P(), P(), P(), P(), P(), P(), P(), P()),
        out_specs=P("frame", "pos", None),
        check_vma=False,
    )
```

```python
import jax
import jax.numpy as jnp
from jax import lax
from jax.experimental import pallas as pl
from jax.experimental.pallas import tpu as pltpu
from jax.sharding import PartitionSpec as P

HEADS = 4

MESH = pl.DeviceIdType.MESH


def exchange(x, names, sizes, cid):
    n = x.shape[0]

    def where(peer):
        if len(names) == 1:
            return {names[0]: peer}
        return {names[0]: peer // sizes[1], names[1]: peer % sizes[1]}

    def kernel(x_ref, o_ref, send_sem, recv_sem):
        me = lax.axis_index(names[0])
        if len(names) == 2:
            me = me * sizes[1] + lax.axis_index(names[1])
        barrier = pltpu.get_barrier_semaphore()
        for k in range(1, n):
            pl.semaphore_signal(barrier, inc=1, device_id=where((me + k) % n), device_id_type=MESH)
        pl.semaphore_wait(barrier, n - 1)
        copies = []
        for k in range(1, n):
            peer = (me + k) % n
            copy = pltpu.make_async_remote_copy(
                src_ref=x_ref.at[peer],
                dst_ref=o_ref.at[me],
                send_sem=send_sem.at[k],
                recv_sem=recv_sem.at[k],
                device_id=where(peer),
                device_id_type=MESH,
            )
            copy.start()
            copies.append(copy)
        o_ref[me] = x_ref[me]
        for copy in copies:
            copy.wait()

    return pl.pallas_call(
        kernel,
        out_shape=jax.ShapeDtypeStruct(x.shape, x.dtype),
        in_specs=[pl.BlockSpec(memory_space=pltpu.VMEM)],
        out_specs=pl.BlockSpec(memory_space=pltpu.VMEM),
        scratch_shapes=[pltpu.SemaphoreType.DMA((n,)), pltpu.SemaphoreType.DMA((n,))],
        compiler_params=pltpu.CompilerParams(collective_id=cid, has_side_effects=True),
    )(x)


def spatial_exchange(x, n_pos, n_frame, cid):
    _, per, places, width = x.shape

    def kernel(x_ref, o_ref, z_ref, send_sem, recv_sem, fsend_sem, frecv_sem, zsend_sem, zrecv_sem, local_sem):
        fi = lax.axis_index("frame")
        pi = lax.axis_index("pos")
        barrier = pltpu.get_barrier_semaphore()
        for k in range(1, n_pos):
            pl.semaphore_signal(barrier, inc=1, device_id={"pos": (pi + k) % n_pos}, device_id_type=MESH)
        for g in range(1, n_frame):
            pl.semaphore_signal(barrier, inc=1, device_id={"frame": (fi + g) % n_frame}, device_id_type=MESH)
        pl.semaphore_wait(barrier, n_pos - 1 + n_frame - 1)
        copies = []
        for k in range(1, n_pos):
            peer = (pi + k) % n_pos
            copy = pltpu.make_async_remote_copy(
                src_ref=x_ref.at[peer],
                dst_ref=o_ref.at[pi],
                send_sem=send_sem.at[k],
                recv_sem=recv_sem.at[k],
                device_id={"pos": peer},
                device_id_type=MESH,
            )
            copy.start()
            copies.append(copy)
        o_ref[pi] = x_ref[pi]

        def spread(g):
            return pltpu.make_async_remote_copy(
                src_ref=x_ref.at[0, 0],
                dst_ref=z_ref.at[pi],
                send_sem=fsend_sem.at[g],
                recv_sem=frecv_sem,
                device_id={"frame": g},
                device_id_type=MESH,
            )

        @pl.when(fi == 0)
        def _():
            local = pltpu.make_async_copy(x_ref.at[0, 0], z_ref.at[pi], local_sem)
            local.start()
            sends = [spread(g) for g in range(1, n_frame)]
            for send in sends:
                send.start()
            local.wait()
            for send in sends:
                send.wait_send()

        @pl.when(fi != 0)
        def _():
            spread(1).wait_recv()

        for k in range(1, n_pos):
            peer = (pi + k) % n_pos
            copy = pltpu.make_async_remote_copy(
                src_ref=z_ref.at[pi],
                dst_ref=z_ref.at[pi],
                send_sem=zsend_sem.at[k],
                recv_sem=zrecv_sem.at[k],
                device_id={"pos": peer},
                device_id_type=MESH,
            )
            copy.start()
            copies.append(copy)
        for copy in copies:
            copy.wait()

    return pl.pallas_call(
        kernel,
        out_shape=(
            jax.ShapeDtypeStruct(x.shape, x.dtype),
            jax.ShapeDtypeStruct((n_pos, places, width), x.dtype),
        ),
        in_specs=[pl.BlockSpec(memory_space=pltpu.VMEM)],
        out_specs=(pl.BlockSpec(memory_space=pltpu.VMEM), pl.BlockSpec(memory_space=pltpu.VMEM)),
        scratch_shapes=[
            pltpu.SemaphoreType.DMA((n_pos,)),
            pltpu.SemaphoreType.DMA((n_pos,)),
            pltpu.SemaphoreType.DMA((n_frame,)),
            pltpu.SemaphoreType.DMA,
            pltpu.SemaphoreType.DMA((n_pos,)),
            pltpu.SemaphoreType.DMA((n_pos,)),
            pltpu.SemaphoreType.DMA,
        ],
        compiler_params=pltpu.CompilerParams(collective_id=cid, has_side_effects=True),
    )(x)


def spatial_attend(x, q, kt, vt, k0t, v0t, out_w, rows, n_frame, n_pos, cid):
    frames, places, width = x.shape
    depth = width // HEADS
    scale = depth ** (-0.5)
    n_dev = n_frame * n_pos
    run = places // n_dev
    chunks = rows // run

    def kernel(x_ref, q_ref, kt_ref, vt_ref, k0t_ref, v0t_ref, w_ref, o_ref, made, got, send_sem, recv_sem):
        f = pl.program_id(0)
        t = pl.program_id(1)
        fi = lax.axis_index("frame")
        pi = lax.axis_index("pos")
        me = fi * n_pos + pi

        @pl.when((f == 0) & (t == 0))
        def _():
            barrier = pltpu.get_barrier_semaphore()
            for k in range(1, n_dev):
                peer = (me + k) % n_dev
                pl.semaphore_signal(
                    barrier, inc=1, device_id={"frame": peer // n_pos, "pos": peer % n_pos}, device_id_type=MESH
                )
            pl.semaphore_wait(barrier, n_dev - 1)

        acc = x_ref[0].astype(jnp.float32)
        for h in range(HEADS):
            part = pl.ds(h * depth, depth)
            qh = q_ref[0, :, part]
            own = jnp.dot(qh, kt_ref[0, part, :], preferred_element_type=jnp.float32) * scale
            first = jnp.dot(qh, k0t_ref[part, :], preferred_element_type=jnp.float32) * scale
            high = jnp.maximum(jnp.max(own, axis=-1, keepdims=True), jnp.max(first, axis=-1, keepdims=True))
            own = jnp.exp(own - high)
            first = jnp.exp(first - high)
            totals = jnp.sum(own, axis=-1, keepdims=True) + jnp.sum(first, axis=-1, keepdims=True)
            contract = (((1,), (1,)), ((), ()))
            summed = lax.dot_general(
                own.astype(jnp.bfloat16), vt_ref[0, part, :], contract, preferred_element_type=jnp.float32
            ) + lax.dot_general(
                first.astype(jnp.bfloat16), v0t_ref[part, :], contract, preferred_element_type=jnp.float32
            )
            attended = (summed / totals).astype(jnp.bfloat16)
            acc = acc + jnp.dot(attended, w_ref[part, :], preferred_element_type=jnp.float32)
        base = t * chunks
        made[f, pl.ds(base, chunks)] = acc.reshape(chunks, run, width).astype(made.dtype)

        for i in range(chunks):
            gf = i % n_frame
            gp = (base + i) // n_frame

            @pl.when((gf == fi) & (gp == pi))
            def _():
                got[me, f] = made[f, base + i]

            @pl.when((gf != fi) | (gp != pi))
            def _():
                pltpu.make_async_remote_copy(
                    src_ref=made.at[f, base + i],
                    dst_ref=got.at[me, f],
                    send_sem=send_sem,
                    recv_sem=recv_sem,
                    device_id={"frame": gf, "pos": gp},
                    device_id_type=MESH,
                ).start()

        @pl.when((f == frames - 1) & (t == places // rows - 1))
        def _():
            others = pltpu.make_async_copy(got.at[pl.ds(0, n_dev - 1)], got.at[pl.ds(1, n_dev - 1)], recv_sem)
            others.wait()
            sent = pltpu.make_async_copy(got.at[pl.ds(0, n_dev - 1)], got.at[pl.ds(1, n_dev - 1)], send_sem)
            sent.wait()
            o_ref[...] = got[...]

    tile = lambda f, t: (f, t, 0)
    whole = lambda f, t: (f, 0, 0)
    fixed = lambda f, t: (0, 0)
    return pl.pallas_call(
        kernel,
        out_shape=jax.ShapeDtypeStruct((n_dev, frames, run, width), x.dtype),
        grid=(frames, places // rows),
        in_specs=[
            pl.BlockSpec((1, rows, width), tile),
            pl.BlockSpec((1, rows, width), tile),
            pl.BlockSpec((1, width, places), whole),
            pl.BlockSpec((1, width, places), whole),
            pl.BlockSpec((width, places), fixed),
            pl.BlockSpec((width, places), fixed),
            pl.BlockSpec((width, width), fixed),
        ],
        out_specs=pl.BlockSpec(memory_space=pltpu.VMEM),
        scratch_shapes=[
            pltpu.VMEM((frames, n_dev, run, width), x.dtype),
            pltpu.VMEM((n_dev, frames, run, width), x.dtype),
            pltpu.SemaphoreType.DMA,
            pltpu.SemaphoreType.DMA,
        ],
        compiler_params=pltpu.CompilerParams(collective_id=cid, has_side_effects=True),
    )(x, q, kt, vt, k0t, v0t, out_w)


def temporal_attend(x, gain, wq, wk, wv, out_w, n_frame, cid):
    run, every, width = x.shape
    depth = width // HEADS
    scale = depth ** (-0.5)
    frames = every // n_frame

    def kernel(x_ref, g_ref, wq_ref, wk_ref, wv_ref, w_ref, o_ref, made, got, send_sem, recv_sem):
        p = pl.program_id(0)
        fi = lax.axis_index("frame")

        @pl.when(p == 0)
        def _():
            barrier = pltpu.get_barrier_semaphore()
            for k in range(1, n_frame):
                pl.semaphore_signal(barrier, inc=1, device_id={"frame": (fi + k) % n_frame}, device_id_type=MESH)
            pl.semaphore_wait(barrier, n_frame - 1)

        wide = x_ref[0].astype(jnp.float32)
        factor = lax.rsqrt(jnp.mean(wide * wide, axis=-1, keepdims=True) + 1e-06)
        normed_two = (wide * factor * g_ref[...]).astype(jnp.bfloat16)
        acc = wide
        for h in range(HEADS):
            qh = jnp.dot(normed_two, wq_ref[h], preferred_element_type=jnp.float32).astype(jnp.bfloat16)
            kh = jnp.dot(normed_two, wk_ref[h], preferred_element_type=jnp.float32).astype(jnp.bfloat16)
            vh = jnp.dot(normed_two, wv_ref[h], preferred_element_type=jnp.float32).astype(jnp.bfloat16)
            contract = (((1,), (1,)), ((), ()))
            scores = lax.dot_general(qh, kh, contract, preferred_element_type=jnp.float32) * scale
            weights = jnp.exp(scores - jnp.max(scores, axis=-1, keepdims=True))
            totals = jnp.sum(weights, axis=-1, keepdims=True)
            summed = jnp.dot(weights.astype(jnp.bfloat16), vh, preferred_element_type=jnp.float32)
            attended = (summed / totals).astype(jnp.bfloat16)
            acc = acc + jnp.dot(attended, w_ref[pl.ds(h * depth, depth), :], preferred_element_type=jnp.float32)
        made[p] = acc.astype(made.dtype)

        for g in range(n_frame):
            @pl.when(g == fi)
            def _():
                got[fi, p] = made[p, pl.ds(g * frames, frames)]

            @pl.when(g != fi)
            def _():
                pltpu.make_async_remote_copy(
                    src_ref=made.at[p, pl.ds(g * frames, frames)],
                    dst_ref=got.at[fi, p],
                    send_sem=send_sem,
                    recv_sem=recv_sem,
                    device_id={"frame": g},
                    device_id_type=MESH,
                ).start()

        @pl.when(p == run - 1)
        def _():
            others = pltpu.make_async_copy(got.at[pl.ds(0, n_frame - 1)], got.at[pl.ds(1, n_frame - 1)], recv_sem)
            others.wait()
            sent = pltpu.make_async_copy(got.at[pl.ds(0, n_frame - 1)], got.at[pl.ds(1, n_frame - 1)], send_sem)
            sent.wait()
            o_ref[...] = got[...]

    fixed = lambda p: (0, 0)
    fixed3 = lambda p: (0, 0, 0)
    split = lambda w: w.reshape(width, HEADS, depth).transpose(1, 0, 2)
    return pl.pallas_call(
        kernel,
        out_shape=jax.ShapeDtypeStruct((n_frame, run, frames, width), x.dtype),
        grid=(run,),
        in_specs=[
            pl.BlockSpec((1, every, width), lambda p: (p, 0, 0)),
            pl.BlockSpec((1, width), fixed),
            pl.BlockSpec((HEADS, width, depth), fixed3),
            pl.BlockSpec((HEADS, width, depth), fixed3),
            pl.BlockSpec((HEADS, width, depth), fixed3),
            pl.BlockSpec((width, width), fixed),
        ],
        out_specs=pl.BlockSpec(memory_space=pltpu.VMEM),
        scratch_shapes=[
            pltpu.VMEM((run, every, width), x.dtype),
            pltpu.VMEM((n_frame, run, frames, width), x.dtype),
            pltpu.SemaphoreType.DMA,
            pltpu.SemaphoreType.DMA,
        ],
        compiler_params=pltpu.CompilerParams(collective_id=cid, has_side_effects=True),
    )(x, gain.reshape(1, width), split(wq), split(wk), split(wv), out_w)


def transposed(values, weight):
    result = jnp.einsum("...rc,cd->...dr", values, weight, preferred_element_type=jnp.float32)
    return result.astype(jnp.bfloat16)


def normed(values, gain):
    wide = values.astype(jnp.float32)
    factor = lax.rsqrt(jnp.mean(wide * wide, axis=-1, keepdims=True) + 1e-06)
    return (wide * factor * gain).astype(jnp.bfloat16)


def project(values, weight):
    flat = values.reshape(-1, values.shape[-1])
    result = jnp.dot(flat, weight, preferred_element_type=jnp.float32).astype(jnp.bfloat16)
    return result.reshape(values.shape[:-1] + (weight.shape[1],))


def heads_of(values):
    return values.reshape(values.shape[:-1] + (HEADS, values.shape[-1] // HEADS))


def softmax_attend(query, keys, vals, score_form, value_form, total_form):
    scale = query.shape[-1] ** (-0.5)
    scores = jnp.einsum(score_form, query, keys, preferred_element_type=jnp.float32) * scale
    weights = jnp.exp(scores - jnp.max(scores, axis=-1, keepdims=True))
    totals = jnp.sum(weights, axis=-1)
    summed = jnp.einsum(
        value_form, weights.astype(jnp.bfloat16), vals, preferred_element_type=jnp.float32
    )
    return summed / jnp.einsum(total_form, totals)[..., None]


def shards(
    latents,
    gain_one,
    query_one,
    key_one,
    value_one,
    out_one,
    gain_two,
    query_two,
    key_two,
    value_two,
    out_two,
):
    frames, places, width = latents.shape
    n_pos = lax.axis_size("pos")
    n_frame = lax.axis_size("frame")
    per = frames // n_pos
    got, zero = spatial_exchange(latents.reshape(n_pos, per, places, width), n_pos, n_frame, 1)
    xs = got.transpose(1, 0, 2, 3).reshape(per, n_pos * places, width)
    x0 = zero.reshape(n_pos * places, width)

    n_one = normed(xs, gain_one)
    q_one = project(n_one, query_one)
    n_zero = normed(x0, gain_one)
    got = spatial_attend(
        xs,
        q_one,
        transposed(n_one, key_one),
        transposed(n_one, value_one),
        transposed(n_zero, key_one),
        transposed(n_zero, value_one),
        out_one,
        min(256, n_pos * places),
        n_frame,
        n_pos,
        2,
    )
    all_places = n_pos * places
    run = all_places // (n_pos * n_frame)
    mid_t = got.reshape(n_frame * n_pos * per, run, width).transpose(1, 0, 2)
    got = temporal_attend(mid_t, gain_two, query_two, key_two, value_two, out_two, n_frame, 3)
    return got.transpose(2, 0, 1, 3).reshape(frames, places, width)


def solution(mesh):
    return jax.shard_map(
        shards,
        mesh=mesh,
        in_specs=(P("frame", "pos", None), P(), P(), P(), P(), P(), P(), P(), P(), P(), P()),
        out_specs=P("frame", "pos", None),
        check_vma=False,
    )
```

```python
import jax
import jax.numpy as jnp
from jax import lax
from jax.experimental import pallas as pl
from jax.experimental.pallas import tpu as pltpu
from jax.sharding import PartitionSpec as P

HEADS = 4

MESH = pl.DeviceIdType.MESH


def exchange(x, names, sizes, cid):
    n = x.shape[0]

    def where(peer):
        if len(names) == 1:
            return {names[0]: peer}
        return {names[0]: peer // sizes[1], names[1]: peer % sizes[1]}

    def kernel(x_ref, o_ref, send_sem, recv_sem):
        me = lax.axis_index(names[0])
        if len(names) == 2:
            me = me * sizes[1] + lax.axis_index(names[1])
        barrier = pltpu.get_barrier_semaphore()
        for k in range(1, n):
            pl.semaphore_signal(barrier, inc=1, device_id=where((me + k) % n), device_id_type=MESH)
        pl.semaphore_wait(barrier, n - 1)
        copies = []
        for k in range(1, n):
            peer = (me + k) % n
            copy = pltpu.make_async_remote_copy(
                src_ref=x_ref.at[peer],
                dst_ref=o_ref.at[me],
                send_sem=send_sem.at[k],
                recv_sem=recv_sem.at[k],
                device_id=where(peer),
                device_id_type=MESH,
            )
            copy.start()
            copies.append(copy)
        o_ref[me] = x_ref[me]
        for copy in copies:
            copy.wait()

    return pl.pallas_call(
        kernel,
        out_shape=jax.ShapeDtypeStruct(x.shape, x.dtype),
        in_specs=[pl.BlockSpec(memory_space=pltpu.VMEM)],
        out_specs=pl.BlockSpec(memory_space=pltpu.VMEM),
        scratch_shapes=[pltpu.SemaphoreType.DMA((n,)), pltpu.SemaphoreType.DMA((n,))],
        compiler_params=pltpu.CompilerParams(collective_id=cid, has_side_effects=True),
    )(x)


def spatial_exchange(x, n_pos, n_frame, cid):
    _, per, places, width = x.shape

    def kernel(x_ref, o_ref, z_ref, send_sem, recv_sem, fsend_sem, frecv_sem, zsend_sem, zrecv_sem, local_sem):
        fi = lax.axis_index("frame")
        pi = lax.axis_index("pos")
        barrier = pltpu.get_barrier_semaphore()
        for k in range(1, n_pos):
            pl.semaphore_signal(barrier, inc=1, device_id={"pos": (pi + k) % n_pos}, device_id_type=MESH)
        for g in range(1, n_frame):
            pl.semaphore_signal(barrier, inc=1, device_id={"frame": (fi + g) % n_frame}, device_id_type=MESH)
        pl.semaphore_wait(barrier, n_pos - 1 + n_frame - 1)
        copies = []
        for k in range(1, n_pos):
            peer = (pi + k) % n_pos
            copy = pltpu.make_async_remote_copy(
                src_ref=x_ref.at[peer],
                dst_ref=o_ref.at[pi],
                send_sem=send_sem.at[k],
                recv_sem=recv_sem.at[k],
                device_id={"pos": peer},
                device_id_type=MESH,
            )
            copy.start()
            copies.append(copy)
        o_ref[pi] = x_ref[pi]

        def spread(g):
            return pltpu.make_async_remote_copy(
                src_ref=x_ref.at[0, 0],
                dst_ref=z_ref.at[pi],
                send_sem=fsend_sem.at[g],
                recv_sem=frecv_sem,
                device_id={"frame": g},
                device_id_type=MESH,
            )

        @pl.when(fi == 0)
        def _():
            local = pltpu.make_async_copy(x_ref.at[0, 0], z_ref.at[pi], local_sem)
            local.start()
            sends = [spread(g) for g in range(1, n_frame)]
            for send in sends:
                send.start()
            local.wait()
            for send in sends:
                send.wait_send()

        @pl.when(fi != 0)
        def _():
            spread(1).wait_recv()

        for k in range(1, n_pos):
            peer = (pi + k) % n_pos
            copy = pltpu.make_async_remote_copy(
                src_ref=z_ref.at[pi],
                dst_ref=z_ref.at[pi],
                send_sem=zsend_sem.at[k],
                recv_sem=zrecv_sem.at[k],
                device_id={"pos": peer},
                device_id_type=MESH,
            )
            copy.start()
            copies.append(copy)
        for copy in copies:
            copy.wait()

    return pl.pallas_call(
        kernel,
        out_shape=(
            jax.ShapeDtypeStruct(x.shape, x.dtype),
            jax.ShapeDtypeStruct((n_pos, places, width), x.dtype),
        ),
        in_specs=[pl.BlockSpec(memory_space=pltpu.VMEM)],
        out_specs=(pl.BlockSpec(memory_space=pltpu.VMEM), pl.BlockSpec(memory_space=pltpu.VMEM)),
        scratch_shapes=[
            pltpu.SemaphoreType.DMA((n_pos,)),
            pltpu.SemaphoreType.DMA((n_pos,)),
            pltpu.SemaphoreType.DMA((n_frame,)),
            pltpu.SemaphoreType.DMA,
            pltpu.SemaphoreType.DMA((n_pos,)),
            pltpu.SemaphoreType.DMA((n_pos,)),
            pltpu.SemaphoreType.DMA,
        ],
        compiler_params=pltpu.CompilerParams(collective_id=cid, has_side_effects=True),
    )(x)


def spatial_attend(x, q, kt, vt, k0t, v0t, out_w, rows, n_frame, n_pos, cid):
    frames, places, width = x.shape
    depth = width // HEADS
    scale = depth ** (-0.5)
    n_dev = n_frame * n_pos
    run = places // n_dev
    chunks = rows // run

    def kernel(x_ref, q_ref, kt_ref, vt_ref, k0t_ref, v0t_ref, w_ref, o_ref, made, got, send_sem, recv_sem):
        t = pl.program_id(0)
        fi = lax.axis_index("frame")
        pi = lax.axis_index("pos")
        me = fi * n_pos + pi
        barrier = pltpu.get_barrier_semaphore()

        @pl.when(t == 0)
        def _():
            for k in range(1, n_dev):
                peer = (me + k) % n_dev
                pl.semaphore_signal(
                    barrier, inc=1, device_id={"frame": peer // n_pos, "pos": peer % n_pos}, device_id_type=MESH
                )

        base = t * chunks
        for f in range(frames):
            acc = x_ref[f].astype(jnp.float32)
            for h in range(HEADS):
                part = pl.ds(h * depth, depth)
                qh = q_ref[f, :, part]
                own = jnp.dot(qh, kt_ref[f, part, :], preferred_element_type=jnp.float32) * scale
                first = jnp.dot(qh, k0t_ref[part, :], preferred_element_type=jnp.float32) * scale
                high = jnp.maximum(
                    jnp.max(own, axis=-1, keepdims=True), jnp.max(first, axis=-1, keepdims=True)
                )
                own = jnp.exp(own - high)
                first = jnp.exp(first - high)
                totals = jnp.sum(own, axis=-1, keepdims=True) + jnp.sum(first, axis=-1, keepdims=True)
                contract = (((1,), (1,)), ((), ()))
                summed = lax.dot_general(
                    own.astype(jnp.bfloat16), vt_ref[f, part, :], contract, preferred_element_type=jnp.float32
                ) + lax.dot_general(
                    first.astype(jnp.bfloat16), v0t_ref[part, :], contract, preferred_element_type=jnp.float32
                )
                attended = (summed / totals).astype(jnp.bfloat16)
                acc = acc + jnp.dot(attended, w_ref[part, :], preferred_element_type=jnp.float32)
            made[pl.ds(base, chunks), f] = acc.reshape(chunks, run, width).astype(made.dtype)

        @pl.when(t == 0)
        def _():
            pl.semaphore_wait(barrier, n_dev - 1)

        for i in range(chunks):
            gf = i % n_frame
            gp = (base + i) // n_frame

            @pl.when((gf == fi) & (gp == pi))
            def _():
                got[me] = made[base + i]

            @pl.when((gf != fi) | (gp != pi))
            def _():
                pltpu.make_async_remote_copy(
                    src_ref=made.at[base + i],
                    dst_ref=got.at[me],
                    send_sem=send_sem,
                    recv_sem=recv_sem,
                    device_id={"frame": gf, "pos": gp},
                    device_id_type=MESH,
                ).start()

        @pl.when(t == places // rows - 1)
        def _():
            others = pltpu.make_async_copy(got.at[pl.ds(0, n_dev - 1)], got.at[pl.ds(1, n_dev - 1)], recv_sem)
            others.wait()
            sent = pltpu.make_async_copy(got.at[pl.ds(0, n_dev - 1)], got.at[pl.ds(1, n_dev - 1)], send_sem)
            sent.wait()
            o_ref[...] = got[...]

    tile = lambda t: (0, t, 0)
    whole = lambda t: (0, 0, 0)
    fixed = lambda t: (0, 0)
    return pl.pallas_call(
        kernel,
        out_shape=jax.ShapeDtypeStruct((n_dev, frames, run, width), x.dtype),
        grid=(places // rows,),
        in_specs=[
            pl.BlockSpec((frames, rows, width), tile),
            pl.BlockSpec((frames, rows, width), tile),
            pl.BlockSpec((frames, width, places), whole),
            pl.BlockSpec((frames, width, places), whole),
            pl.BlockSpec((width, places), fixed),
            pl.BlockSpec((width, places), fixed),
            pl.BlockSpec((width, width), fixed),
        ],
        out_specs=pl.BlockSpec(memory_space=pltpu.VMEM),
        scratch_shapes=[
            pltpu.VMEM((n_dev, frames, run, width), x.dtype),
            pltpu.VMEM((n_dev, frames, run, width), x.dtype),
            pltpu.SemaphoreType.DMA,
            pltpu.SemaphoreType.DMA,
        ],
        compiler_params=pltpu.CompilerParams(collective_id=cid, has_side_effects=True),
    )(x, q, kt, vt, k0t, v0t, out_w)


def temporal_attend(x, gain, wq, wk, wv, out_w, n_frame, cid):
    run, every, width = x.shape
    depth = width // HEADS
    scale = depth ** (-0.5)
    frames = every // n_frame

    def kernel(x_ref, g_ref, wq_ref, wk_ref, wv_ref, w_ref, o_ref, made, got, send_sem, recv_sem):
        p = pl.program_id(0)
        fi = lax.axis_index("frame")

        barrier = pltpu.get_barrier_semaphore()

        @pl.when(p == 0)
        def _():
            for k in range(1, n_frame):
                pl.semaphore_signal(barrier, inc=1, device_id={"frame": (fi + k) % n_frame}, device_id_type=MESH)

        wide = x_ref[0].astype(jnp.float32)
        factor = lax.rsqrt(jnp.mean(wide * wide, axis=-1, keepdims=True) + 1e-06)
        normed_two = (wide * factor * g_ref[...]).astype(jnp.bfloat16)
        acc = wide
        for h in range(HEADS):
            qh = jnp.dot(normed_two, wq_ref[h], preferred_element_type=jnp.float32).astype(jnp.bfloat16)
            kh = jnp.dot(normed_two, wk_ref[h], preferred_element_type=jnp.float32).astype(jnp.bfloat16)
            vh = jnp.dot(normed_two, wv_ref[h], preferred_element_type=jnp.float32).astype(jnp.bfloat16)
            contract = (((1,), (1,)), ((), ()))
            scores = lax.dot_general(qh, kh, contract, preferred_element_type=jnp.float32) * scale
            weights = jnp.exp(scores - jnp.max(scores, axis=-1, keepdims=True))
            totals = jnp.sum(weights, axis=-1, keepdims=True)
            summed = jnp.dot(weights.astype(jnp.bfloat16), vh, preferred_element_type=jnp.float32)
            attended = (summed / totals).astype(jnp.bfloat16)
            acc = acc + jnp.dot(attended, w_ref[pl.ds(h * depth, depth), :], preferred_element_type=jnp.float32)
        made[p] = acc.astype(made.dtype)

        @pl.when(p == 0)
        def _():
            pl.semaphore_wait(barrier, n_frame - 1)

        for g in range(n_frame):
            @pl.when(g == fi)
            def _():
                got[fi, p] = made[p, pl.ds(g * frames, frames)]

            @pl.when(g != fi)
            def _():
                pltpu.make_async_remote_copy(
                    src_ref=made.at[p, pl.ds(g * frames, frames)],
                    dst_ref=got.at[fi, p],
                    send_sem=send_sem,
                    recv_sem=recv_sem,
                    device_id={"frame": g},
                    device_id_type=MESH,
                ).start()

        @pl.when(p == run - 1)
        def _():
            others = pltpu.make_async_copy(got.at[pl.ds(0, n_frame - 1)], got.at[pl.ds(1, n_frame - 1)], recv_sem)
            others.wait()
            sent = pltpu.make_async_copy(got.at[pl.ds(0, n_frame - 1)], got.at[pl.ds(1, n_frame - 1)], send_sem)
            sent.wait()
            o_ref[...] = got[...]

    fixed = lambda p: (0, 0)
    fixed3 = lambda p: (0, 0, 0)
    split = lambda w: w.reshape(width, HEADS, depth).transpose(1, 0, 2)
    return pl.pallas_call(
        kernel,
        out_shape=jax.ShapeDtypeStruct((n_frame, run, frames, width), x.dtype),
        grid=(run,),
        in_specs=[
            pl.BlockSpec((1, every, width), lambda p: (p, 0, 0)),
            pl.BlockSpec((1, width), fixed),
            pl.BlockSpec((HEADS, width, depth), fixed3),
            pl.BlockSpec((HEADS, width, depth), fixed3),
            pl.BlockSpec((HEADS, width, depth), fixed3),
            pl.BlockSpec((width, width), fixed),
        ],
        out_specs=pl.BlockSpec(memory_space=pltpu.VMEM),
        scratch_shapes=[
            pltpu.VMEM((run, every, width), x.dtype),
            pltpu.VMEM((n_frame, run, frames, width), x.dtype),
            pltpu.SemaphoreType.DMA,
            pltpu.SemaphoreType.DMA,
        ],
        compiler_params=pltpu.CompilerParams(collective_id=cid, has_side_effects=True),
    )(x, gain.reshape(1, width), split(wq), split(wk), split(wv), out_w)


def transposed(values, weight):
    result = jnp.einsum("...rc,cd->...dr", values, weight, preferred_element_type=jnp.float32)
    return result.astype(jnp.bfloat16)


def normed(values, gain):
    wide = values.astype(jnp.float32)
    factor = lax.rsqrt(jnp.mean(wide * wide, axis=-1, keepdims=True) + 1e-06)
    return (wide * factor * gain).astype(jnp.bfloat16)


def project(values, weight):
    flat = values.reshape(-1, values.shape[-1])
    result = jnp.dot(flat, weight, preferred_element_type=jnp.float32).astype(jnp.bfloat16)
    return result.reshape(values.shape[:-1] + (weight.shape[1],))


def heads_of(values):
    return values.reshape(values.shape[:-1] + (HEADS, values.shape[-1] // HEADS))


def softmax_attend(query, keys, vals, score_form, value_form, total_form):
    scale = query.shape[-1] ** (-0.5)
    scores = jnp.einsum(score_form, query, keys, preferred_element_type=jnp.float32) * scale
    weights = jnp.exp(scores - jnp.max(scores, axis=-1, keepdims=True))
    totals = jnp.sum(weights, axis=-1)
    summed = jnp.einsum(
        value_form, weights.astype(jnp.bfloat16), vals, preferred_element_type=jnp.float32
    )
    return summed / jnp.einsum(total_form, totals)[..., None]


def shards(
    latents,
    gain_one,
    query_one,
    key_one,
    value_one,
    out_one,
    gain_two,
    query_two,
    key_two,
    value_two,
    out_two,
):
    frames, places, width = latents.shape
    n_pos = lax.axis_size("pos")
    n_frame = lax.axis_size("frame")
    per = frames // n_pos
    got, zero = spatial_exchange(latents.reshape(n_pos, per, places, width), n_pos, n_frame, 1)
    xs = got.transpose(1, 0, 2, 3).reshape(per, n_pos * places, width)
    x0 = zero.reshape(n_pos * places, width)

    n_one = normed(xs, gain_one)
    q_one = project(n_one, query_one)
    n_zero = normed(x0, gain_one)
    got = spatial_attend(
        xs,
        q_one,
        transposed(n_one, key_one),
        transposed(n_one, value_one),
        transposed(n_zero, key_one),
        transposed(n_zero, value_one),
        out_one,
        min(256, n_pos * places),
        n_frame,
        n_pos,
        2,
    )
    all_places = n_pos * places
    run = all_places // (n_pos * n_frame)
    mid_t = got.reshape(n_frame * n_pos * per, run, width).transpose(1, 0, 2)
    got = temporal_attend(mid_t, gain_two, query_two, key_two, value_two, out_two, n_frame, 3)
    return got.transpose(2, 0, 1, 3).reshape(frames, places, width)


def solution(mesh):
    return jax.shard_map(
        shards,
        mesh=mesh,
        in_specs=(P("frame", "pos", None), P(), P(), P(), P(), P(), P(), P(), P(), P(), P()),
        out_specs=P("frame", "pos", None),
        check_vma=False,
    )
```

```python
import jax
import jax.numpy as jnp
from jax import lax
from jax.experimental import pallas as pl
from jax.experimental.pallas import tpu as pltpu
from jax.sharding import PartitionSpec as P

HEADS = 4

MESH = pl.DeviceIdType.MESH


def exchange(x, names, sizes, cid):
    n = x.shape[0]

    def where(peer):
        if len(names) == 1:
            return {names[0]: peer}
        return {names[0]: peer // sizes[1], names[1]: peer % sizes[1]}

    def kernel(x_ref, o_ref, send_sem, recv_sem):
        me = lax.axis_index(names[0])
        if len(names) == 2:
            me = me * sizes[1] + lax.axis_index(names[1])
        barrier = pltpu.get_barrier_semaphore()
        for k in range(1, n):
            pl.semaphore_signal(barrier, inc=1, device_id=where((me + k) % n), device_id_type=MESH)
        pl.semaphore_wait(barrier, n - 1)
        copies = []
        for k in range(1, n):
            peer = (me + k) % n
            copy = pltpu.make_async_remote_copy(
                src_ref=x_ref.at[peer],
                dst_ref=o_ref.at[me],
                send_sem=send_sem.at[k],
                recv_sem=recv_sem.at[k],
                device_id=where(peer),
                device_id_type=MESH,
            )
            copy.start()
            copies.append(copy)
        o_ref[me] = x_ref[me]
        for copy in copies:
            copy.wait()

    return pl.pallas_call(
        kernel,
        out_shape=jax.ShapeDtypeStruct(x.shape, x.dtype),
        in_specs=[pl.BlockSpec(memory_space=pltpu.VMEM)],
        out_specs=pl.BlockSpec(memory_space=pltpu.VMEM),
        scratch_shapes=[pltpu.SemaphoreType.DMA((n,)), pltpu.SemaphoreType.DMA((n,))],
        compiler_params=pltpu.CompilerParams(collective_id=cid, has_side_effects=True),
    )(x)


def spatial_exchange(x, n_pos, n_frame, cid):
    _, per, places, width = x.shape

    def kernel(x_ref, o_ref, z_ref, send_sem, recv_sem, fsend_sem, frecv_sem, zsend_sem, zrecv_sem, local_sem):
        fi = lax.axis_index("frame")
        pi = lax.axis_index("pos")
        barrier = pltpu.get_barrier_semaphore()
        for k in range(1, n_pos):
            pl.semaphore_signal(barrier, inc=1, device_id={"pos": (pi + k) % n_pos}, device_id_type=MESH)
        for g in range(1, n_frame):
            pl.semaphore_signal(barrier, inc=1, device_id={"frame": (fi + g) % n_frame}, device_id_type=MESH)
        pl.semaphore_wait(barrier, n_pos - 1 + n_frame - 1)
        copies = []
        for k in range(1, n_pos):
            peer = (pi + k) % n_pos
            copy = pltpu.make_async_remote_copy(
                src_ref=x_ref.at[peer],
                dst_ref=o_ref.at[pi],
                send_sem=send_sem.at[k],
                recv_sem=recv_sem.at[k],
                device_id={"pos": peer},
                device_id_type=MESH,
            )
            copy.start()
            copies.append(copy)
        o_ref[pi] = x_ref[pi]

        def spread(g):
            return pltpu.make_async_remote_copy(
                src_ref=x_ref.at[0, 0],
                dst_ref=z_ref.at[pi],
                send_sem=fsend_sem.at[g],
                recv_sem=frecv_sem,
                device_id={"frame": g},
                device_id_type=MESH,
            )

        @pl.when(fi == 0)
        def _():
            local = pltpu.make_async_copy(x_ref.at[0, 0], z_ref.at[pi], local_sem)
            local.start()
            sends = [spread(g) for g in range(1, n_frame)]
            for send in sends:
                send.start()
            local.wait()
            for send in sends:
                send.wait_send()

        @pl.when(fi != 0)
        def _():
            spread(1).wait_recv()

        for k in range(1, n_pos):
            peer = (pi + k) % n_pos
            copy = pltpu.make_async_remote_copy(
                src_ref=z_ref.at[pi],
                dst_ref=z_ref.at[pi],
                send_sem=zsend_sem.at[k],
                recv_sem=zrecv_sem.at[k],
                device_id={"pos": peer},
                device_id_type=MESH,
            )
            copy.start()
            copies.append(copy)
        for copy in copies:
            copy.wait()

    return pl.pallas_call(
        kernel,
        out_shape=(
            jax.ShapeDtypeStruct(x.shape, x.dtype),
            jax.ShapeDtypeStruct((n_pos, places, width), x.dtype),
        ),
        in_specs=[pl.BlockSpec(memory_space=pltpu.VMEM)],
        out_specs=(pl.BlockSpec(memory_space=pltpu.VMEM), pl.BlockSpec(memory_space=pltpu.VMEM)),
        scratch_shapes=[
            pltpu.SemaphoreType.DMA((n_pos,)),
            pltpu.SemaphoreType.DMA((n_pos,)),
            pltpu.SemaphoreType.DMA((n_frame,)),
            pltpu.SemaphoreType.DMA,
            pltpu.SemaphoreType.DMA((n_pos,)),
            pltpu.SemaphoreType.DMA((n_pos,)),
            pltpu.SemaphoreType.DMA,
        ],
        compiler_params=pltpu.CompilerParams(collective_id=cid, has_side_effects=True),
    )(x)


def spatial_attend(x, q, kt, vt, k0t, v0t, out_w, rows, n_frame, n_pos, cid):
    frames, places, width = x.shape
    depth = width // HEADS
    scale = depth ** (-0.5)
    n_dev = n_frame * n_pos
    run = places // n_dev
    chunks = rows // run

    def kernel(x_ref, q_ref, kt_ref, vt_ref, k0t_ref, v0t_ref, w_ref, o_ref, made, got, send_sem, recv_sem):
        t = pl.program_id(0)
        fi = lax.axis_index("frame")
        pi = lax.axis_index("pos")
        me = fi * n_pos + pi
        barrier = pltpu.get_barrier_semaphore()

        @pl.when(t == 0)
        def _():
            for k in range(1, n_dev):
                peer = (me + k) % n_dev
                pl.semaphore_signal(
                    barrier, inc=1, device_id={"frame": peer // n_pos, "pos": peer % n_pos}, device_id_type=MESH
                )

        base = t * chunks
        for f in range(frames):
            acc = x_ref[f].astype(jnp.float32)
            for h in range(HEADS):
                part = pl.ds(h * depth, depth)
                qh = q_ref[f, :, part]
                own = jnp.dot(qh, kt_ref[f, part, :], preferred_element_type=jnp.float32) * scale
                first = jnp.dot(qh, k0t_ref[part, :], preferred_element_type=jnp.float32) * scale
                high = jnp.maximum(
                    jnp.max(own, axis=-1, keepdims=True), jnp.max(first, axis=-1, keepdims=True)
                )
                own = jnp.exp(own - high)
                first = jnp.exp(first - high)
                totals = jnp.sum(own, axis=-1, keepdims=True) + jnp.sum(first, axis=-1, keepdims=True)
                contract = (((1,), (1,)), ((), ()))
                summed = lax.dot_general(
                    own.astype(jnp.bfloat16), vt_ref[f, part, :], contract, preferred_element_type=jnp.float32
                ) + lax.dot_general(
                    first.astype(jnp.bfloat16), v0t_ref[part, :], contract, preferred_element_type=jnp.float32
                )
                attended = (summed / totals).astype(jnp.bfloat16)
                acc = acc + jnp.dot(attended, w_ref[part, :], preferred_element_type=jnp.float32)
            made[pl.ds(base, chunks), f] = acc.reshape(chunks, run, width).astype(made.dtype)

        @pl.when(t == 0)
        def _():
            pl.semaphore_wait(barrier, n_dev - 1)

        for i in range(chunks):
            gf = i % n_frame
            gp = (base + i) // n_frame

            @pl.when((gf == fi) & (gp == pi))
            def _():
                got[me] = made[base + i]

            @pl.when((gf != fi) | (gp != pi))
            def _():
                pltpu.make_async_remote_copy(
                    src_ref=made.at[base + i],
                    dst_ref=got.at[me],
                    send_sem=send_sem,
                    recv_sem=recv_sem,
                    device_id={"frame": gf, "pos": gp},
                    device_id_type=MESH,
                ).start()

        @pl.when(t == places // rows - 1)
        def _():
            others = pltpu.make_async_copy(got.at[pl.ds(0, n_dev - 1)], got.at[pl.ds(1, n_dev - 1)], recv_sem)
            others.wait()
            sent = pltpu.make_async_copy(got.at[pl.ds(0, n_dev - 1)], got.at[pl.ds(1, n_dev - 1)], send_sem)
            sent.wait()
            o_ref[...] = got[...]

    tile = lambda t: (0, t, 0)
    whole = lambda t: (0, 0, 0)
    fixed = lambda t: (0, 0)
    return pl.pallas_call(
        kernel,
        out_shape=jax.ShapeDtypeStruct((n_dev, frames, run, width), x.dtype),
        grid=(places // rows,),
        in_specs=[
            pl.BlockSpec((frames, rows, width), tile),
            pl.BlockSpec((frames, rows, width), tile),
            pl.BlockSpec((frames, width, places), whole),
            pl.BlockSpec((frames, width, places), whole),
            pl.BlockSpec((width, places), fixed),
            pl.BlockSpec((width, places), fixed),
            pl.BlockSpec((width, width), fixed),
        ],
        out_specs=pl.BlockSpec(memory_space=pltpu.VMEM),
        scratch_shapes=[
            pltpu.VMEM((n_dev, frames, run, width), x.dtype),
            pltpu.VMEM((n_dev, frames, run, width), x.dtype),
            pltpu.SemaphoreType.DMA,
            pltpu.SemaphoreType.DMA,
        ],
        compiler_params=pltpu.CompilerParams(collective_id=cid, has_side_effects=True),
    )(x, q, kt, vt, k0t, v0t, out_w)


def temporal_attend(x, gain, wq, wk, wv, out_w, n_frame, cid, per_step=2):
    run, every, width = x.shape
    depth = width // HEADS
    scale = depth ** (-0.5)
    frames = every // n_frame

    def kernel(x_ref, g_ref, wq_ref, wk_ref, wv_ref, w_ref, o_ref, made, got, send_sem, recv_sem):
        step = pl.program_id(0)
        fi = lax.axis_index("frame")
        barrier = pltpu.get_barrier_semaphore()

        @pl.when(step == 0)
        def _():
            for k in range(1, n_frame):
                pl.semaphore_signal(barrier, inc=1, device_id={"frame": (fi + k) % n_frame}, device_id_type=MESH)

        for s in range(per_step):
            wide = x_ref[s].astype(jnp.float32)
            factor = lax.rsqrt(jnp.mean(wide * wide, axis=-1, keepdims=True) + 1e-06)
            normed_two = (wide * factor * g_ref[...]).astype(jnp.bfloat16)
            q = jnp.dot(normed_two, wq_ref[...], preferred_element_type=jnp.float32).astype(jnp.bfloat16)
            k = jnp.dot(normed_two, wk_ref[...], preferred_element_type=jnp.float32).astype(jnp.bfloat16)
            v = jnp.dot(normed_two, wv_ref[...], preferred_element_type=jnp.float32).astype(jnp.bfloat16)
            acc = wide
            for h in range(HEADS):
                part = slice(h * depth, (h + 1) * depth)
                contract = (((1,), (1,)), ((), ()))
                scores = lax.dot_general(q[:, part], k[:, part], contract, preferred_element_type=jnp.float32) * scale
                weights = jnp.exp(scores - jnp.max(scores, axis=-1, keepdims=True))
                totals = jnp.sum(weights, axis=-1, keepdims=True)
                summed = jnp.dot(weights.astype(jnp.bfloat16), v[:, part], preferred_element_type=jnp.float32)
                attended = (summed / totals).astype(jnp.bfloat16)
                acc = acc + jnp.dot(attended, w_ref[part, :], preferred_element_type=jnp.float32)
            made[step * per_step + s] = acc.astype(made.dtype)

        @pl.when(step == 0)
        def _():
            pl.semaphore_wait(barrier, n_frame - 1)

        these = pl.ds(step * per_step, per_step)
        for g in range(n_frame):
            @pl.when(g == fi)
            def _():
                got[fi, these] = made[these, pl.ds(g * frames, frames)]

            @pl.when(g != fi)
            def _():
                pltpu.make_async_remote_copy(
                    src_ref=made.at[these, pl.ds(g * frames, frames)],
                    dst_ref=got.at[fi, these],
                    send_sem=send_sem,
                    recv_sem=recv_sem,
                    device_id={"frame": g},
                    device_id_type=MESH,
                ).start()

        @pl.when(step == run // per_step - 1)
        def _():
            others = pltpu.make_async_copy(got.at[pl.ds(0, n_frame - 1)], got.at[pl.ds(1, n_frame - 1)], recv_sem)
            others.wait()
            sent = pltpu.make_async_copy(got.at[pl.ds(0, n_frame - 1)], got.at[pl.ds(1, n_frame - 1)], send_sem)
            sent.wait()
            o_ref[...] = got[...]

    fixed = lambda p: (0, 0)
    return pl.pallas_call(
        kernel,
        out_shape=jax.ShapeDtypeStruct((n_frame, run, frames, width), x.dtype),
        grid=(run // per_step,),
        in_specs=[
            pl.BlockSpec((per_step, every, width), lambda p: (p, 0, 0)),
            pl.BlockSpec((1, width), fixed),
            pl.BlockSpec((width, width), fixed),
            pl.BlockSpec((width, width), fixed),
            pl.BlockSpec((width, width), fixed),
            pl.BlockSpec((width, width), fixed),
        ],
        out_specs=pl.BlockSpec(memory_space=pltpu.VMEM),
        scratch_shapes=[
            pltpu.VMEM((run, every, width), x.dtype),
            pltpu.VMEM((n_frame, run, frames, width), x.dtype),
            pltpu.SemaphoreType.DMA,
            pltpu.SemaphoreType.DMA,
        ],
        compiler_params=pltpu.CompilerParams(collective_id=cid, has_side_effects=True),
    )(x, gain.reshape(1, width), wq, wk, wv, out_w)


def transposed(values, weight):
    result = jnp.einsum("...rc,cd->...dr", values, weight, preferred_element_type=jnp.float32)
    return result.astype(jnp.bfloat16)


def normed(values, gain):
    wide = values.astype(jnp.float32)
    factor = lax.rsqrt(jnp.mean(wide * wide, axis=-1, keepdims=True) + 1e-06)
    return (wide * factor * gain).astype(jnp.bfloat16)


def project(values, weight):
    flat = values.reshape(-1, values.shape[-1])
    result = jnp.dot(flat, weight, preferred_element_type=jnp.float32).astype(jnp.bfloat16)
    return result.reshape(values.shape[:-1] + (weight.shape[1],))


def heads_of(values):
    return values.reshape(values.shape[:-1] + (HEADS, values.shape[-1] // HEADS))


def softmax_attend(query, keys, vals, score_form, value_form, total_form):
    scale = query.shape[-1] ** (-0.5)
    scores = jnp.einsum(score_form, query, keys, preferred_element_type=jnp.float32) * scale
    weights = jnp.exp(scores - jnp.max(scores, axis=-1, keepdims=True))
    totals = jnp.sum(weights, axis=-1)
    summed = jnp.einsum(
        value_form, weights.astype(jnp.bfloat16), vals, preferred_element_type=jnp.float32
    )
    return summed / jnp.einsum(total_form, totals)[..., None]


def shards(
    latents,
    gain_one,
    query_one,
    key_one,
    value_one,
    out_one,
    gain_two,
    query_two,
    key_two,
    value_two,
    out_two,
):
    frames, places, width = latents.shape
    n_pos = lax.axis_size("pos")
    n_frame = lax.axis_size("frame")
    per = frames // n_pos
    got, zero = spatial_exchange(latents.reshape(n_pos, per, places, width), n_pos, n_frame, 1)
    xs = got.transpose(1, 0, 2, 3).reshape(per, n_pos * places, width)
    x0 = zero.reshape(n_pos * places, width)

    n_one = normed(xs, gain_one)
    q_one = project(n_one, query_one)
    n_zero = normed(x0, gain_one)
    got = spatial_attend(
        xs,
        q_one,
        transposed(n_one, key_one),
        transposed(n_one, value_one),
        transposed(n_zero, key_one),
        transposed(n_zero, value_one),
        out_one,
        min(256, n_pos * places),
        n_frame,
        n_pos,
        2,
    )
    all_places = n_pos * places
    run = all_places // (n_pos * n_frame)
    mid_t = got.reshape(n_frame * n_pos * per, run, width).transpose(1, 0, 2)
    got = temporal_attend(mid_t, gain_two, query_two, key_two, value_two, out_two, n_frame, 3)
    return got.transpose(2, 0, 1, 3).reshape(frames, places, width)


def solution(mesh):
    return jax.shard_map(
        shards,
        mesh=mesh,
        in_specs=(P("frame", "pos", None), P(), P(), P(), P(), P(), P(), P(), P(), P(), P()),
        out_specs=P("frame", "pos", None),
        check_vma=False,
    )
```

```python
import jax
import jax.numpy as jnp
from jax import lax
from jax.experimental import pallas as pl
from jax.experimental.pallas import tpu as pltpu
from jax.sharding import PartitionSpec as P

HEADS = 4

MESH = pl.DeviceIdType.MESH


def exchange(x, names, sizes, cid):
    n = x.shape[0]

    def where(peer):
        if len(names) == 1:
            return {names[0]: peer}
        return {names[0]: peer // sizes[1], names[1]: peer % sizes[1]}

    def kernel(x_ref, o_ref, send_sem, recv_sem):
        me = lax.axis_index(names[0])
        if len(names) == 2:
            me = me * sizes[1] + lax.axis_index(names[1])
        barrier = pltpu.get_barrier_semaphore()
        for k in range(1, n):
            pl.semaphore_signal(barrier, inc=1, device_id=where((me + k) % n), device_id_type=MESH)
        pl.semaphore_wait(barrier, n - 1)
        copies = []
        for k in range(1, n):
            peer = (me + k) % n
            copy = pltpu.make_async_remote_copy(
                src_ref=x_ref.at[peer],
                dst_ref=o_ref.at[me],
                send_sem=send_sem.at[k],
                recv_sem=recv_sem.at[k],
                device_id=where(peer),
                device_id_type=MESH,
            )
            copy.start()
            copies.append(copy)
        o_ref[me] = x_ref[me]
        for copy in copies:
            copy.wait()

    return pl.pallas_call(
        kernel,
        out_shape=jax.ShapeDtypeStruct(x.shape, x.dtype),
        in_specs=[pl.BlockSpec(memory_space=pltpu.VMEM)],
        out_specs=pl.BlockSpec(memory_space=pltpu.VMEM),
        scratch_shapes=[pltpu.SemaphoreType.DMA((n,)), pltpu.SemaphoreType.DMA((n,))],
        compiler_params=pltpu.CompilerParams(collective_id=cid, has_side_effects=True),
    )(x)


def spatial_exchange(x, n_pos, n_frame, cid):
    _, per, places, width = x.shape

    def kernel(x_ref, o_ref, z_ref, send_sem, recv_sem, fsend_sem, frecv_sem, zsend_sem, zrecv_sem, local_sem):
        fi = lax.axis_index("frame")
        pi = lax.axis_index("pos")
        barrier = pltpu.get_barrier_semaphore()
        for k in range(1, n_pos):
            pl.semaphore_signal(barrier, inc=1, device_id={"pos": (pi + k) % n_pos}, device_id_type=MESH)
        for g in range(1, n_frame):
            pl.semaphore_signal(barrier, inc=1, device_id={"frame": (fi + g) % n_frame}, device_id_type=MESH)
        pl.semaphore_wait(barrier, n_pos - 1 + n_frame - 1)
        def spread(g):
            return pltpu.make_async_remote_copy(
                src_ref=x_ref.at[0, 0],
                dst_ref=z_ref.at[pi],
                send_sem=fsend_sem.at[g],
                recv_sem=frecv_sem,
                device_id={"frame": g},
                device_id_type=MESH,
            )

        @pl.when(fi == 0)
        def _():
            for g in range(1, n_frame):
                spread(g).start()

        copies = []
        for k in range(1, n_pos):
            peer = (pi + k) % n_pos
            copy = pltpu.make_async_remote_copy(
                src_ref=x_ref.at[peer],
                dst_ref=o_ref.at[pi],
                send_sem=send_sem.at[k],
                recv_sem=recv_sem.at[k],
                device_id={"pos": peer},
                device_id_type=MESH,
            )
            copy.start()
            copies.append(copy)

        @pl.when(fi == 0)
        def _():
            local = pltpu.make_async_copy(x_ref.at[0, 0], z_ref.at[pi], local_sem)
            local.start()
            local.wait()

        @pl.when(fi != 0)
        def _():
            spread(1).wait_recv()

        for k in range(1, n_pos):
            peer = (pi + k) % n_pos
            copy = pltpu.make_async_remote_copy(
                src_ref=z_ref.at[pi],
                dst_ref=z_ref.at[pi],
                send_sem=zsend_sem.at[k],
                recv_sem=zrecv_sem.at[k],
                device_id={"pos": peer},
                device_id_type=MESH,
            )
            copy.start()
            copies.append(copy)

        @pl.when(fi == 0)
        def _():
            for g in range(1, n_frame):
                spread(g).wait_send()

        for copy in copies:
            copy.wait()
        o_ref[pi] = x_ref[pi]

    return pl.pallas_call(
        kernel,
        out_shape=(
            jax.ShapeDtypeStruct(x.shape, x.dtype),
            jax.ShapeDtypeStruct((n_pos, places, width), x.dtype),
        ),
        in_specs=[pl.BlockSpec(memory_space=pltpu.VMEM)],
        out_specs=(pl.BlockSpec(memory_space=pltpu.VMEM), pl.BlockSpec(memory_space=pltpu.VMEM)),
        scratch_shapes=[
            pltpu.SemaphoreType.DMA((n_pos,)),
            pltpu.SemaphoreType.DMA((n_pos,)),
            pltpu.SemaphoreType.DMA((n_frame,)),
            pltpu.SemaphoreType.DMA,
            pltpu.SemaphoreType.DMA((n_pos,)),
            pltpu.SemaphoreType.DMA((n_pos,)),
            pltpu.SemaphoreType.DMA,
        ],
        compiler_params=pltpu.CompilerParams(collective_id=cid, has_side_effects=True),
    )(x)


def spatial_attend(x, q, kt, vt, k0t, v0t, out_w, rows, n_frame, n_pos, cid):
    frames, places, width = x.shape
    depth = width // HEADS
    scale = depth ** (-0.5)
    n_dev = n_frame * n_pos
    run = places // n_dev
    chunks = rows // run

    def kernel(x_ref, q_ref, kt_ref, vt_ref, k0t_ref, v0t_ref, w_ref, o_ref, made, got, send_sem, recv_sem):
        t = pl.program_id(0)
        fi = lax.axis_index("frame")
        pi = lax.axis_index("pos")
        me = fi * n_pos + pi
        barrier = pltpu.get_barrier_semaphore()

        @pl.when(t == 0)
        def _():
            for k in range(1, n_dev):
                peer = (me + k) % n_dev
                pl.semaphore_signal(
                    barrier, inc=1, device_id={"frame": peer // n_pos, "pos": peer % n_pos}, device_id_type=MESH
                )

        base = t * chunks
        for f in range(frames):
            acc = x_ref[f].astype(jnp.float32)
            for h in range(HEADS):
                part = pl.ds(h * depth, depth)
                qh = q_ref[f, :, part]
                own = jnp.dot(qh, kt_ref[f, part, :], preferred_element_type=jnp.float32) * scale
                first = jnp.dot(qh, k0t_ref[part, :], preferred_element_type=jnp.float32) * scale
                high = jnp.maximum(
                    jnp.max(own, axis=-1, keepdims=True), jnp.max(first, axis=-1, keepdims=True)
                )
                own = jnp.exp(own - high)
                first = jnp.exp(first - high)
                totals = jnp.sum(own, axis=-1, keepdims=True) + jnp.sum(first, axis=-1, keepdims=True)
                contract = (((1,), (1,)), ((), ()))
                summed = lax.dot_general(
                    own.astype(jnp.bfloat16), vt_ref[f, part, :], contract, preferred_element_type=jnp.float32
                ) + lax.dot_general(
                    first.astype(jnp.bfloat16), v0t_ref[part, :], contract, preferred_element_type=jnp.float32
                )
                attended = (summed / totals).astype(jnp.bfloat16)
                acc = acc + jnp.dot(attended, w_ref[part, :], preferred_element_type=jnp.float32)
            made[pl.ds(base, chunks), f] = acc.reshape(chunks, run, width).astype(made.dtype)

        @pl.when(t == 0)
        def _():
            pl.semaphore_wait(barrier, n_dev - 1)

        for i in range(chunks):
            gf = i % n_frame
            gp = (base + i) // n_frame

            @pl.when((gf == fi) & (gp == pi))
            def _():
                got[me] = made[base + i]

            @pl.when((gf != fi) | (gp != pi))
            def _():
                pltpu.make_async_remote_copy(
                    src_ref=made.at[base + i],
                    dst_ref=got.at[me],
                    send_sem=send_sem,
                    recv_sem=recv_sem,
                    device_id={"frame": gf, "pos": gp},
                    device_id_type=MESH,
                ).start()

        @pl.when(t == places // rows - 1)
        def _():
            others = pltpu.make_async_copy(got.at[pl.ds(0, n_dev - 1)], got.at[pl.ds(1, n_dev - 1)], recv_sem)
            others.wait()
            sent = pltpu.make_async_copy(got.at[pl.ds(0, n_dev - 1)], got.at[pl.ds(1, n_dev - 1)], send_sem)
            sent.wait()
            o_ref[...] = got[...]

    tile = lambda t: (0, t, 0)
    whole = lambda t: (0, 0, 0)
    fixed = lambda t: (0, 0)
    return pl.pallas_call(
        kernel,
        out_shape=jax.ShapeDtypeStruct((n_dev, frames, run, width), x.dtype),
        grid=(places // rows,),
        in_specs=[
            pl.BlockSpec((frames, rows, width), tile),
            pl.BlockSpec((frames, rows, width), tile),
            pl.BlockSpec((frames, width, places), whole),
            pl.BlockSpec((frames, width, places), whole),
            pl.BlockSpec((width, places), fixed),
            pl.BlockSpec((width, places), fixed),
            pl.BlockSpec((width, width), fixed),
        ],
        out_specs=pl.BlockSpec(memory_space=pltpu.VMEM),
        scratch_shapes=[
            pltpu.VMEM((n_dev, frames, run, width), x.dtype),
            pltpu.VMEM((n_dev, frames, run, width), x.dtype),
            pltpu.SemaphoreType.DMA,
            pltpu.SemaphoreType.DMA,
        ],
        compiler_params=pltpu.CompilerParams(collective_id=cid, has_side_effects=True),
    )(x, q, kt, vt, k0t, v0t, out_w)


def temporal_attend(x, gain, wq, wk, wv, out_w, n_frame, cid, per_step=2):
    run, every, width = x.shape
    depth = width // HEADS
    scale = depth ** (-0.5)
    frames = every // n_frame

    def kernel(x_ref, g_ref, wq_ref, wk_ref, wv_ref, w_ref, o_ref, made, got, send_sem, recv_sem):
        step = pl.program_id(0)
        fi = lax.axis_index("frame")
        barrier = pltpu.get_barrier_semaphore()

        @pl.when(step == 0)
        def _():
            for k in range(1, n_frame):
                pl.semaphore_signal(barrier, inc=1, device_id={"frame": (fi + k) % n_frame}, device_id_type=MESH)

        for s in range(per_step):
            wide = x_ref[s].astype(jnp.float32)
            factor = lax.rsqrt(jnp.mean(wide * wide, axis=-1, keepdims=True) + 1e-06)
            normed_two = (wide * factor * g_ref[...]).astype(jnp.bfloat16)
            q = jnp.dot(normed_two, wq_ref[...], preferred_element_type=jnp.float32).astype(jnp.bfloat16)
            k = jnp.dot(normed_two, wk_ref[...], preferred_element_type=jnp.float32).astype(jnp.bfloat16)
            v = jnp.dot(normed_two, wv_ref[...], preferred_element_type=jnp.float32).astype(jnp.bfloat16)
            acc = wide
            for h in range(HEADS):
                part = slice(h * depth, (h + 1) * depth)
                contract = (((1,), (1,)), ((), ()))
                scores = lax.dot_general(q[:, part], k[:, part], contract, preferred_element_type=jnp.float32) * scale
                weights = jnp.exp(scores - jnp.max(scores, axis=-1, keepdims=True))
                totals = jnp.sum(weights, axis=-1, keepdims=True)
                summed = jnp.dot(weights.astype(jnp.bfloat16), v[:, part], preferred_element_type=jnp.float32)
                attended = (summed / totals).astype(jnp.bfloat16)
                acc = acc + jnp.dot(attended, w_ref[part, :], preferred_element_type=jnp.float32)
            made[step * per_step + s] = acc.astype(made.dtype)

        @pl.when(step == 0)
        def _():
            pl.semaphore_wait(barrier, n_frame - 1)

        these = pl.ds(step * per_step, per_step)
        for g in range(n_frame):
            @pl.when(g == fi)
            def _():
                got[fi, these] = made[these, pl.ds(g * frames, frames)]

            @pl.when(g != fi)
            def _():
                pltpu.make_async_remote_copy(
                    src_ref=made.at[these, pl.ds(g * frames, frames)],
                    dst_ref=got.at[fi, these],
                    send_sem=send_sem,
                    recv_sem=recv_sem,
                    device_id={"frame": g},
                    device_id_type=MESH,
                ).start()

        @pl.when(step == run // per_step - 1)
        def _():
            others = pltpu.make_async_copy(got.at[pl.ds(0, n_frame - 1)], got.at[pl.ds(1, n_frame - 1)], recv_sem)
            others.wait()
            sent = pltpu.make_async_copy(got.at[pl.ds(0, n_frame - 1)], got.at[pl.ds(1, n_frame - 1)], send_sem)
            sent.wait()
            o_ref[...] = got[...]

    fixed = lambda p: (0, 0)
    return pl.pallas_call(
        kernel,
        out_shape=jax.ShapeDtypeStruct((n_frame, run, frames, width), x.dtype),
        grid=(run // per_step,),
        in_specs=[
            pl.BlockSpec((per_step, every, width), lambda p: (p, 0, 0)),
            pl.BlockSpec((1, width), fixed),
            pl.BlockSpec((width, width), fixed),
            pl.BlockSpec((width, width), fixed),
            pl.BlockSpec((width, width), fixed),
            pl.BlockSpec((width, width), fixed),
        ],
        out_specs=pl.BlockSpec(memory_space=pltpu.VMEM),
        scratch_shapes=[
            pltpu.VMEM((run, every, width), x.dtype),
            pltpu.VMEM((n_frame, run, frames, width), x.dtype),
            pltpu.SemaphoreType.DMA,
            pltpu.SemaphoreType.DMA,
        ],
        compiler_params=pltpu.CompilerParams(collective_id=cid, has_side_effects=True),
    )(x, gain.reshape(1, width), wq, wk, wv, out_w)


def transposed(values, weight):
    result = jnp.einsum("...rc,cd->...dr", values, weight, preferred_element_type=jnp.float32)
    return result.astype(jnp.bfloat16)


def normed(values, gain):
    wide = values.astype(jnp.float32)
    factor = lax.rsqrt(jnp.mean(wide * wide, axis=-1, keepdims=True) + 1e-06)
    return (wide * factor * gain).astype(jnp.bfloat16)


def project(values, weight):
    flat = values.reshape(-1, values.shape[-1])
    result = jnp.dot(flat, weight, preferred_element_type=jnp.float32).astype(jnp.bfloat16)
    return result.reshape(values.shape[:-1] + (weight.shape[1],))


def heads_of(values):
    return values.reshape(values.shape[:-1] + (HEADS, values.shape[-1] // HEADS))


def softmax_attend(query, keys, vals, score_form, value_form, total_form):
    scale = query.shape[-1] ** (-0.5)
    scores = jnp.einsum(score_form, query, keys, preferred_element_type=jnp.float32) * scale
    weights = jnp.exp(scores - jnp.max(scores, axis=-1, keepdims=True))
    totals = jnp.sum(weights, axis=-1)
    summed = jnp.einsum(
        value_form, weights.astype(jnp.bfloat16), vals, preferred_element_type=jnp.float32
    )
    return summed / jnp.einsum(total_form, totals)[..., None]


def shards(
    latents,
    gain_one,
    query_one,
    key_one,
    value_one,
    out_one,
    gain_two,
    query_two,
    key_two,
    value_two,
    out_two,
):
    frames, places, width = latents.shape
    n_pos = lax.axis_size("pos")
    n_frame = lax.axis_size("frame")
    per = frames // n_pos
    got, zero = spatial_exchange(latents.reshape(n_pos, per, places, width), n_pos, n_frame, 1)
    xs = got.transpose(1, 0, 2, 3).reshape(per, n_pos * places, width)
    x0 = zero.reshape(n_pos * places, width)

    n_one = normed(xs, gain_one)
    q_one = project(n_one, query_one)
    n_zero = normed(x0, gain_one)
    got = spatial_attend(
        xs,
        q_one,
        transposed(n_one, key_one),
        transposed(n_one, value_one),
        transposed(n_zero, key_one),
        transposed(n_zero, value_one),
        out_one,
        min(256, n_pos * places),
        n_frame,
        n_pos,
        2,
    )
    all_places = n_pos * places
    run = all_places // (n_pos * n_frame)
    mid_t = got.reshape(n_frame * n_pos * per, run, width).transpose(1, 0, 2)
    got = temporal_attend(mid_t, gain_two, query_two, key_two, value_two, out_two, n_frame, 3)
    return got.transpose(2, 0, 1, 3).reshape(frames, places, width)


def solution(mesh):
    return jax.shard_map(
        shards,
        mesh=mesh,
        in_specs=(P("frame", "pos", None), P(), P(), P(), P(), P(), P(), P(), P(), P(), P()),
        out_specs=P("frame", "pos", None),
        check_vma=False,
    )
```

```python
import jax
import jax.numpy as jnp
from jax import lax
from jax.experimental import pallas as pl
from jax.experimental.pallas import tpu as pltpu
from jax.sharding import PartitionSpec as P

HEADS = 4

MESH = pl.DeviceIdType.MESH


def exchange(x, names, sizes, cid):
    n = x.shape[0]

    def where(peer):
        if len(names) == 1:
            return {names[0]: peer}
        return {names[0]: peer // sizes[1], names[1]: peer % sizes[1]}

    def kernel(x_ref, o_ref, send_sem, recv_sem):
        me = lax.axis_index(names[0])
        if len(names) == 2:
            me = me * sizes[1] + lax.axis_index(names[1])
        barrier = pltpu.get_barrier_semaphore()
        for k in range(1, n):
            pl.semaphore_signal(barrier, inc=1, device_id=where((me + k) % n), device_id_type=MESH)
        pl.semaphore_wait(barrier, n - 1)
        copies = []
        for k in range(1, n):
            peer = (me + k) % n
            copy = pltpu.make_async_remote_copy(
                src_ref=x_ref.at[peer],
                dst_ref=o_ref.at[me],
                send_sem=send_sem.at[k],
                recv_sem=recv_sem.at[k],
                device_id=where(peer),
                device_id_type=MESH,
            )
            copy.start()
            copies.append(copy)
        o_ref[me] = x_ref[me]
        for copy in copies:
            copy.wait()

    return pl.pallas_call(
        kernel,
        out_shape=jax.ShapeDtypeStruct(x.shape, x.dtype),
        in_specs=[pl.BlockSpec(memory_space=pltpu.VMEM)],
        out_specs=pl.BlockSpec(memory_space=pltpu.VMEM),
        scratch_shapes=[pltpu.SemaphoreType.DMA((n,)), pltpu.SemaphoreType.DMA((n,))],
        compiler_params=pltpu.CompilerParams(collective_id=cid, has_side_effects=True),
    )(x)


def spatial_exchange(x, n_pos, n_frame, cid):
    _, per, places, width = x.shape

    def kernel(x_ref, o_ref, z_ref, send_sem, recv_sem, fsend_sem, frecv_sem, zsend_sem, zrecv_sem, local_sem):
        fi = lax.axis_index("frame")
        pi = lax.axis_index("pos")
        barrier = pltpu.get_barrier_semaphore()
        for k in range(1, n_pos):
            pl.semaphore_signal(barrier, inc=1, device_id={"pos": (pi + k) % n_pos}, device_id_type=MESH)
        for g in range(1, n_frame):
            pl.semaphore_signal(barrier, inc=1, device_id={"frame": (fi + g) % n_frame}, device_id_type=MESH)
        pl.semaphore_wait(barrier, n_pos - 1 + n_frame - 1)
        def spread(g):
            return pltpu.make_async_remote_copy(
                src_ref=x_ref.at[0, 0],
                dst_ref=z_ref.at[pi],
                send_sem=fsend_sem.at[g],
                recv_sem=frecv_sem,
                device_id={"frame": g},
                device_id_type=MESH,
            )

        @pl.when(fi == 0)
        def _():
            for g in range(1, n_frame):
                spread(g).start()

        copies = []
        for k in range(1, n_pos):
            peer = (pi + k) % n_pos
            copy = pltpu.make_async_remote_copy(
                src_ref=x_ref.at[peer],
                dst_ref=o_ref.at[pi],
                send_sem=send_sem.at[k],
                recv_sem=recv_sem.at[k],
                device_id={"pos": peer},
                device_id_type=MESH,
            )
            copy.start()
            copies.append(copy)

        @pl.when(fi == 0)
        def _():
            local = pltpu.make_async_copy(x_ref.at[0, 0], z_ref.at[pi], local_sem)
            local.start()
            local.wait()

        @pl.when(fi != 0)
        def _():
            spread(1).wait_recv()

        for k in range(1, n_pos):
            peer = (pi + k) % n_pos
            copy = pltpu.make_async_remote_copy(
                src_ref=z_ref.at[pi],
                dst_ref=z_ref.at[pi],
                send_sem=zsend_sem.at[k],
                recv_sem=zrecv_sem.at[k],
                device_id={"pos": peer},
                device_id_type=MESH,
            )
            copy.start()
            copies.append(copy)

        @pl.when(fi == 0)
        def _():
            for g in range(1, n_frame):
                spread(g).wait_send()

        for copy in copies:
            copy.wait()
        o_ref[pi] = x_ref[pi]

    return pl.pallas_call(
        kernel,
        out_shape=(
            jax.ShapeDtypeStruct(x.shape, x.dtype),
            jax.ShapeDtypeStruct((n_pos, places, width), x.dtype),
        ),
        in_specs=[pl.BlockSpec(memory_space=pltpu.VMEM)],
        out_specs=(pl.BlockSpec(memory_space=pltpu.VMEM), pl.BlockSpec(memory_space=pltpu.VMEM)),
        scratch_shapes=[
            pltpu.SemaphoreType.DMA((n_pos,)),
            pltpu.SemaphoreType.DMA((n_pos,)),
            pltpu.SemaphoreType.DMA((n_frame,)),
            pltpu.SemaphoreType.DMA,
            pltpu.SemaphoreType.DMA((n_pos,)),
            pltpu.SemaphoreType.DMA((n_pos,)),
            pltpu.SemaphoreType.DMA,
        ],
        compiler_params=pltpu.CompilerParams(collective_id=cid, has_side_effects=True),
    )(x)


def spatial_attend(x, q, kt, vt, k0t, v0t, out_w, rows, n_frame, n_pos, cid):
    frames, places, width = x.shape
    depth = width // HEADS
    scale = depth ** (-0.5)
    n_dev = n_frame * n_pos
    run = places // n_dev
    chunks = rows // run
    n_tiles = places // rows

    def kernel(x_ref, q_ref, kt_ref, vt_ref, k0t_ref, v0t_ref, w_ref, o_ref, made, got, send_sem, recv_sem):
        t = pl.program_id(0)
        fi = lax.axis_index("frame")
        pi = lax.axis_index("pos")
        me = fi * n_pos + pi
        barrier = pltpu.get_barrier_semaphore()

        @pl.when(t == 0)
        def _():
            for k in range(1, n_dev):
                peer = (me + k) % n_dev
                pl.semaphore_signal(
                    barrier, inc=1, device_id={"frame": peer // n_pos, "pos": peer % n_pos}, device_id_type=MESH
                )

        tt = (t + fi + pi) % n_tiles
        base = tt * chunks
        these = pl.ds(pl.multiple_of(tt * rows, rows), rows)
        for f in range(frames):
            acc = x_ref[f, these, :].astype(jnp.float32)
            for h in range(HEADS):
                part = pl.ds(h * depth, depth)
                qh = q_ref[f, these, part]
                own = jnp.dot(qh, kt_ref[f, part, :], preferred_element_type=jnp.float32) * scale
                first = jnp.dot(qh, k0t_ref[part, :], preferred_element_type=jnp.float32) * scale
                high = jnp.maximum(
                    jnp.max(own, axis=-1, keepdims=True), jnp.max(first, axis=-1, keepdims=True)
                )
                own = jnp.exp(own - high)
                first = jnp.exp(first - high)
                totals = jnp.sum(own, axis=-1, keepdims=True) + jnp.sum(first, axis=-1, keepdims=True)
                contract = (((1,), (1,)), ((), ()))
                summed = lax.dot_general(
                    own.astype(jnp.bfloat16), vt_ref[f, part, :], contract, preferred_element_type=jnp.float32
                ) + lax.dot_general(
                    first.astype(jnp.bfloat16), v0t_ref[part, :], contract, preferred_element_type=jnp.float32
                )
                attended = (summed / totals).astype(jnp.bfloat16)
                acc = acc + jnp.dot(attended, w_ref[part, :], preferred_element_type=jnp.float32)
            made[pl.ds(base, chunks), f] = acc.reshape(chunks, run, width).astype(made.dtype)

        @pl.when(t == 0)
        def _():
            pl.semaphore_wait(barrier, n_dev - 1)

        for i in range(chunks):
            gf = i % n_frame
            gp = (base + i) // n_frame

            @pl.when((gf == fi) & (gp == pi))
            def _():
                got[me] = made[base + i]

            @pl.when((gf != fi) | (gp != pi))
            def _():
                pltpu.make_async_remote_copy(
                    src_ref=made.at[base + i],
                    dst_ref=got.at[me],
                    send_sem=send_sem,
                    recv_sem=recv_sem,
                    device_id={"frame": gf, "pos": gp},
                    device_id_type=MESH,
                ).start()

        @pl.when(t == n_tiles - 1)
        def _():
            others = pltpu.make_async_copy(got.at[pl.ds(0, n_dev - 1)], got.at[pl.ds(1, n_dev - 1)], recv_sem)
            others.wait()
            sent = pltpu.make_async_copy(got.at[pl.ds(0, n_dev - 1)], got.at[pl.ds(1, n_dev - 1)], send_sem)
            sent.wait()
            o_ref[...] = got[...]

    whole = lambda t: (0, 0, 0)
    fixed = lambda t: (0, 0)
    return pl.pallas_call(
        kernel,
        out_shape=jax.ShapeDtypeStruct((n_dev, frames, run, width), x.dtype),
        grid=(n_tiles,),
        in_specs=[
            pl.BlockSpec(memory_space=pltpu.VMEM),
            pl.BlockSpec(memory_space=pltpu.VMEM),
            pl.BlockSpec((frames, width, places), whole),
            pl.BlockSpec((frames, width, places), whole),
            pl.BlockSpec((width, places), fixed),
            pl.BlockSpec((width, places), fixed),
            pl.BlockSpec((width, width), fixed),
        ],
        out_specs=pl.BlockSpec(memory_space=pltpu.VMEM),
        scratch_shapes=[
            pltpu.VMEM((n_dev, frames, run, width), x.dtype),
            pltpu.VMEM((n_dev, frames, run, width), x.dtype),
            pltpu.SemaphoreType.DMA,
            pltpu.SemaphoreType.DMA,
        ],
        compiler_params=pltpu.CompilerParams(collective_id=cid, has_side_effects=True),
    )(x, q, kt, vt, k0t, v0t, out_w)


def temporal_attend(x, gain, wq, wk, wv, out_w, n_frame, cid, per_step=2):
    run, every, width = x.shape
    depth = width // HEADS
    scale = depth ** (-0.5)
    frames = every // n_frame

    def kernel(x_ref, g_ref, wq_ref, wk_ref, wv_ref, w_ref, o_ref, made, got, send_sem, recv_sem):
        step = pl.program_id(0)
        fi = lax.axis_index("frame")
        barrier = pltpu.get_barrier_semaphore()

        @pl.when(step == 0)
        def _():
            for k in range(1, n_frame):
                pl.semaphore_signal(barrier, inc=1, device_id={"frame": (fi + k) % n_frame}, device_id_type=MESH)

        for s in range(per_step):
            wide = x_ref[s].astype(jnp.float32)
            factor = lax.rsqrt(jnp.mean(wide * wide, axis=-1, keepdims=True) + 1e-06)
            normed_two = (wide * factor * g_ref[...]).astype(jnp.bfloat16)
            q = jnp.dot(normed_two, wq_ref[...], preferred_element_type=jnp.float32).astype(jnp.bfloat16)
            k = jnp.dot(normed_two, wk_ref[...], preferred_element_type=jnp.float32).astype(jnp.bfloat16)
            v = jnp.dot(normed_two, wv_ref[...], preferred_element_type=jnp.float32).astype(jnp.bfloat16)
            acc = wide
            for h in range(HEADS):
                part = slice(h * depth, (h + 1) * depth)
                contract = (((1,), (1,)), ((), ()))
                scores = lax.dot_general(q[:, part], k[:, part], contract, preferred_element_type=jnp.float32) * scale
                weights = jnp.exp(scores - jnp.max(scores, axis=-1, keepdims=True))
                totals = jnp.sum(weights, axis=-1, keepdims=True)
                summed = jnp.dot(weights.astype(jnp.bfloat16), v[:, part], preferred_element_type=jnp.float32)
                attended = (summed / totals).astype(jnp.bfloat16)
                acc = acc + jnp.dot(attended, w_ref[part, :], preferred_element_type=jnp.float32)
            made[step * per_step + s] = acc.astype(made.dtype)

        @pl.when(step == 0)
        def _():
            pl.semaphore_wait(barrier, n_frame - 1)

        these = pl.ds(step * per_step, per_step)
        for g in range(n_frame):
            @pl.when(g == fi)
            def _():
                got[fi, these] = made[these, pl.ds(g * frames, frames)]

            @pl.when(g != fi)
            def _():
                pltpu.make_async_remote_copy(
                    src_ref=made.at[these, pl.ds(g * frames, frames)],
                    dst_ref=got.at[fi, these],
                    send_sem=send_sem,
                    recv_sem=recv_sem,
                    device_id={"frame": g},
                    device_id_type=MESH,
                ).start()

        @pl.when(step == run // per_step - 1)
        def _():
            others = pltpu.make_async_copy(got.at[pl.ds(0, n_frame - 1)], got.at[pl.ds(1, n_frame - 1)], recv_sem)
            others.wait()
            sent = pltpu.make_async_copy(got.at[pl.ds(0, n_frame - 1)], got.at[pl.ds(1, n_frame - 1)], send_sem)
            sent.wait()
            o_ref[...] = got[...]

    fixed = lambda p: (0, 0)
    return pl.pallas_call(
        kernel,
        out_shape=jax.ShapeDtypeStruct((n_frame, run, frames, width), x.dtype),
        grid=(run // per_step,),
        in_specs=[
            pl.BlockSpec((per_step, every, width), lambda p: (p, 0, 0)),
            pl.BlockSpec((1, width), fixed),
            pl.BlockSpec((width, width), fixed),
            pl.BlockSpec((width, width), fixed),
            pl.BlockSpec((width, width), fixed),
            pl.BlockSpec((width, width), fixed),
        ],
        out_specs=pl.BlockSpec(memory_space=pltpu.VMEM),
        scratch_shapes=[
            pltpu.VMEM((run, every, width), x.dtype),
            pltpu.VMEM((n_frame, run, frames, width), x.dtype),
            pltpu.SemaphoreType.DMA,
            pltpu.SemaphoreType.DMA,
        ],
        compiler_params=pltpu.CompilerParams(collective_id=cid, has_side_effects=True),
    )(x, gain.reshape(1, width), wq, wk, wv, out_w)


def transposed(values, weight):
    result = jnp.einsum("...rc,cd->...dr", values, weight, preferred_element_type=jnp.float32)
    return result.astype(jnp.bfloat16)


def normed(values, gain):
    wide = values.astype(jnp.float32)
    factor = lax.rsqrt(jnp.mean(wide * wide, axis=-1, keepdims=True) + 1e-06)
    return (wide * factor * gain).astype(jnp.bfloat16)


def project(values, weight):
    flat = values.reshape(-1, values.shape[-1])
    result = jnp.dot(flat, weight, preferred_element_type=jnp.float32).astype(jnp.bfloat16)
    return result.reshape(values.shape[:-1] + (weight.shape[1],))


def heads_of(values):
    return values.reshape(values.shape[:-1] + (HEADS, values.shape[-1] // HEADS))


def softmax_attend(query, keys, vals, score_form, value_form, total_form):
    scale = query.shape[-1] ** (-0.5)
    scores = jnp.einsum(score_form, query, keys, preferred_element_type=jnp.float32) * scale
    weights = jnp.exp(scores - jnp.max(scores, axis=-1, keepdims=True))
    totals = jnp.sum(weights, axis=-1)
    summed = jnp.einsum(
        value_form, weights.astype(jnp.bfloat16), vals, preferred_element_type=jnp.float32
    )
    return summed / jnp.einsum(total_form, totals)[..., None]


def shards(
    latents,
    gain_one,
    query_one,
    key_one,
    value_one,
    out_one,
    gain_two,
    query_two,
    key_two,
    value_two,
    out_two,
):
    frames, places, width = latents.shape
    n_pos = lax.axis_size("pos")
    n_frame = lax.axis_size("frame")
    per = frames // n_pos
    got, zero = spatial_exchange(latents.reshape(n_pos, per, places, width), n_pos, n_frame, 1)
    xs = got.transpose(1, 0, 2, 3).reshape(per, n_pos * places, width)
    x0 = zero.reshape(n_pos * places, width)

    n_one = normed(xs, gain_one)
    q_one = project(n_one, query_one)
    n_zero = normed(x0, gain_one)
    got = spatial_attend(
        xs,
        q_one,
        transposed(n_one, key_one),
        transposed(n_one, value_one),
        transposed(n_zero, key_one),
        transposed(n_zero, value_one),
        out_one,
        min(256, n_pos * places),
        n_frame,
        n_pos,
        2,
    )
    all_places = n_pos * places
    run = all_places // (n_pos * n_frame)
    mid_t = got.reshape(n_frame * n_pos * per, run, width).transpose(1, 0, 2)
    got = temporal_attend(mid_t, gain_two, query_two, key_two, value_two, out_two, n_frame, 3)
    return got.transpose(2, 0, 1, 3).reshape(frames, places, width)


def solution(mesh):
    return jax.shard_map(
        shards,
        mesh=mesh,
        in_specs=(P("frame", "pos", None), P(), P(), P(), P(), P(), P(), P(), P(), P(), P()),
        out_specs=P("frame", "pos", None),
        check_vma=False,
    )
```

```python
import jax
import jax.numpy as jnp
from jax import lax
from jax.experimental import pallas as pl
from jax.experimental.pallas import tpu as pltpu
from jax.sharding import PartitionSpec as P

HEADS = 4

MESH = pl.DeviceIdType.MESH


def exchange(x, names, sizes, cid):
    n = x.shape[0]

    def where(peer):
        if len(names) == 1:
            return {names[0]: peer}
        return {names[0]: peer // sizes[1], names[1]: peer % sizes[1]}

    def kernel(x_ref, o_ref, send_sem, recv_sem):
        me = lax.axis_index(names[0])
        if len(names) == 2:
            me = me * sizes[1] + lax.axis_index(names[1])
        barrier = pltpu.get_barrier_semaphore()
        for k in range(1, n):
            pl.semaphore_signal(barrier, inc=1, device_id=where((me + k) % n), device_id_type=MESH)
        pl.semaphore_wait(barrier, n - 1)
        copies = []
        for k in range(1, n):
            peer = (me + k) % n
            copy = pltpu.make_async_remote_copy(
                src_ref=x_ref.at[peer],
                dst_ref=o_ref.at[me],
                send_sem=send_sem.at[k],
                recv_sem=recv_sem.at[k],
                device_id=where(peer),
                device_id_type=MESH,
            )
            copy.start()
            copies.append(copy)
        o_ref[me] = x_ref[me]
        for copy in copies:
            copy.wait()

    return pl.pallas_call(
        kernel,
        out_shape=jax.ShapeDtypeStruct(x.shape, x.dtype),
        in_specs=[pl.BlockSpec(memory_space=pltpu.VMEM)],
        out_specs=pl.BlockSpec(memory_space=pltpu.VMEM),
        scratch_shapes=[pltpu.SemaphoreType.DMA((n,)), pltpu.SemaphoreType.DMA((n,))],
        compiler_params=pltpu.CompilerParams(collective_id=cid, has_side_effects=True),
    )(x)


def spatial_exchange(x, n_pos, n_frame, cid):
    _, per, places, width = x.shape

    def kernel(x_ref, o_ref, z_ref, send_sem, recv_sem, fsend_sem, frecv_sem, zsend_sem, zrecv_sem, local_sem):
        fi = lax.axis_index("frame")
        pi = lax.axis_index("pos")
        barrier = pltpu.get_barrier_semaphore()
        for k in range(1, n_pos):
            pl.semaphore_signal(barrier, inc=1, device_id={"pos": (pi + k) % n_pos}, device_id_type=MESH)
        for g in range(1, n_frame):
            pl.semaphore_signal(barrier, inc=1, device_id={"frame": (fi + g) % n_frame}, device_id_type=MESH)
        pl.semaphore_wait(barrier, n_pos - 1 + n_frame - 1)
        def spread(g):
            return pltpu.make_async_remote_copy(
                src_ref=x_ref.at[0, 0],
                dst_ref=z_ref.at[pi],
                send_sem=fsend_sem.at[g],
                recv_sem=frecv_sem,
                device_id={"frame": g},
                device_id_type=MESH,
            )

        @pl.when(fi == 0)
        def _():
            for g in range(1, n_frame):
                spread(g).start()

        copies = []
        for k in range(1, n_pos):
            peer = (pi + k) % n_pos
            copy = pltpu.make_async_remote_copy(
                src_ref=x_ref.at[peer],
                dst_ref=o_ref.at[pi],
                send_sem=send_sem.at[k],
                recv_sem=recv_sem.at[k],
                device_id={"pos": peer},
                device_id_type=MESH,
            )
            copy.start()
            copies.append(copy)

        @pl.when(fi == 0)
        def _():
            local = pltpu.make_async_copy(x_ref.at[0, 0], z_ref.at[pi], local_sem)
            local.start()
            local.wait()

        @pl.when(fi != 0)
        def _():
            spread(1).wait_recv()

        for k in range(1, n_pos):
            peer = (pi + k) % n_pos
            copy = pltpu.make_async_remote_copy(
                src_ref=z_ref.at[pi],
                dst_ref=z_ref.at[pi],
                send_sem=zsend_sem.at[k],
                recv_sem=zrecv_sem.at[k],
                device_id={"pos": peer},
                device_id_type=MESH,
            )
            copy.start()
            copies.append(copy)

        @pl.when(fi == 0)
        def _():
            for g in range(1, n_frame):
                spread(g).wait_send()

        for copy in copies:
            copy.wait()
        o_ref[pi] = x_ref[pi]

    return pl.pallas_call(
        kernel,
        out_shape=(
            jax.ShapeDtypeStruct(x.shape, x.dtype),
            jax.ShapeDtypeStruct((n_pos, places, width), x.dtype),
        ),
        in_specs=[pl.BlockSpec(memory_space=pltpu.VMEM)],
        out_specs=(pl.BlockSpec(memory_space=pltpu.VMEM), pl.BlockSpec(memory_space=pltpu.VMEM)),
        scratch_shapes=[
            pltpu.SemaphoreType.DMA((n_pos,)),
            pltpu.SemaphoreType.DMA((n_pos,)),
            pltpu.SemaphoreType.DMA((n_frame,)),
            pltpu.SemaphoreType.DMA,
            pltpu.SemaphoreType.DMA((n_pos,)),
            pltpu.SemaphoreType.DMA((n_pos,)),
            pltpu.SemaphoreType.DMA,
        ],
        compiler_params=pltpu.CompilerParams(collective_id=cid, has_side_effects=True),
    )(x)


def spatial_attend(got_in, zero, gain, wq, wk, wv, out_w, rows, n_frame, n_pos, cid):
    _, frames, slab, width = got_in.shape
    places = n_pos * slab
    depth = width // HEADS
    scale = depth ** (-0.5)
    n_dev = n_frame * n_pos
    run = places // n_dev
    chunks = rows // run
    n_tiles = places // rows
    per_tile = rows // slab

    def kernel(x_ref, z_ref, g_ref, wq_ref, wkt_ref, wvt_ref, w_ref, o_ref,
               q_ref, kt_ref, vt_ref, k0t_ref, v0t_ref, made, got, send_sem, recv_sem):
        t = pl.program_id(0)
        fi = lax.axis_index("frame")
        pi = lax.axis_index("pos")
        me = fi * n_pos + pi
        barrier = pltpu.get_barrier_semaphore()
        contract = (((1,), (1,)), ((), ()))

        def normed_rows(values):
            wide = values.reshape(places, width).astype(jnp.float32)
            factor = lax.rsqrt(jnp.mean(wide * wide, axis=-1, keepdims=True) + 1e-06)
            return (wide * factor * g_ref[...]).astype(jnp.bfloat16)

        def channels_first(weight_t, values):
            return lax.dot_general(weight_t, values, contract, preferred_element_type=jnp.float32).astype(jnp.bfloat16)

        @pl.when(t == 0)
        def _():
            for k in range(1, n_dev):
                peer = (me + k) % n_dev
                pl.semaphore_signal(
                    barrier, inc=1, device_id={"frame": peer // n_pos, "pos": peer % n_pos}, device_id_type=MESH
                )
            for f in range(frames):
                normed_one = normed_rows(x_ref[:, f])
                q_ref[f] = jnp.dot(normed_one, wq_ref[...], preferred_element_type=jnp.float32).astype(jnp.bfloat16)
                kt_ref[f] = channels_first(wkt_ref[...], normed_one)
                vt_ref[f] = channels_first(wvt_ref[...], normed_one)
            normed_zero = normed_rows(z_ref[...])
            k0t_ref[...] = channels_first(wkt_ref[...], normed_zero)
            v0t_ref[...] = channels_first(wvt_ref[...], normed_zero)

        tt = (t + fi + pi) % n_tiles
        base = tt * chunks
        these = pl.ds(pl.multiple_of(tt * rows, rows), rows)
        for f in range(frames):
            acc = x_ref[pl.ds(tt * per_tile, per_tile), f].reshape(rows, width).astype(jnp.float32)
            for h in range(HEADS):
                part = pl.ds(h * depth, depth)
                qh = q_ref[f, these, part]
                own = jnp.dot(qh, kt_ref[f, part, :], preferred_element_type=jnp.float32) * scale
                first = jnp.dot(qh, k0t_ref[part, :], preferred_element_type=jnp.float32) * scale
                high = jnp.maximum(
                    jnp.max(own, axis=-1, keepdims=True), jnp.max(first, axis=-1, keepdims=True)
                )
                own = jnp.exp(own - high)
                first = jnp.exp(first - high)
                totals = jnp.sum(own, axis=-1, keepdims=True) + jnp.sum(first, axis=-1, keepdims=True)
                summed = lax.dot_general(
                    own.astype(jnp.bfloat16), vt_ref[f, part, :], contract, preferred_element_type=jnp.float32
                ) + lax.dot_general(
                    first.astype(jnp.bfloat16), v0t_ref[part, :], contract, preferred_element_type=jnp.float32
                )
                attended = (summed / totals).astype(jnp.bfloat16)
                acc = acc + jnp.dot(attended, w_ref[part, :], preferred_element_type=jnp.float32)
            made[pl.ds(base, chunks), f] = acc.reshape(chunks, run, width).astype(made.dtype)

        @pl.when(t == 0)
        def _():
            pl.semaphore_wait(barrier, n_dev - 1)

        for i in range(chunks):
            gf = i % n_frame
            gp = (base + i) // n_frame

            @pl.when((gf == fi) & (gp == pi))
            def _():
                got[me] = made[base + i]

            @pl.when((gf != fi) | (gp != pi))
            def _():
                pltpu.make_async_remote_copy(
                    src_ref=made.at[base + i],
                    dst_ref=got.at[me],
                    send_sem=send_sem,
                    recv_sem=recv_sem,
                    device_id={"frame": gf, "pos": gp},
                    device_id_type=MESH,
                ).start()

        @pl.when(t == n_tiles - 1)
        def _():
            others = pltpu.make_async_copy(got.at[pl.ds(0, n_dev - 1)], got.at[pl.ds(1, n_dev - 1)], recv_sem)
            others.wait()
            sent = pltpu.make_async_copy(got.at[pl.ds(0, n_dev - 1)], got.at[pl.ds(1, n_dev - 1)], send_sem)
            sent.wait()
            o_ref[...] = got[...]

    fixed = lambda t: (0, 0)
    dtype = got_in.dtype
    return pl.pallas_call(
        kernel,
        out_shape=jax.ShapeDtypeStruct((n_dev, frames, run, width), dtype),
        grid=(n_tiles,),
        in_specs=[
            pl.BlockSpec(memory_space=pltpu.VMEM),
            pl.BlockSpec(memory_space=pltpu.VMEM),
            pl.BlockSpec((1, width), fixed),
            pl.BlockSpec((width, width), fixed),
            pl.BlockSpec((width, width), fixed),
            pl.BlockSpec((width, width), fixed),
            pl.BlockSpec((width, width), fixed),
        ],
        out_specs=pl.BlockSpec(memory_space=pltpu.VMEM),
        scratch_shapes=[
            pltpu.VMEM((frames, places, width), dtype),
            pltpu.VMEM((frames, width, places), dtype),
            pltpu.VMEM((frames, width, places), dtype),
            pltpu.VMEM((width, places), dtype),
            pltpu.VMEM((width, places), dtype),
            pltpu.VMEM((n_dev, frames, run, width), dtype),
            pltpu.VMEM((n_dev, frames, run, width), dtype),
            pltpu.SemaphoreType.DMA,
            pltpu.SemaphoreType.DMA,
        ],
        compiler_params=pltpu.CompilerParams(collective_id=cid, has_side_effects=True),
    )(got_in, zero, gain.reshape(1, width), wq, wk.T, wv.T, out_w)


def temporal_attend(x, gain, wq, wk, wv, out_w, n_frame, cid, per_step=2):
    run, every, width = x.shape
    depth = width // HEADS
    scale = depth ** (-0.5)
    frames = every // n_frame

    def kernel(x_ref, g_ref, wq_ref, wk_ref, wv_ref, w_ref, o_ref, made, got, send_sem, recv_sem):
        step = pl.program_id(0)
        fi = lax.axis_index("frame")
        barrier = pltpu.get_barrier_semaphore()

        @pl.when(step == 0)
        def _():
            for k in range(1, n_frame):
                pl.semaphore_signal(barrier, inc=1, device_id={"frame": (fi + k) % n_frame}, device_id_type=MESH)

        for s in range(per_step):
            wide = x_ref[s].astype(jnp.float32)
            factor = lax.rsqrt(jnp.mean(wide * wide, axis=-1, keepdims=True) + 1e-06)
            normed_two = (wide * factor * g_ref[...]).astype(jnp.bfloat16)
            q = jnp.dot(normed_two, wq_ref[...], preferred_element_type=jnp.float32).astype(jnp.bfloat16)
            k = jnp.dot(normed_two, wk_ref[...], preferred_element_type=jnp.float32).astype(jnp.bfloat16)
            v = jnp.dot(normed_two, wv_ref[...], preferred_element_type=jnp.float32).astype(jnp.bfloat16)
            acc = wide
            for h in range(HEADS):
                part = slice(h * depth, (h + 1) * depth)
                contract = (((1,), (1,)), ((), ()))
                scores = lax.dot_general(q[:, part], k[:, part], contract, preferred_element_type=jnp.float32) * scale
                weights = jnp.exp(scores - jnp.max(scores, axis=-1, keepdims=True))
                totals = jnp.sum(weights, axis=-1, keepdims=True)
                summed = jnp.dot(weights.astype(jnp.bfloat16), v[:, part], preferred_element_type=jnp.float32)
                attended = (summed / totals).astype(jnp.bfloat16)
                acc = acc + jnp.dot(attended, w_ref[part, :], preferred_element_type=jnp.float32)
            made[step * per_step + s] = acc.astype(made.dtype)

        @pl.when(step == 0)
        def _():
            pl.semaphore_wait(barrier, n_frame - 1)

        these = pl.ds(step * per_step, per_step)
        for g in range(n_frame):
            @pl.when(g == fi)
            def _():
                got[fi, these] = made[these, pl.ds(g * frames, frames)]

            @pl.when(g != fi)
            def _():
                pltpu.make_async_remote_copy(
                    src_ref=made.at[these, pl.ds(g * frames, frames)],
                    dst_ref=got.at[fi, these],
                    send_sem=send_sem,
                    recv_sem=recv_sem,
                    device_id={"frame": g},
                    device_id_type=MESH,
                ).start()

        @pl.when(step == run // per_step - 1)
        def _():
            others = pltpu.make_async_copy(got.at[pl.ds(0, n_frame - 1)], got.at[pl.ds(1, n_frame - 1)], recv_sem)
            others.wait()
            sent = pltpu.make_async_copy(got.at[pl.ds(0, n_frame - 1)], got.at[pl.ds(1, n_frame - 1)], send_sem)
            sent.wait()
            o_ref[...] = got[...]

    fixed = lambda p: (0, 0)
    return pl.pallas_call(
        kernel,
        out_shape=jax.ShapeDtypeStruct((n_frame, run, frames, width), x.dtype),
        grid=(run // per_step,),
        in_specs=[
            pl.BlockSpec((per_step, every, width), lambda p: (p, 0, 0)),
            pl.BlockSpec((1, width), fixed),
            pl.BlockSpec((width, width), fixed),
            pl.BlockSpec((width, width), fixed),
            pl.BlockSpec((width, width), fixed),
            pl.BlockSpec((width, width), fixed),
        ],
        out_specs=pl.BlockSpec(memory_space=pltpu.VMEM),
        scratch_shapes=[
            pltpu.VMEM((run, every, width), x.dtype),
            pltpu.VMEM((n_frame, run, frames, width), x.dtype),
            pltpu.SemaphoreType.DMA,
            pltpu.SemaphoreType.DMA,
        ],
        compiler_params=pltpu.CompilerParams(collective_id=cid, has_side_effects=True),
    )(x, gain.reshape(1, width), wq, wk, wv, out_w)


def transposed(values, weight):
    result = jnp.einsum("...rc,cd->...dr", values, weight, preferred_element_type=jnp.float32)
    return result.astype(jnp.bfloat16)


def normed(values, gain):
    wide = values.astype(jnp.float32)
    factor = lax.rsqrt(jnp.mean(wide * wide, axis=-1, keepdims=True) + 1e-06)
    return (wide * factor * gain).astype(jnp.bfloat16)


def project(values, weight):
    flat = values.reshape(-1, values.shape[-1])
    result = jnp.dot(flat, weight, preferred_element_type=jnp.float32).astype(jnp.bfloat16)
    return result.reshape(values.shape[:-1] + (weight.shape[1],))


def heads_of(values):
    return values.reshape(values.shape[:-1] + (HEADS, values.shape[-1] // HEADS))


def softmax_attend(query, keys, vals, score_form, value_form, total_form):
    scale = query.shape[-1] ** (-0.5)
    scores = jnp.einsum(score_form, query, keys, preferred_element_type=jnp.float32) * scale
    weights = jnp.exp(scores - jnp.max(scores, axis=-1, keepdims=True))
    totals = jnp.sum(weights, axis=-1)
    summed = jnp.einsum(
        value_form, weights.astype(jnp.bfloat16), vals, preferred_element_type=jnp.float32
    )
    return summed / jnp.einsum(total_form, totals)[..., None]


def shards(
    latents,
    gain_one,
    query_one,
    key_one,
    value_one,
    out_one,
    gain_two,
    query_two,
    key_two,
    value_two,
    out_two,
):
    frames, places, width = latents.shape
    n_pos = lax.axis_size("pos")
    n_frame = lax.axis_size("frame")
    per = frames // n_pos
    got, zero = spatial_exchange(latents.reshape(n_pos, per, places, width), n_pos, n_frame, 1)
    got = spatial_attend(
        got, zero, gain_one, query_one, key_one, value_one, out_one,
        min(256, n_pos * places), n_frame, n_pos, 2,
    )
    all_places = n_pos * places
    run = all_places // (n_pos * n_frame)
    mid_t = got.reshape(n_frame * n_pos * per, run, width).transpose(1, 0, 2)
    got = temporal_attend(mid_t, gain_two, query_two, key_two, value_two, out_two, n_frame, 3)
    return got.transpose(2, 0, 1, 3).reshape(frames, places, width)


def solution(mesh):
    return jax.shard_map(
        shards,
        mesh=mesh,
        in_specs=(P("frame", "pos", None), P(), P(), P(), P(), P(), P(), P(), P(), P(), P()),
        out_specs=P("frame", "pos", None),
        check_vma=False,
    )
```

```python
import jax
import jax.numpy as jnp
from jax import lax
from jax.experimental import pallas as pl
from jax.experimental.pallas import tpu as pltpu
from jax.sharding import PartitionSpec as P

HEADS = 4

MESH = pl.DeviceIdType.MESH


def exchange(x, names, sizes, cid):
    n = x.shape[0]

    def where(peer):
        if len(names) == 1:
            return {names[0]: peer}
        return {names[0]: peer // sizes[1], names[1]: peer % sizes[1]}

    def kernel(x_ref, o_ref, send_sem, recv_sem):
        me = lax.axis_index(names[0])
        if len(names) == 2:
            me = me * sizes[1] + lax.axis_index(names[1])
        barrier = pltpu.get_barrier_semaphore()
        for k in range(1, n):
            pl.semaphore_signal(barrier, inc=1, device_id=where((me + k) % n), device_id_type=MESH)
        pl.semaphore_wait(barrier, n - 1)
        copies = []
        for k in range(1, n):
            peer = (me + k) % n
            copy = pltpu.make_async_remote_copy(
                src_ref=x_ref.at[peer],
                dst_ref=o_ref.at[me],
                send_sem=send_sem.at[k],
                recv_sem=recv_sem.at[k],
                device_id=where(peer),
                device_id_type=MESH,
            )
            copy.start()
            copies.append(copy)
        o_ref[me] = x_ref[me]
        for copy in copies:
            copy.wait()

    return pl.pallas_call(
        kernel,
        out_shape=jax.ShapeDtypeStruct(x.shape, x.dtype),
        in_specs=[pl.BlockSpec(memory_space=pltpu.VMEM)],
        out_specs=pl.BlockSpec(memory_space=pltpu.VMEM),
        scratch_shapes=[pltpu.SemaphoreType.DMA((n,)), pltpu.SemaphoreType.DMA((n,))],
        compiler_params=pltpu.CompilerParams(collective_id=cid, has_side_effects=True),
    )(x)


def spatial_exchange(x, n_pos, n_frame, cid):
    _, per, places, width = x.shape

    def kernel(x_ref, o_ref, z_ref, send_sem, recv_sem, fsend_sem, frecv_sem, zsend_sem, zrecv_sem, local_sem):
        fi = lax.axis_index("frame")
        pi = lax.axis_index("pos")
        barrier = pltpu.get_barrier_semaphore()
        for k in range(1, n_pos):
            pl.semaphore_signal(barrier, inc=1, device_id={"pos": (pi + k) % n_pos}, device_id_type=MESH)
        for g in range(1, n_frame):
            pl.semaphore_signal(barrier, inc=1, device_id={"frame": (fi + g) % n_frame}, device_id_type=MESH)
        pl.semaphore_wait(barrier, n_pos - 1 + n_frame - 1)
        def spread(g):
            return pltpu.make_async_remote_copy(
                src_ref=x_ref.at[0, 0],
                dst_ref=z_ref.at[pi],
                send_sem=fsend_sem.at[g],
                recv_sem=frecv_sem,
                device_id={"frame": g},
                device_id_type=MESH,
            )

        @pl.when(fi == 0)
        def _():
            for g in range(1, n_frame):
                spread(g).start()

        copies = []
        for k in range(1, n_pos):
            peer = (pi + k) % n_pos
            copy = pltpu.make_async_remote_copy(
                src_ref=x_ref.at[peer],
                dst_ref=o_ref.at[pi],
                send_sem=send_sem.at[k],
                recv_sem=recv_sem.at[k],
                device_id={"pos": peer},
                device_id_type=MESH,
            )
            copy.start()
            copies.append(copy)

        @pl.when(fi == 0)
        def _():
            local = pltpu.make_async_copy(x_ref.at[0, 0], z_ref.at[pi], local_sem)
            local.start()
            local.wait()

        @pl.when(fi != 0)
        def _():
            spread(1).wait_recv()

        for k in range(1, n_pos):
            peer = (pi + k) % n_pos
            copy = pltpu.make_async_remote_copy(
                src_ref=z_ref.at[pi],
                dst_ref=z_ref.at[pi],
                send_sem=zsend_sem.at[k],
                recv_sem=zrecv_sem.at[k],
                device_id={"pos": peer},
                device_id_type=MESH,
            )
            copy.start()
            copies.append(copy)

        @pl.when(fi == 0)
        def _():
            for g in range(1, n_frame):
                spread(g).wait_send()

        for copy in copies:
            copy.wait()
        o_ref[pi] = x_ref[pi]

    return pl.pallas_call(
        kernel,
        out_shape=(
            jax.ShapeDtypeStruct(x.shape, x.dtype),
            jax.ShapeDtypeStruct((n_pos, places, width), x.dtype),
        ),
        in_specs=[pl.BlockSpec(memory_space=pltpu.VMEM)],
        out_specs=(pl.BlockSpec(memory_space=pltpu.VMEM), pl.BlockSpec(memory_space=pltpu.VMEM)),
        scratch_shapes=[
            pltpu.SemaphoreType.DMA((n_pos,)),
            pltpu.SemaphoreType.DMA((n_pos,)),
            pltpu.SemaphoreType.DMA((n_frame,)),
            pltpu.SemaphoreType.DMA,
            pltpu.SemaphoreType.DMA((n_pos,)),
            pltpu.SemaphoreType.DMA((n_pos,)),
            pltpu.SemaphoreType.DMA,
        ],
        compiler_params=pltpu.CompilerParams(collective_id=cid, has_side_effects=True),
    )(x)


def spatial_attend(got_in, zero, gain, wq, wk, wv, out_w, rows, n_frame, n_pos, cid):
    _, frames, slab, width = got_in.shape
    places = n_pos * slab
    depth = width // HEADS
    scale = depth ** (-0.5)
    n_dev = n_frame * n_pos
    run = places // n_dev
    chunks = rows // run
    n_tiles = places // rows
    per_tile = rows // slab

    def kernel(x_ref, z_ref, g_ref, wq_ref, wkt_ref, wvt_ref, w_ref, o_ref,
               q_ref, kt_ref, vt_ref, k0t_ref, v0t_ref, made, got, send_sem, recv_sem):
        t = pl.program_id(0)
        fi = lax.axis_index("frame")
        pi = lax.axis_index("pos")
        me = fi * n_pos + pi
        barrier = pltpu.get_barrier_semaphore()
        contract = (((1,), (1,)), ((), ()))

        def normed_rows(values):
            wide = values.reshape(places, width).astype(jnp.float32)
            factor = lax.rsqrt(jnp.mean(wide * wide, axis=-1, keepdims=True) + 1e-06)
            return (wide * factor * g_ref[...]).astype(jnp.bfloat16)

        def channels_first(weight_t, values):
            return lax.dot_general(weight_t, values, contract, preferred_element_type=jnp.float32).astype(jnp.bfloat16)

        @pl.when(t == 0)
        def _():
            for k in range(1, n_dev):
                peer = (me + k) % n_dev
                pl.semaphore_signal(
                    barrier, inc=1, device_id={"frame": peer // n_pos, "pos": peer % n_pos}, device_id_type=MESH
                )
            wkt = wkt_ref[...].T
            wvt = wvt_ref[...].T
            for f in range(frames):
                normed_one = normed_rows(x_ref[:, f])
                q_ref[f] = jnp.dot(normed_one, wq_ref[...], preferred_element_type=jnp.float32).astype(jnp.bfloat16)
                kt_ref[f] = channels_first(wkt, normed_one)
                vt_ref[f] = channels_first(wvt, normed_one)
            normed_zero = normed_rows(z_ref[...])
            k0t_ref[...] = channels_first(wkt, normed_zero)
            v0t_ref[...] = channels_first(wvt, normed_zero)

        tt = (t + fi + pi) % n_tiles
        base = tt * chunks
        these = pl.ds(pl.multiple_of(tt * rows, rows), rows)
        for f in range(frames):
            acc = x_ref[pl.ds(tt * per_tile, per_tile), f].reshape(rows, width).astype(jnp.float32)
            for h in range(HEADS):
                part = pl.ds(h * depth, depth)
                qh = q_ref[f, these, part]
                own = jnp.dot(qh, kt_ref[f, part, :], preferred_element_type=jnp.float32) * scale
                first = jnp.dot(qh, k0t_ref[part, :], preferred_element_type=jnp.float32) * scale
                high = jnp.maximum(
                    jnp.max(own, axis=-1, keepdims=True), jnp.max(first, axis=-1, keepdims=True)
                )
                own = jnp.exp(own - high)
                first = jnp.exp(first - high)
                totals = jnp.sum(own, axis=-1, keepdims=True) + jnp.sum(first, axis=-1, keepdims=True)
                summed = lax.dot_general(
                    own.astype(jnp.bfloat16), vt_ref[f, part, :], contract, preferred_element_type=jnp.float32
                ) + lax.dot_general(
                    first.astype(jnp.bfloat16), v0t_ref[part, :], contract, preferred_element_type=jnp.float32
                )
                attended = (summed / totals).astype(jnp.bfloat16)
                acc = acc + jnp.dot(attended, w_ref[part, :], preferred_element_type=jnp.float32)
            made[pl.ds(base, chunks), f] = acc.reshape(chunks, run, width).astype(made.dtype)

        @pl.when(t == 0)
        def _():
            pl.semaphore_wait(barrier, n_dev - 1)

        for i in range(chunks):
            gf = i % n_frame
            gp = (base + i) // n_frame

            @pl.when((gf == fi) & (gp == pi))
            def _():
                got[me] = made[base + i]

            @pl.when((gf != fi) | (gp != pi))
            def _():
                pltpu.make_async_remote_copy(
                    src_ref=made.at[base + i],
                    dst_ref=got.at[me],
                    send_sem=send_sem,
                    recv_sem=recv_sem,
                    device_id={"frame": gf, "pos": gp},
                    device_id_type=MESH,
                ).start()

        @pl.when(t == n_tiles - 1)
        def _():
            others = pltpu.make_async_copy(got.at[pl.ds(0, n_dev - 1)], got.at[pl.ds(1, n_dev - 1)], recv_sem)
            others.wait()
            sent = pltpu.make_async_copy(got.at[pl.ds(0, n_dev - 1)], got.at[pl.ds(1, n_dev - 1)], send_sem)
            sent.wait()
            o_ref[...] = got[...]

    fixed = lambda t: (0, 0)
    dtype = got_in.dtype
    return pl.pallas_call(
        kernel,
        out_shape=jax.ShapeDtypeStruct((n_dev, frames, run, width), dtype),
        grid=(n_tiles,),
        in_specs=[
            pl.BlockSpec(memory_space=pltpu.VMEM),
            pl.BlockSpec(memory_space=pltpu.VMEM),
            pl.BlockSpec((1, width), fixed),
            pl.BlockSpec((width, width), fixed),
            pl.BlockSpec((width, width), fixed),
            pl.BlockSpec((width, width), fixed),
            pl.BlockSpec((width, width), fixed),
        ],
        out_specs=pl.BlockSpec(memory_space=pltpu.VMEM),
        scratch_shapes=[
            pltpu.VMEM((frames, places, width), dtype),
            pltpu.VMEM((frames, width, places), dtype),
            pltpu.VMEM((frames, width, places), dtype),
            pltpu.VMEM((width, places), dtype),
            pltpu.VMEM((width, places), dtype),
            pltpu.VMEM((n_dev, frames, run, width), dtype),
            pltpu.VMEM((n_dev, frames, run, width), dtype),
            pltpu.SemaphoreType.DMA,
            pltpu.SemaphoreType.DMA,
        ],
        compiler_params=pltpu.CompilerParams(collective_id=cid, has_side_effects=True),
    )(got_in, zero, gain.reshape(1, width), wq, wk, wv, out_w)


def temporal_attend(x, gain, wq, wk, wv, out_w, n_frame, cid, per_step=2):
    run, every, width = x.shape
    depth = width // HEADS
    scale = depth ** (-0.5)
    frames = every // n_frame

    def kernel(x_ref, g_ref, wq_ref, wk_ref, wv_ref, w_ref, o_ref, made, got, send_sem, recv_sem):
        step = pl.program_id(0)
        fi = lax.axis_index("frame")
        barrier = pltpu.get_barrier_semaphore()

        @pl.when(step == 0)
        def _():
            for k in range(1, n_frame):
                pl.semaphore_signal(barrier, inc=1, device_id={"frame": (fi + k) % n_frame}, device_id_type=MESH)

        for s in range(per_step):
            wide = x_ref[s].astype(jnp.float32)
            factor = lax.rsqrt(jnp.mean(wide * wide, axis=-1, keepdims=True) + 1e-06)
            normed_two = (wide * factor * g_ref[...]).astype(jnp.bfloat16)
            q = jnp.dot(normed_two, wq_ref[...], preferred_element_type=jnp.float32).astype(jnp.bfloat16)
            k = jnp.dot(normed_two, wk_ref[...], preferred_element_type=jnp.float32).astype(jnp.bfloat16)
            v = jnp.dot(normed_two, wv_ref[...], preferred_element_type=jnp.float32).astype(jnp.bfloat16)
            acc = wide
            for h in range(HEADS):
                part = slice(h * depth, (h + 1) * depth)
                contract = (((1,), (1,)), ((), ()))
                scores = lax.dot_general(q[:, part], k[:, part], contract, preferred_element_type=jnp.float32) * scale
                weights = jnp.exp(scores - jnp.max(scores, axis=-1, keepdims=True))
                totals = jnp.sum(weights, axis=-1, keepdims=True)
                summed = jnp.dot(weights.astype(jnp.bfloat16), v[:, part], preferred_element_type=jnp.float32)
                attended = (summed / totals).astype(jnp.bfloat16)
                acc = acc + jnp.dot(attended, w_ref[part, :], preferred_element_type=jnp.float32)
            made[step * per_step + s] = acc.astype(made.dtype)

        @pl.when(step == 0)
        def _():
            pl.semaphore_wait(barrier, n_frame - 1)

        these = pl.ds(step * per_step, per_step)
        for g in range(n_frame):
            @pl.when(g == fi)
            def _():
                got[fi, these] = made[these, pl.ds(g * frames, frames)]

            @pl.when(g != fi)
            def _():
                pltpu.make_async_remote_copy(
                    src_ref=made.at[these, pl.ds(g * frames, frames)],
                    dst_ref=got.at[fi, these],
                    send_sem=send_sem,
                    recv_sem=recv_sem,
                    device_id={"frame": g},
                    device_id_type=MESH,
                ).start()

        @pl.when(step == run // per_step - 1)
        def _():
            others = pltpu.make_async_copy(got.at[pl.ds(0, n_frame - 1)], got.at[pl.ds(1, n_frame - 1)], recv_sem)
            others.wait()
            sent = pltpu.make_async_copy(got.at[pl.ds(0, n_frame - 1)], got.at[pl.ds(1, n_frame - 1)], send_sem)
            sent.wait()
            o_ref[...] = got[...]

    fixed = lambda p: (0, 0)
    return pl.pallas_call(
        kernel,
        out_shape=jax.ShapeDtypeStruct((n_frame, run, frames, width), x.dtype),
        grid=(run // per_step,),
        in_specs=[
            pl.BlockSpec((per_step, every, width), lambda p: (p, 0, 0)),
            pl.BlockSpec((1, width), fixed),
            pl.BlockSpec((width, width), fixed),
            pl.BlockSpec((width, width), fixed),
            pl.BlockSpec((width, width), fixed),
            pl.BlockSpec((width, width), fixed),
        ],
        out_specs=pl.BlockSpec(memory_space=pltpu.VMEM),
        scratch_shapes=[
            pltpu.VMEM((run, every, width), x.dtype),
            pltpu.VMEM((n_frame, run, frames, width), x.dtype),
            pltpu.SemaphoreType.DMA,
            pltpu.SemaphoreType.DMA,
        ],
        compiler_params=pltpu.CompilerParams(collective_id=cid, has_side_effects=True),
    )(x, gain.reshape(1, width), wq, wk, wv, out_w)


def transposed(values, weight):
    result = jnp.einsum("...rc,cd->...dr", values, weight, preferred_element_type=jnp.float32)
    return result.astype(jnp.bfloat16)


def normed(values, gain):
    wide = values.astype(jnp.float32)
    factor = lax.rsqrt(jnp.mean(wide * wide, axis=-1, keepdims=True) + 1e-06)
    return (wide * factor * gain).astype(jnp.bfloat16)


def project(values, weight):
    flat = values.reshape(-1, values.shape[-1])
    result = jnp.dot(flat, weight, preferred_element_type=jnp.float32).astype(jnp.bfloat16)
    return result.reshape(values.shape[:-1] + (weight.shape[1],))


def heads_of(values):
    return values.reshape(values.shape[:-1] + (HEADS, values.shape[-1] // HEADS))


def softmax_attend(query, keys, vals, score_form, value_form, total_form):
    scale = query.shape[-1] ** (-0.5)
    scores = jnp.einsum(score_form, query, keys, preferred_element_type=jnp.float32) * scale
    weights = jnp.exp(scores - jnp.max(scores, axis=-1, keepdims=True))
    totals = jnp.sum(weights, axis=-1)
    summed = jnp.einsum(
        value_form, weights.astype(jnp.bfloat16), vals, preferred_element_type=jnp.float32
    )
    return summed / jnp.einsum(total_form, totals)[..., None]


def shards(
    latents,
    gain_one,
    query_one,
    key_one,
    value_one,
    out_one,
    gain_two,
    query_two,
    key_two,
    value_two,
    out_two,
):
    frames, places, width = latents.shape
    n_pos = lax.axis_size("pos")
    n_frame = lax.axis_size("frame")
    per = frames // n_pos
    got, zero = spatial_exchange(latents.reshape(n_pos, per, places, width), n_pos, n_frame, 1)
    got = spatial_attend(
        got, zero, gain_one, query_one, key_one, value_one, out_one,
        min(256, n_pos * places), n_frame, n_pos, 2,
    )
    all_places = n_pos * places
    run = all_places // (n_pos * n_frame)
    mid_t = got.reshape(n_frame * n_pos * per, run, width).transpose(1, 0, 2)
    got = temporal_attend(mid_t, gain_two, query_two, key_two, value_two, out_two, n_frame, 3)
    return got.transpose(2, 0, 1, 3).reshape(frames, places, width)


def solution(mesh):
    return jax.shard_map(
        shards,
        mesh=mesh,
        in_specs=(P("frame", "pos", None), P(), P(), P(), P(), P(), P(), P(), P(), P(), P()),
        out_specs=P("frame", "pos", None),
        check_vma=False,
    )
```

```python
import jax
import jax.numpy as jnp
from jax import lax
from jax.experimental import pallas as pl
from jax.experimental.pallas import tpu as pltpu
from jax.sharding import PartitionSpec as P

HEADS = 4

MESH = pl.DeviceIdType.MESH


def exchange(x, names, sizes, cid):
    n = x.shape[0]

    def where(peer):
        if len(names) == 1:
            return {names[0]: peer}
        return {names[0]: peer // sizes[1], names[1]: peer % sizes[1]}

    def kernel(x_ref, o_ref, send_sem, recv_sem):
        me = lax.axis_index(names[0])
        if len(names) == 2:
            me = me * sizes[1] + lax.axis_index(names[1])
        barrier = pltpu.get_barrier_semaphore()
        for k in range(1, n):
            pl.semaphore_signal(barrier, inc=1, device_id=where((me + k) % n), device_id_type=MESH)
        pl.semaphore_wait(barrier, n - 1)
        copies = []
        for k in range(1, n):
            peer = (me + k) % n
            copy = pltpu.make_async_remote_copy(
                src_ref=x_ref.at[peer],
                dst_ref=o_ref.at[me],
                send_sem=send_sem.at[k],
                recv_sem=recv_sem.at[k],
                device_id=where(peer),
                device_id_type=MESH,
            )
            copy.start()
            copies.append(copy)
        o_ref[me] = x_ref[me]
        for copy in copies:
            copy.wait()

    return pl.pallas_call(
        kernel,
        out_shape=jax.ShapeDtypeStruct(x.shape, x.dtype),
        in_specs=[pl.BlockSpec(memory_space=pltpu.VMEM)],
        out_specs=pl.BlockSpec(memory_space=pltpu.VMEM),
        scratch_shapes=[pltpu.SemaphoreType.DMA((n,)), pltpu.SemaphoreType.DMA((n,))],
        compiler_params=pltpu.CompilerParams(collective_id=cid, has_side_effects=True),
    )(x)


def spatial_exchange(x, n_pos, n_frame, cid):
    _, per, places, width = x.shape

    def kernel(x_ref, o_ref, z_ref, send_sem, recv_sem, fsend_sem, frecv_sem, zsend_sem, zrecv_sem, local_sem):
        fi = lax.axis_index("frame")
        pi = lax.axis_index("pos")
        barrier = pltpu.get_barrier_semaphore()
        for k in range(1, n_pos):
            pl.semaphore_signal(barrier, inc=1, device_id={"pos": (pi + k) % n_pos}, device_id_type=MESH)
        for g in range(1, n_frame):
            pl.semaphore_signal(barrier, inc=1, device_id={"frame": (fi + g) % n_frame}, device_id_type=MESH)
        pl.semaphore_wait(barrier, n_pos - 1 + n_frame - 1)
        def spread(g):
            return pltpu.make_async_remote_copy(
                src_ref=x_ref.at[0, 0],
                dst_ref=z_ref.at[pi],
                send_sem=fsend_sem.at[g],
                recv_sem=frecv_sem,
                device_id={"frame": g},
                device_id_type=MESH,
            )

        @pl.when(fi == 0)
        def _():
            for g in range(1, n_frame):
                spread(g).start()

        copies = []
        for k in range(1, n_pos):
            peer = (pi + k) % n_pos
            copy = pltpu.make_async_remote_copy(
                src_ref=x_ref.at[peer],
                dst_ref=o_ref.at[pi],
                send_sem=send_sem.at[k],
                recv_sem=recv_sem.at[k],
                device_id={"pos": peer},
                device_id_type=MESH,
            )
            copy.start()
            copies.append(copy)

        @pl.when(fi == 0)
        def _():
            local = pltpu.make_async_copy(x_ref.at[0, 0], z_ref.at[pi], local_sem)
            local.start()
            local.wait()

        @pl.when(fi != 0)
        def _():
            spread(1).wait_recv()

        for k in range(1, n_pos):
            peer = (pi + k) % n_pos
            copy = pltpu.make_async_remote_copy(
                src_ref=z_ref.at[pi],
                dst_ref=z_ref.at[pi],
                send_sem=zsend_sem.at[k],
                recv_sem=zrecv_sem.at[k],
                device_id={"pos": peer},
                device_id_type=MESH,
            )
            copy.start()
            copies.append(copy)

        @pl.when(fi == 0)
        def _():
            for g in range(1, n_frame):
                spread(g).wait_send()

        for copy in copies:
            copy.wait()
        o_ref[pi] = x_ref[pi]

    return pl.pallas_call(
        kernel,
        out_shape=(
            jax.ShapeDtypeStruct(x.shape, x.dtype),
            jax.ShapeDtypeStruct((n_pos, places, width), x.dtype),
        ),
        in_specs=[pl.BlockSpec(memory_space=pltpu.VMEM)],
        out_specs=(pl.BlockSpec(memory_space=pltpu.VMEM), pl.BlockSpec(memory_space=pltpu.VMEM)),
        scratch_shapes=[
            pltpu.SemaphoreType.DMA((n_pos,)),
            pltpu.SemaphoreType.DMA((n_pos,)),
            pltpu.SemaphoreType.DMA((n_frame,)),
            pltpu.SemaphoreType.DMA,
            pltpu.SemaphoreType.DMA((n_pos,)),
            pltpu.SemaphoreType.DMA((n_pos,)),
            pltpu.SemaphoreType.DMA,
        ],
        compiler_params=pltpu.CompilerParams(collective_id=cid, has_side_effects=True),
    )(x)


def spatial_attend(got_in, zero, gain, wq, wk, wv, out_w, rows, n_frame, n_pos, cid):
    _, frames, slab, width = got_in.shape
    places = n_pos * slab
    depth = width // HEADS
    scale = depth ** (-0.5)
    n_dev = n_frame * n_pos
    run = places // n_dev
    chunks = rows // run
    n_tiles = places // rows
    per_tile = rows // slab

    def kernel(x_ref, z_ref, g_ref, wq_ref, wkt_ref, wvt_ref, w_ref, o_ref,
               q_ref, kt_ref, vt_ref, k0t_ref, v0t_ref, made, got, send_sem, recv_sem):
        t = pl.program_id(0)
        fi = lax.axis_index("frame")
        pi = lax.axis_index("pos")
        me = fi * n_pos + pi
        barrier = pltpu.get_barrier_semaphore()
        contract = (((1,), (1,)), ((), ()))

        def normed_rows(values):
            wide = values.reshape(places, width).astype(jnp.float32)
            factor = lax.rsqrt(jnp.mean(wide * wide, axis=-1, keepdims=True) + 1e-06)
            return (wide * factor * g_ref[...]).astype(jnp.bfloat16)

        def channels_first(weight_t, values):
            return lax.dot_general(weight_t, values, contract, preferred_element_type=jnp.float32).astype(jnp.bfloat16)

        @pl.when(t == 0)
        def _():
            for k in range(1, n_dev):
                peer = (me + k) % n_dev
                pl.semaphore_signal(
                    barrier, inc=1, device_id={"frame": peer // n_pos, "pos": peer % n_pos}, device_id_type=MESH
                )
            wkt = wkt_ref[...].T
            wvt = wvt_ref[...].T
            for f in range(frames):
                normed_one = normed_rows(x_ref[:, f])
                q_ref[f] = jnp.dot(normed_one, wq_ref[...], preferred_element_type=jnp.float32).astype(jnp.bfloat16)
                kt_ref[f] = channels_first(wkt, normed_one)
                vt_ref[f] = channels_first(wvt, normed_one)
            normed_zero = normed_rows(z_ref[...])
            k0t_ref[...] = channels_first(wkt, normed_zero)
            v0t_ref[...] = channels_first(wvt, normed_zero)

        tt = (t + fi + pi) % n_tiles
        base = tt * chunks
        these = pl.ds(pl.multiple_of(tt * rows, rows), rows)
        for f in range(frames):
            acc = x_ref[pl.ds(tt * per_tile, per_tile), f].reshape(rows, width).astype(jnp.float32)
            for h in range(HEADS):
                part = pl.ds(h * depth, depth)
                qh = q_ref[f, these, part]
                own = jnp.dot(qh, kt_ref[f, part, :], preferred_element_type=jnp.float32) * scale
                first = jnp.dot(qh, k0t_ref[part, :], preferred_element_type=jnp.float32) * scale
                high = jnp.maximum(
                    jnp.max(own, axis=-1, keepdims=True), jnp.max(first, axis=-1, keepdims=True)
                )
                own = jnp.exp(own - high)
                first = jnp.exp(first - high)
                totals = jnp.sum(own, axis=-1, keepdims=True) + jnp.sum(first, axis=-1, keepdims=True)
                summed = lax.dot_general(
                    own.astype(jnp.bfloat16), vt_ref[f, part, :], contract, preferred_element_type=jnp.float32
                ) + lax.dot_general(
                    first.astype(jnp.bfloat16), v0t_ref[part, :], contract, preferred_element_type=jnp.float32
                )
                attended = (summed / totals).astype(jnp.bfloat16)
                acc = acc + jnp.dot(attended, w_ref[part, :], preferred_element_type=jnp.float32)
            made[pl.ds(base, chunks), f] = acc.reshape(chunks, run, width).astype(made.dtype)

        @pl.when(t == 0)
        def _():
            pl.semaphore_wait(barrier, n_dev - 1)

        for i in range(chunks):
            gf = i % n_frame
            gp = (base + i) // n_frame

            @pl.when((gf == fi) & (gp == pi))
            def _():
                got[me] = made[base + i]

            @pl.when((gf != fi) | (gp != pi))
            def _():
                pltpu.make_async_remote_copy(
                    src_ref=made.at[base + i],
                    dst_ref=got.at[me],
                    send_sem=send_sem,
                    recv_sem=recv_sem,
                    device_id={"frame": gf, "pos": gp},
                    device_id_type=MESH,
                ).start()

        @pl.when(t == n_tiles - 1)
        def _():
            others = pltpu.make_async_copy(got.at[pl.ds(0, n_dev - 1)], got.at[pl.ds(1, n_dev - 1)], recv_sem)
            others.wait()
            sent = pltpu.make_async_copy(got.at[pl.ds(0, n_dev - 1)], got.at[pl.ds(1, n_dev - 1)], send_sem)
            sent.wait()
            o_ref[...] = got[...]

    fixed = lambda t: (0, 0)
    dtype = got_in.dtype
    return pl.pallas_call(
        kernel,
        out_shape=jax.ShapeDtypeStruct((n_dev, frames, run, width), dtype),
        grid=(n_tiles,),
        in_specs=[
            pl.BlockSpec(memory_space=pltpu.VMEM),
            pl.BlockSpec(memory_space=pltpu.VMEM),
            pl.BlockSpec((1, width), fixed),
            pl.BlockSpec((width, width), fixed),
            pl.BlockSpec((width, width), fixed),
            pl.BlockSpec((width, width), fixed),
            pl.BlockSpec((width, width), fixed),
        ],
        out_specs=pl.BlockSpec(memory_space=pltpu.VMEM),
        scratch_shapes=[
            pltpu.VMEM((frames, places, width), dtype),
            pltpu.VMEM((frames, width, places), dtype),
            pltpu.VMEM((frames, width, places), dtype),
            pltpu.VMEM((width, places), dtype),
            pltpu.VMEM((width, places), dtype),
            pltpu.VMEM((n_dev, frames, run, width), dtype),
            pltpu.VMEM((n_dev, frames, run, width), dtype),
            pltpu.SemaphoreType.DMA,
            pltpu.SemaphoreType.DMA,
        ],
        compiler_params=pltpu.CompilerParams(collective_id=cid, has_side_effects=True),
    )(got_in, zero, gain.reshape(1, width), wq, wk, wv, out_w)


def temporal_attend(x, gain, wq, wk, wv, out_w, n_frame, cid):
    every, run, width = x.shape
    depth = width // HEADS
    scale = depth ** (-0.5)
    frames = every // n_frame
    rows = every * run
    lanes = width // 128

    def kernel(x_ref, g_ref, wq_ref, wk_ref, wv_ref, w_ref, o_ref, xs, qs, ks, vs, made, got, send_sem, recv_sem):
        fi = lax.axis_index("frame")
        barrier = pltpu.get_barrier_semaphore()
        for k in range(1, n_frame):
            pl.semaphore_signal(barrier, inc=1, device_id={"frame": (fi + k) % n_frame}, device_id_type=MESH)

        wide = x_ref[...].astype(jnp.float32).reshape(rows, width)
        factor = lax.rsqrt(jnp.mean(wide * wide, axis=-1, keepdims=True) + 1e-06)
        normed_two = (wide * factor * g_ref[...]).astype(jnp.bfloat16)
        def keep(ref, values):
            for c in range(lanes):
                ref[c] = values[:, c * 128 : (c + 1) * 128]

        def gather(ref, p):
            place = pl.ds(p, every, stride=run)
            return jnp.concatenate([ref[c, place, :] for c in range(lanes)], axis=-1)

        keep(xs, wide)
        for ref, weight in ((qs, wq_ref), (ks, wk_ref), (vs, wv_ref)):
            projected = jnp.dot(normed_two, weight[...], preferred_element_type=jnp.float32)
            keep(ref, projected.astype(jnp.bfloat16).astype(jnp.float32))

        for p in range(run):
            q = gather(qs, p).astype(jnp.bfloat16)
            k = gather(ks, p).astype(jnp.bfloat16)
            v = gather(vs, p).astype(jnp.bfloat16)
            acc = gather(xs, p)
            for h in range(HEADS):
                part = slice(h * depth, (h + 1) * depth)
                contract = (((1,), (1,)), ((), ()))
                scores = lax.dot_general(q[:, part], k[:, part], contract, preferred_element_type=jnp.float32) * scale
                weights = jnp.exp(scores - jnp.max(scores, axis=-1, keepdims=True))
                totals = jnp.sum(weights, axis=-1, keepdims=True)
                summed = jnp.dot(weights.astype(jnp.bfloat16), v[:, part], preferred_element_type=jnp.float32)
                attended = (summed / totals).astype(jnp.bfloat16)
                acc = acc + jnp.dot(attended, w_ref[part, :], preferred_element_type=jnp.float32)
            made[p] = acc.astype(made.dtype)
            if p == 0:
                pl.semaphore_wait(barrier, n_frame - 1)
            for g in range(n_frame):
                @pl.when(g == fi)
                def _():
                    got[fi, p] = made[p, pl.ds(g * frames, frames)]

                @pl.when(g != fi)
                def _():
                    pltpu.make_async_remote_copy(
                        src_ref=made.at[p, pl.ds(g * frames, frames)],
                        dst_ref=got.at[fi, p],
                        send_sem=send_sem,
                        recv_sem=recv_sem,
                        device_id={"frame": g},
                        device_id_type=MESH,
                    ).start()

        others = pltpu.make_async_copy(got.at[pl.ds(0, n_frame - 1)], got.at[pl.ds(1, n_frame - 1)], recv_sem)
        others.wait()
        sent = pltpu.make_async_copy(got.at[pl.ds(0, n_frame - 1)], got.at[pl.ds(1, n_frame - 1)], send_sem)
        sent.wait()
        o_ref[...] = got[...]

    vmem = pl.BlockSpec(memory_space=pltpu.VMEM)
    return pl.pallas_call(
        kernel,
        out_shape=jax.ShapeDtypeStruct((n_frame, run, frames, width), x.dtype),
        in_specs=[vmem] * 6,
        out_specs=vmem,
        scratch_shapes=[
            pltpu.VMEM((lanes, rows, 128), jnp.float32),
            pltpu.VMEM((lanes, rows, 128), jnp.float32),
            pltpu.VMEM((lanes, rows, 128), jnp.float32),
            pltpu.VMEM((lanes, rows, 128), jnp.float32),
            pltpu.VMEM((run, every, width), x.dtype),
            pltpu.VMEM((n_frame, run, frames, width), x.dtype),
            pltpu.SemaphoreType.DMA,
            pltpu.SemaphoreType.DMA,
        ],
        compiler_params=pltpu.CompilerParams(collective_id=cid, has_side_effects=True),
    )(x, gain.reshape(1, width), wq, wk, wv, out_w)


def transposed(values, weight):
    result = jnp.einsum("...rc,cd->...dr", values, weight, preferred_element_type=jnp.float32)
    return result.astype(jnp.bfloat16)


def normed(values, gain):
    wide = values.astype(jnp.float32)
    factor = lax.rsqrt(jnp.mean(wide * wide, axis=-1, keepdims=True) + 1e-06)
    return (wide * factor * gain).astype(jnp.bfloat16)


def project(values, weight):
    flat = values.reshape(-1, values.shape[-1])
    result = jnp.dot(flat, weight, preferred_element_type=jnp.float32).astype(jnp.bfloat16)
    return result.reshape(values.shape[:-1] + (weight.shape[1],))


def heads_of(values):
    return values.reshape(values.shape[:-1] + (HEADS, values.shape[-1] // HEADS))


def softmax_attend(query, keys, vals, score_form, value_form, total_form):
    scale = query.shape[-1] ** (-0.5)
    scores = jnp.einsum(score_form, query, keys, preferred_element_type=jnp.float32) * scale
    weights = jnp.exp(scores - jnp.max(scores, axis=-1, keepdims=True))
    totals = jnp.sum(weights, axis=-1)
    summed = jnp.einsum(
        value_form, weights.astype(jnp.bfloat16), vals, preferred_element_type=jnp.float32
    )
    return summed / jnp.einsum(total_form, totals)[..., None]


def shards(
    latents,
    gain_one,
    query_one,
    key_one,
    value_one,
    out_one,
    gain_two,
    query_two,
    key_two,
    value_two,
    out_two,
):
    frames, places, width = latents.shape
    n_pos = lax.axis_size("pos")
    n_frame = lax.axis_size("frame")
    per = frames // n_pos
    got, zero = spatial_exchange(latents.reshape(n_pos, per, places, width), n_pos, n_frame, 1)
    got = spatial_attend(
        got, zero, gain_one, query_one, key_one, value_one, out_one,
        min(256, n_pos * places), n_frame, n_pos, 2,
    )
    all_places = n_pos * places
    run = all_places // (n_pos * n_frame)
    mid_t = got.reshape(n_frame * n_pos * per, run, width)
    got = temporal_attend(mid_t, gain_two, query_two, key_two, value_two, out_two, n_frame, 3)
    return got.transpose(2, 0, 1, 3).reshape(frames, places, width)


def solution(mesh):
    return jax.shard_map(
        shards,
        mesh=mesh,
        in_specs=(P("frame", "pos", None), P(), P(), P(), P(), P(), P(), P(), P(), P(), P()),
        out_specs=P("frame", "pos", None),
        check_vma=False,
    )
```

```python
import jax
import jax.numpy as jnp
from jax import lax
from jax.experimental import pallas as pl
from jax.experimental.pallas import tpu as pltpu
from jax.sharding import PartitionSpec as P

HEADS = 4

MESH = pl.DeviceIdType.MESH


def exchange(x, names, sizes, cid):
    n = x.shape[0]

    def where(peer):
        if len(names) == 1:
            return {names[0]: peer}
        return {names[0]: peer // sizes[1], names[1]: peer % sizes[1]}

    def kernel(x_ref, o_ref, send_sem, recv_sem):
        me = lax.axis_index(names[0])
        if len(names) == 2:
            me = me * sizes[1] + lax.axis_index(names[1])
        barrier = pltpu.get_barrier_semaphore()
        for k in range(1, n):
            pl.semaphore_signal(barrier, inc=1, device_id=where((me + k) % n), device_id_type=MESH)
        pl.semaphore_wait(barrier, n - 1)
        copies = []
        for k in range(1, n):
            peer = (me + k) % n
            copy = pltpu.make_async_remote_copy(
                src_ref=x_ref.at[peer],
                dst_ref=o_ref.at[me],
                send_sem=send_sem.at[k],
                recv_sem=recv_sem.at[k],
                device_id=where(peer),
                device_id_type=MESH,
            )
            copy.start()
            copies.append(copy)
        o_ref[me] = x_ref[me]
        for copy in copies:
            copy.wait()

    return pl.pallas_call(
        kernel,
        out_shape=jax.ShapeDtypeStruct(x.shape, x.dtype),
        in_specs=[pl.BlockSpec(memory_space=pltpu.VMEM)],
        out_specs=pl.BlockSpec(memory_space=pltpu.VMEM),
        scratch_shapes=[pltpu.SemaphoreType.DMA((n,)), pltpu.SemaphoreType.DMA((n,))],
        compiler_params=pltpu.CompilerParams(collective_id=cid, has_side_effects=True),
    )(x)


def spatial_exchange(x, n_pos, n_frame, cid):
    _, per, places, width = x.shape

    def kernel(x_ref, o_ref, z_ref, send_sem, recv_sem, fsend_sem, frecv_sem, zsend_sem, zrecv_sem, local_sem):
        fi = lax.axis_index("frame")
        pi = lax.axis_index("pos")
        barrier = pltpu.get_barrier_semaphore()
        for k in range(1, n_pos):
            pl.semaphore_signal(barrier, inc=1, device_id={"pos": (pi + k) % n_pos}, device_id_type=MESH)
        for g in range(1, n_frame):
            pl.semaphore_signal(barrier, inc=1, device_id={"frame": (fi + g) % n_frame}, device_id_type=MESH)
        pl.semaphore_wait(barrier, n_pos - 1 + n_frame - 1)
        def spread(g):
            return pltpu.make_async_remote_copy(
                src_ref=x_ref.at[0, 0],
                dst_ref=z_ref.at[pi],
                send_sem=fsend_sem.at[g],
                recv_sem=frecv_sem,
                device_id={"frame": g},
                device_id_type=MESH,
            )

        @pl.when(fi == 0)
        def _():
            for g in range(1, n_frame):
                spread(g).start()

        copies = []
        for k in range(1, n_pos):
            peer = (pi + k) % n_pos
            copy = pltpu.make_async_remote_copy(
                src_ref=x_ref.at[peer],
                dst_ref=o_ref.at[pi],
                send_sem=send_sem.at[k],
                recv_sem=recv_sem.at[k],
                device_id={"pos": peer},
                device_id_type=MESH,
            )
            copy.start()
            copies.append(copy)

        @pl.when(fi == 0)
        def _():
            local = pltpu.make_async_copy(x_ref.at[0, 0], z_ref.at[pi], local_sem)
            local.start()
            local.wait()

        @pl.when(fi != 0)
        def _():
            spread(1).wait_recv()

        for k in range(1, n_pos):
            peer = (pi + k) % n_pos
            copy = pltpu.make_async_remote_copy(
                src_ref=z_ref.at[pi],
                dst_ref=z_ref.at[pi],
                send_sem=zsend_sem.at[k],
                recv_sem=zrecv_sem.at[k],
                device_id={"pos": peer},
                device_id_type=MESH,
            )
            copy.start()
            copies.append(copy)

        @pl.when(fi == 0)
        def _():
            for g in range(1, n_frame):
                spread(g).wait_send()

        for copy in copies:
            copy.wait()
        o_ref[pi] = x_ref[pi]

    return pl.pallas_call(
        kernel,
        out_shape=(
            jax.ShapeDtypeStruct(x.shape, x.dtype),
            jax.ShapeDtypeStruct((n_pos, places, width), x.dtype),
        ),
        in_specs=[pl.BlockSpec(memory_space=pltpu.VMEM)],
        out_specs=(pl.BlockSpec(memory_space=pltpu.VMEM), pl.BlockSpec(memory_space=pltpu.VMEM)),
        scratch_shapes=[
            pltpu.SemaphoreType.DMA((n_pos,)),
            pltpu.SemaphoreType.DMA((n_pos,)),
            pltpu.SemaphoreType.DMA((n_frame,)),
            pltpu.SemaphoreType.DMA,
            pltpu.SemaphoreType.DMA((n_pos,)),
            pltpu.SemaphoreType.DMA((n_pos,)),
            pltpu.SemaphoreType.DMA,
        ],
        compiler_params=pltpu.CompilerParams(collective_id=cid, has_side_effects=True),
    )(x)


def spatial_attend(got_in, zero, gain, wq, wk, wv, out_w, rows, n_frame, n_pos, cid):
    _, frames, slab, width = got_in.shape
    places = n_pos * slab
    depth = width // HEADS
    scale = depth ** (-0.5)
    n_dev = n_frame * n_pos
    run = places // n_dev
    chunks = rows // run
    n_tiles = places // rows
    per_tile = rows // slab

    def kernel(x_ref, z_ref, g_ref, wq_ref, wkt_ref, wvt_ref, w_ref, o_ref,
               q_ref, kt_ref, vt_ref, k0t_ref, v0t_ref, made, got, send_sem, recv_sem):
        t = pl.program_id(0)
        fi = lax.axis_index("frame")
        pi = lax.axis_index("pos")
        me = fi * n_pos + pi
        barrier = pltpu.get_barrier_semaphore()
        contract = (((1,), (1,)), ((), ()))

        def normed_rows(values):
            wide = values.reshape(places, width).astype(jnp.float32)
            factor = lax.rsqrt(jnp.mean(wide * wide, axis=-1, keepdims=True) + 1e-06)
            return (wide * factor * g_ref[...]).astype(jnp.bfloat16)

        def channels_first(weight_t, values):
            return lax.dot_general(weight_t, values, contract, preferred_element_type=jnp.float32).astype(jnp.bfloat16)

        @pl.when(t == 0)
        def _():
            for k in range(1, n_dev):
                peer = (me + k) % n_dev
                pl.semaphore_signal(
                    barrier, inc=1, device_id={"frame": peer // n_pos, "pos": peer % n_pos}, device_id_type=MESH
                )
            wkt = wkt_ref[...].T
            wvt = wvt_ref[...].T
            for f in range(frames):
                normed_one = normed_rows(x_ref[:, f])
                q_ref[f] = jnp.dot(normed_one, wq_ref[...], preferred_element_type=jnp.float32).astype(jnp.bfloat16)
                kt_ref[f] = channels_first(wkt, normed_one)
                vt_ref[f] = channels_first(wvt, normed_one)
            normed_zero = normed_rows(z_ref[...])
            k0t_ref[...] = channels_first(wkt, normed_zero)
            v0t_ref[...] = channels_first(wvt, normed_zero)

        tt = (t + fi + pi) % n_tiles
        base = tt * chunks
        these = pl.ds(pl.multiple_of(tt * rows, rows), rows)
        for f in range(frames):
            acc = x_ref[pl.ds(tt * per_tile, per_tile), f].reshape(rows, width).astype(jnp.float32)
            for h in range(HEADS):
                part = pl.ds(h * depth, depth)
                qh = q_ref[f, these, part]
                own = jnp.dot(qh, kt_ref[f, part, :], preferred_element_type=jnp.float32) * scale
                first = jnp.dot(qh, k0t_ref[part, :], preferred_element_type=jnp.float32) * scale
                high = jnp.maximum(
                    jnp.max(own, axis=-1, keepdims=True), jnp.max(first, axis=-1, keepdims=True)
                )
                own = jnp.exp(own - high)
                first = jnp.exp(first - high)
                totals = jnp.sum(own, axis=-1, keepdims=True) + jnp.sum(first, axis=-1, keepdims=True)
                summed = lax.dot_general(
                    own.astype(jnp.bfloat16), vt_ref[f, part, :], contract, preferred_element_type=jnp.float32
                ) + lax.dot_general(
                    first.astype(jnp.bfloat16), v0t_ref[part, :], contract, preferred_element_type=jnp.float32
                )
                attended = (summed / totals).astype(jnp.bfloat16)
                acc = acc + jnp.dot(attended, w_ref[part, :], preferred_element_type=jnp.float32)
            made[pl.ds(base, chunks), f] = acc.reshape(chunks, run, width).astype(made.dtype)

        @pl.when(t == 0)
        def _():
            pl.semaphore_wait(barrier, n_dev - 1)

        for i in range(chunks):
            gf = i % n_frame
            gp = (base + i) // n_frame

            @pl.when((gf == fi) & (gp == pi))
            def _():
                got[me] = made[base + i]

            @pl.when((gf != fi) | (gp != pi))
            def _():
                pltpu.make_async_remote_copy(
                    src_ref=made.at[base + i],
                    dst_ref=got.at[me],
                    send_sem=send_sem,
                    recv_sem=recv_sem,
                    device_id={"frame": gf, "pos": gp},
                    device_id_type=MESH,
                ).start()

        @pl.when(t == n_tiles - 1)
        def _():
            others = pltpu.make_async_copy(got.at[pl.ds(0, n_dev - 1)], got.at[pl.ds(1, n_dev - 1)], recv_sem)
            others.wait()
            sent = pltpu.make_async_copy(got.at[pl.ds(0, n_dev - 1)], got.at[pl.ds(1, n_dev - 1)], send_sem)
            sent.wait()
            o_ref[...] = got[...]

    fixed = lambda t: (0, 0)
    dtype = got_in.dtype
    return pl.pallas_call(
        kernel,
        out_shape=jax.ShapeDtypeStruct((n_dev, frames, run, width), dtype),
        grid=(n_tiles,),
        in_specs=[
            pl.BlockSpec(memory_space=pltpu.VMEM),
            pl.BlockSpec(memory_space=pltpu.VMEM),
            pl.BlockSpec((1, width), fixed),
            pl.BlockSpec((width, width), fixed),
            pl.BlockSpec((width, width), fixed),
            pl.BlockSpec((width, width), fixed),
            pl.BlockSpec((width, width), fixed),
        ],
        out_specs=pl.BlockSpec(memory_space=pltpu.VMEM),
        scratch_shapes=[
            pltpu.VMEM((frames, places, width), dtype),
            pltpu.VMEM((frames, width, places), dtype),
            pltpu.VMEM((frames, width, places), dtype),
            pltpu.VMEM((width, places), dtype),
            pltpu.VMEM((width, places), dtype),
            pltpu.VMEM((n_dev, frames, run, width), dtype),
            pltpu.VMEM((n_dev, frames, run, width), dtype),
            pltpu.SemaphoreType.DMA,
            pltpu.SemaphoreType.DMA,
        ],
        compiler_params=pltpu.CompilerParams(collective_id=cid, has_side_effects=True),
    )(got_in, zero, gain.reshape(1, width), wq, wk, wv, out_w)


def temporal_attend(x, gain, wq, wk, wv, out_w, n_frame, cid):
    every, run, width = x.shape
    depth = width // HEADS
    scale = depth ** (-0.5)
    frames = every // n_frame
    rows = every * run
    lanes = width // 128

    def kernel(x_ref, g_ref, wq_ref, wk_ref, wv_ref, w_ref, o_ref, xs, qs, ks, vs, made, got, send_sem, recv_sem):
        fi = lax.axis_index("frame")
        barrier = pltpu.get_barrier_semaphore()
        for k in range(1, n_frame):
            pl.semaphore_signal(barrier, inc=1, device_id={"frame": (fi + k) % n_frame}, device_id_type=MESH)

        wide = x_ref[...].astype(jnp.float32).reshape(rows, width)
        factor = lax.rsqrt(jnp.mean(wide * wide, axis=-1, keepdims=True) + 1e-06)
        normed_two = (wide * factor * g_ref[...]).astype(jnp.bfloat16)
        def keep(ref, values):
            for c in range(lanes):
                ref[c] = values[:, c * 128 : (c + 1) * 128]

        def gather(ref, p):
            place = pl.ds(p, every, stride=run)
            return jnp.concatenate([ref[c, place, :] for c in range(lanes)], axis=-1)

        keep(xs, wide)
        for ref, weight in ((qs, wq_ref), (ks, wk_ref), (vs, wv_ref)):
            projected = jnp.dot(normed_two, weight[...], preferred_element_type=jnp.float32)
            keep(ref, projected.astype(jnp.bfloat16).astype(jnp.float32))

        for p in range(run):
            q = gather(qs, p).astype(jnp.bfloat16)
            k = gather(ks, p).astype(jnp.bfloat16)
            v = gather(vs, p).astype(jnp.bfloat16)
            acc = gather(xs, p)
            for h in range(HEADS):
                part = slice(h * depth, (h + 1) * depth)
                contract = (((1,), (1,)), ((), ()))
                scores = lax.dot_general(q[:, part], k[:, part], contract, preferred_element_type=jnp.float32) * scale
                weights = jnp.exp(scores - jnp.max(scores, axis=-1, keepdims=True))
                totals = jnp.sum(weights, axis=-1, keepdims=True)
                summed = jnp.dot(weights.astype(jnp.bfloat16), v[:, part], preferred_element_type=jnp.float32)
                attended = (summed / totals).astype(jnp.bfloat16)
                acc = acc + jnp.dot(attended, w_ref[part, :], preferred_element_type=jnp.float32)
            made[p] = acc.astype(made.dtype)
            if p == 0:
                pl.semaphore_wait(barrier, n_frame - 1)
            for g in range(n_frame):
                @pl.when(g == fi)
                def _():
                    got[fi, p] = made[p, pl.ds(g * frames, frames)]

                @pl.when(g != fi)
                def _():
                    pltpu.make_async_remote_copy(
                        src_ref=made.at[p, pl.ds(g * frames, frames)],
                        dst_ref=got.at[fi, p],
                        send_sem=send_sem,
                        recv_sem=recv_sem,
                        device_id={"frame": g},
                        device_id_type=MESH,
                    ).start()

        others = pltpu.make_async_copy(got.at[pl.ds(0, n_frame - 1)], got.at[pl.ds(1, n_frame - 1)], recv_sem)
        others.wait()
        sent = pltpu.make_async_copy(got.at[pl.ds(0, n_frame - 1)], got.at[pl.ds(1, n_frame - 1)], send_sem)
        sent.wait()
        for g in range(n_frame):
            for p in range(run):
                block = got[g, p].astype(jnp.float32)
                for c in range(lanes):
                    xs[c, pl.ds(g * run + p, frames, stride=n_frame * run), :] = block[:, c * 128 : (c + 1) * 128]
        whole = jnp.concatenate([xs[c, pl.ds(0, frames * n_frame * run), :] for c in range(lanes)], axis=-1)
        o_ref[...] = whole.astype(o_ref.dtype).reshape(frames, n_frame * run, width)

    vmem = pl.BlockSpec(memory_space=pltpu.VMEM)
    return pl.pallas_call(
        kernel,
        out_shape=jax.ShapeDtypeStruct((frames, n_frame * run, width), x.dtype),
        in_specs=[vmem] * 6,
        out_specs=vmem,
        scratch_shapes=[
            pltpu.VMEM((lanes, rows, 128), jnp.float32),
            pltpu.VMEM((lanes, rows, 128), jnp.float32),
            pltpu.VMEM((lanes, rows, 128), jnp.float32),
            pltpu.VMEM((lanes, rows, 128), jnp.float32),
            pltpu.VMEM((run, every, width), x.dtype),
            pltpu.VMEM((n_frame, run, frames, width), x.dtype),
            pltpu.SemaphoreType.DMA,
            pltpu.SemaphoreType.DMA,
        ],
        compiler_params=pltpu.CompilerParams(collective_id=cid, has_side_effects=True),
    )(x, gain.reshape(1, width), wq, wk, wv, out_w)


def transposed(values, weight):
    result = jnp.einsum("...rc,cd->...dr", values, weight, preferred_element_type=jnp.float32)
    return result.astype(jnp.bfloat16)


def normed(values, gain):
    wide = values.astype(jnp.float32)
    factor = lax.rsqrt(jnp.mean(wide * wide, axis=-1, keepdims=True) + 1e-06)
    return (wide * factor * gain).astype(jnp.bfloat16)


def project(values, weight):
    flat = values.reshape(-1, values.shape[-1])
    result = jnp.dot(flat, weight, preferred_element_type=jnp.float32).astype(jnp.bfloat16)
    return result.reshape(values.shape[:-1] + (weight.shape[1],))


def heads_of(values):
    return values.reshape(values.shape[:-1] + (HEADS, values.shape[-1] // HEADS))


def softmax_attend(query, keys, vals, score_form, value_form, total_form):
    scale = query.shape[-1] ** (-0.5)
    scores = jnp.einsum(score_form, query, keys, preferred_element_type=jnp.float32) * scale
    weights = jnp.exp(scores - jnp.max(scores, axis=-1, keepdims=True))
    totals = jnp.sum(weights, axis=-1)
    summed = jnp.einsum(
        value_form, weights.astype(jnp.bfloat16), vals, preferred_element_type=jnp.float32
    )
    return summed / jnp.einsum(total_form, totals)[..., None]


def shards(
    latents,
    gain_one,
    query_one,
    key_one,
    value_one,
    out_one,
    gain_two,
    query_two,
    key_two,
    value_two,
    out_two,
):
    frames, places, width = latents.shape
    n_pos = lax.axis_size("pos")
    n_frame = lax.axis_size("frame")
    per = frames // n_pos
    got, zero = spatial_exchange(latents.reshape(n_pos, per, places, width), n_pos, n_frame, 1)
    got = spatial_attend(
        got, zero, gain_one, query_one, key_one, value_one, out_one,
        min(256, n_pos * places), n_frame, n_pos, 2,
    )
    all_places = n_pos * places
    run = all_places // (n_pos * n_frame)
    mid_t = got.reshape(n_frame * n_pos * per, run, width)
    return temporal_attend(mid_t, gain_two, query_two, key_two, value_two, out_two, n_frame, 3)


def solution(mesh):
    return jax.shard_map(
        shards,
        mesh=mesh,
        in_specs=(P("frame", "pos", None), P(), P(), P(), P(), P(), P(), P(), P(), P(), P()),
        out_specs=P("frame", "pos", None),
        check_vma=False,
    )
```

```python
import jax
import jax.numpy as jnp
from jax import lax
from jax.experimental import pallas as pl
from jax.experimental.pallas import tpu as pltpu
from jax.sharding import PartitionSpec as P

HEADS = 4

MESH = pl.DeviceIdType.MESH


def exchange(x, names, sizes, cid):
    n = x.shape[0]

    def where(peer):
        if len(names) == 1:
            return {names[0]: peer}
        return {names[0]: peer // sizes[1], names[1]: peer % sizes[1]}

    def kernel(x_ref, o_ref, send_sem, recv_sem):
        me = lax.axis_index(names[0])
        if len(names) == 2:
            me = me * sizes[1] + lax.axis_index(names[1])
        barrier = pltpu.get_barrier_semaphore()
        for k in range(1, n):
            pl.semaphore_signal(barrier, inc=1, device_id=where((me + k) % n), device_id_type=MESH)
        pl.semaphore_wait(barrier, n - 1)
        copies = []
        for k in range(1, n):
            peer = (me + k) % n
            copy = pltpu.make_async_remote_copy(
                src_ref=x_ref.at[peer],
                dst_ref=o_ref.at[me],
                send_sem=send_sem.at[k],
                recv_sem=recv_sem.at[k],
                device_id=where(peer),
                device_id_type=MESH,
            )
            copy.start()
            copies.append(copy)
        o_ref[me] = x_ref[me]
        for copy in copies:
            copy.wait()

    return pl.pallas_call(
        kernel,
        out_shape=jax.ShapeDtypeStruct(x.shape, x.dtype),
        in_specs=[pl.BlockSpec(memory_space=pltpu.VMEM)],
        out_specs=pl.BlockSpec(memory_space=pltpu.VMEM),
        scratch_shapes=[pltpu.SemaphoreType.DMA((n,)), pltpu.SemaphoreType.DMA((n,))],
        compiler_params=pltpu.CompilerParams(collective_id=cid, has_side_effects=True),
    )(x)


def spatial_exchange(x, n_pos, n_frame, cid):
    _, per, places, width = x.shape

    def kernel(x_ref, o_ref, z_ref, send_sem, recv_sem, fsend_sem, frecv_sem, zsend_sem, zrecv_sem, local_sem):
        fi = lax.axis_index("frame")
        pi = lax.axis_index("pos")
        barrier = pltpu.get_barrier_semaphore()
        for k in range(1, n_pos):
            pl.semaphore_signal(barrier, inc=1, device_id={"pos": (pi + k) % n_pos}, device_id_type=MESH)
        for g in range(1, n_frame):
            pl.semaphore_signal(barrier, inc=1, device_id={"frame": (fi + g) % n_frame}, device_id_type=MESH)
        pl.semaphore_wait(barrier, n_pos - 1 + n_frame - 1)
        def spread(g):
            return pltpu.make_async_remote_copy(
                src_ref=x_ref.at[0, 0],
                dst_ref=z_ref.at[pi],
                send_sem=fsend_sem.at[g],
                recv_sem=frecv_sem,
                device_id={"frame": g},
                device_id_type=MESH,
            )

        @pl.when(fi == 0)
        def _():
            for g in range(1, n_frame):
                spread(g).start()

        copies = []
        for k in range(1, n_pos):
            peer = (pi + k) % n_pos
            copy = pltpu.make_async_remote_copy(
                src_ref=x_ref.at[peer],
                dst_ref=o_ref.at[pi],
                send_sem=send_sem.at[k],
                recv_sem=recv_sem.at[k],
                device_id={"pos": peer},
                device_id_type=MESH,
            )
            copy.start()
            copies.append(copy)

        @pl.when(fi == 0)
        def _():
            local = pltpu.make_async_copy(x_ref.at[0, 0], z_ref.at[pi], local_sem)
            local.start()
            local.wait()

        @pl.when(fi != 0)
        def _():
            spread(1).wait_recv()

        for k in range(1, n_pos):
            peer = (pi + k) % n_pos
            copy = pltpu.make_async_remote_copy(
                src_ref=z_ref.at[pi],
                dst_ref=z_ref.at[pi],
                send_sem=zsend_sem.at[k],
                recv_sem=zrecv_sem.at[k],
                device_id={"pos": peer},
                device_id_type=MESH,
            )
            copy.start()
            copies.append(copy)

        @pl.when(fi == 0)
        def _():
            for g in range(1, n_frame):
                spread(g).wait_send()

        for copy in copies:
            copy.wait()
        o_ref[pi] = x_ref[pi]

    return pl.pallas_call(
        kernel,
        out_shape=(
            jax.ShapeDtypeStruct(x.shape, x.dtype),
            jax.ShapeDtypeStruct((n_pos, places, width), x.dtype),
        ),
        in_specs=[pl.BlockSpec(memory_space=pltpu.VMEM)],
        out_specs=(pl.BlockSpec(memory_space=pltpu.VMEM), pl.BlockSpec(memory_space=pltpu.VMEM)),
        scratch_shapes=[
            pltpu.SemaphoreType.DMA((n_pos,)),
            pltpu.SemaphoreType.DMA((n_pos,)),
            pltpu.SemaphoreType.DMA((n_frame,)),
            pltpu.SemaphoreType.DMA,
            pltpu.SemaphoreType.DMA((n_pos,)),
            pltpu.SemaphoreType.DMA((n_pos,)),
            pltpu.SemaphoreType.DMA,
        ],
        compiler_params=pltpu.CompilerParams(collective_id=cid, has_side_effects=True),
    )(x)


def spatial_attend(got_in, zero, gain, wq, wk, wv, out_w, rows, n_frame, n_pos, cid):
    _, frames, slab, width = got_in.shape
    places = n_pos * slab
    depth = width // HEADS
    scale = depth ** (-0.5)
    n_dev = n_frame * n_pos
    run = places // n_dev
    chunks = rows // run
    n_tiles = places // rows
    per_tile = rows // slab

    def kernel(x_ref, z_ref, g_ref, wq_ref, wkt_ref, wvt_ref, w_ref, o_ref,
               q_ref, kt_ref, vt_ref, k0t_ref, v0t_ref, made, got, send_sem, recv_sem):
        t = pl.program_id(0)
        fi = lax.axis_index("frame")
        pi = lax.axis_index("pos")
        me = fi * n_pos + pi
        barrier = pltpu.get_barrier_semaphore()
        contract = (((1,), (1,)), ((), ()))

        def normed_rows(values):
            wide = values.reshape(places, width).astype(jnp.float32)
            factor = lax.rsqrt(jnp.mean(wide * wide, axis=-1, keepdims=True) + 1e-06)
            return (wide * factor * g_ref[...]).astype(jnp.bfloat16)

        def channels_first(weight_t, values):
            return lax.dot_general(weight_t, values, contract, preferred_element_type=jnp.float32).astype(jnp.bfloat16)

        @pl.when(t == 0)
        def _():
            for k in range(1, n_dev):
                peer = (me + k) % n_dev
                pl.semaphore_signal(
                    barrier, inc=1, device_id={"frame": peer // n_pos, "pos": peer % n_pos}, device_id_type=MESH
                )
            wkt = wkt_ref[...].T
            wvt = wvt_ref[...].T
            for f in range(frames):
                normed_one = normed_rows(x_ref[:, f])
                q_ref[f] = jnp.dot(normed_one, wq_ref[...], preferred_element_type=jnp.float32).astype(jnp.bfloat16)
                kt_ref[f] = channels_first(wkt, normed_one)
                vt_ref[f] = channels_first(wvt, normed_one)
            normed_zero = normed_rows(z_ref[...])
            k0t_ref[...] = channels_first(wkt, normed_zero)
            v0t_ref[...] = channels_first(wvt, normed_zero)

        tt = (t + fi + pi) % n_tiles
        base = tt * chunks
        these = pl.ds(pl.multiple_of(tt * rows, rows), rows)
        for f in range(frames):
            acc = x_ref[pl.ds(tt * per_tile, per_tile), f].reshape(rows, width).astype(jnp.float32)
            for h in range(HEADS):
                part = pl.ds(h * depth, depth)
                qh = q_ref[f, these, part]
                own = jnp.dot(qh, kt_ref[f, part, :], preferred_element_type=jnp.float32) * scale
                first = jnp.dot(qh, k0t_ref[part, :], preferred_element_type=jnp.float32) * scale
                high = jnp.maximum(
                    jnp.max(own, axis=-1, keepdims=True), jnp.max(first, axis=-1, keepdims=True)
                )
                own = jnp.exp(own - high)
                first = jnp.exp(first - high)
                totals = jnp.sum(own, axis=-1, keepdims=True) + jnp.sum(first, axis=-1, keepdims=True)
                summed = lax.dot_general(
                    own.astype(jnp.bfloat16), vt_ref[f, part, :], contract, preferred_element_type=jnp.float32
                ) + lax.dot_general(
                    first.astype(jnp.bfloat16), v0t_ref[part, :], contract, preferred_element_type=jnp.float32
                )
                attended = (summed / totals).astype(jnp.bfloat16)
                acc = acc + jnp.dot(attended, w_ref[part, :], preferred_element_type=jnp.float32)
            made[pl.ds(base, chunks), f] = acc.reshape(chunks, run, width).astype(made.dtype)

        @pl.when(t == 0)
        def _():
            pl.semaphore_wait(barrier, n_dev - 1)

        for i in range(chunks):
            gf = i % n_frame
            gp = (base + i) // n_frame

            @pl.when((gf == fi) & (gp == pi))
            def _():
                got[me] = made[base + i]

            @pl.when((gf != fi) | (gp != pi))
            def _():
                pltpu.make_async_remote_copy(
                    src_ref=made.at[base + i],
                    dst_ref=got.at[me],
                    send_sem=send_sem,
                    recv_sem=recv_sem,
                    device_id={"frame": gf, "pos": gp},
                    device_id_type=MESH,
                ).start()

        @pl.when(t == n_tiles - 1)
        def _():
            others = pltpu.make_async_copy(got.at[pl.ds(0, n_dev - 1)], got.at[pl.ds(1, n_dev - 1)], recv_sem)
            others.wait()
            sent = pltpu.make_async_copy(got.at[pl.ds(0, n_dev - 1)], got.at[pl.ds(1, n_dev - 1)], send_sem)
            sent.wait()
            o_ref[...] = got[...]

    fixed = lambda t: (0, 0)
    dtype = got_in.dtype
    return pl.pallas_call(
        kernel,
        out_shape=jax.ShapeDtypeStruct((n_dev, frames, run, width), dtype),
        grid=(n_tiles,),
        in_specs=[
            pl.BlockSpec(memory_space=pltpu.VMEM),
            pl.BlockSpec(memory_space=pltpu.VMEM),
            pl.BlockSpec((1, width), fixed),
            pl.BlockSpec((width, width), fixed),
            pl.BlockSpec((width, width), fixed),
            pl.BlockSpec((width, width), fixed),
            pl.BlockSpec((width, width), fixed),
        ],
        out_specs=pl.BlockSpec(memory_space=pltpu.VMEM),
        scratch_shapes=[
            pltpu.VMEM((frames, places, width), dtype),
            pltpu.VMEM((frames, width, places), dtype),
            pltpu.VMEM((frames, width, places), dtype),
            pltpu.VMEM((width, places), dtype),
            pltpu.VMEM((width, places), dtype),
            pltpu.VMEM((n_dev, frames, run, width), dtype),
            pltpu.VMEM((n_dev, frames, run, width), dtype),
            pltpu.SemaphoreType.DMA,
            pltpu.SemaphoreType.DMA,
        ],
        compiler_params=pltpu.CompilerParams(collective_id=cid, has_side_effects=True),
    )(got_in, zero, gain.reshape(1, width), wq, wk, wv, out_w)


def temporal_attend(x, gain, wq, wk, wv, out_w, n_frame, cid):
    every, run, width = x.shape
    depth = width // HEADS
    scale = depth ** (-0.5)
    frames = every // n_frame
    rows = every * run
    lanes = width // 128

    def kernel(x_ref, g_ref, wq_ref, wk_ref, wv_ref, w_ref, o_ref, xs, qs, ks, vs, made, got, send_sem, recv_sem):
        fi = lax.axis_index("frame")
        barrier = pltpu.get_barrier_semaphore()
        for k in range(1, n_frame):
            pl.semaphore_signal(barrier, inc=1, device_id={"frame": (fi + k) % n_frame}, device_id_type=MESH)

        wide = x_ref[...].astype(jnp.float32).reshape(rows, width)
        factor = lax.rsqrt(jnp.mean(wide * wide, axis=-1, keepdims=True) + 1e-06)
        normed_two = (wide * factor * g_ref[...]).astype(jnp.bfloat16)
        def keep(ref, values):
            for c in range(lanes):
                ref[c] = values[:, c * 128 : (c + 1) * 128]

        def gather(ref, p):
            place = pl.ds(p, every, stride=run)
            return jnp.concatenate([ref[c, place, :] for c in range(lanes)], axis=-1)

        keep(xs, wide)
        for ref, weight in ((qs, wq_ref), (ks, wk_ref), (vs, wv_ref)):
            projected = jnp.dot(normed_two, weight[...], preferred_element_type=jnp.float32)
            keep(ref, projected.astype(jnp.bfloat16).astype(jnp.float32))

        for p in range(run):
            q = gather(qs, p).astype(jnp.bfloat16)
            k = gather(ks, p).astype(jnp.bfloat16)
            v = gather(vs, p).astype(jnp.bfloat16)
            acc = gather(xs, p)
            for h in range(HEADS):
                part = slice(h * depth, (h + 1) * depth)
                contract = (((1,), (1,)), ((), ()))
                scores = lax.dot_general(q[:, part], k[:, part], contract, preferred_element_type=jnp.float32) * scale
                weights = jnp.exp(scores - jnp.max(scores, axis=-1, keepdims=True))
                totals = jnp.sum(weights, axis=-1, keepdims=True)
                summed = jnp.dot(weights.astype(jnp.bfloat16), v[:, part], preferred_element_type=jnp.float32)
                attended = (summed / totals).astype(jnp.bfloat16)
                acc = acc + jnp.dot(attended, w_ref[part, :], preferred_element_type=jnp.float32)
            made[p] = acc.astype(made.dtype)
            if p == 0:
                pl.semaphore_wait(barrier, n_frame - 1)
            for g in range(n_frame):
                @pl.when(g == fi)
                def _():
                    got[fi, p] = made[p, pl.ds(g * frames, frames)]

                @pl.when(g != fi)
                def _():
                    pltpu.make_async_remote_copy(
                        src_ref=made.at[p, pl.ds(g * frames, frames)],
                        dst_ref=got.at[fi, p],
                        send_sem=send_sem,
                        recv_sem=recv_sem,
                        device_id={"frame": g},
                        device_id_type=MESH,
                    ).start()

        others = pltpu.make_async_copy(got.at[pl.ds(0, n_frame - 1)], got.at[pl.ds(1, n_frame - 1)], recv_sem)
        others.wait()
        sent = pltpu.make_async_copy(got.at[pl.ds(0, n_frame - 1)], got.at[pl.ds(1, n_frame - 1)], send_sem)
        sent.wait()
        o_ref[...] = got[...]

    vmem = pl.BlockSpec(memory_space=pltpu.VMEM)
    return pl.pallas_call(
        kernel,
        out_shape=jax.ShapeDtypeStruct((n_frame, run, frames, width), x.dtype),
        in_specs=[vmem] * 6,
        out_specs=vmem,
        scratch_shapes=[
            pltpu.VMEM((lanes, rows, 128), jnp.float32),
            pltpu.VMEM((lanes, rows, 128), jnp.float32),
            pltpu.VMEM((lanes, rows, 128), jnp.float32),
            pltpu.VMEM((lanes, rows, 128), jnp.float32),
            pltpu.VMEM((run, every, width), x.dtype),
            pltpu.VMEM((n_frame, run, frames, width), x.dtype),
            pltpu.SemaphoreType.DMA,
            pltpu.SemaphoreType.DMA,
        ],
        compiler_params=pltpu.CompilerParams(collective_id=cid, has_side_effects=True),
    )(x, gain.reshape(1, width), wq, wk, wv, out_w)


def transposed(values, weight):
    result = jnp.einsum("...rc,cd->...dr", values, weight, preferred_element_type=jnp.float32)
    return result.astype(jnp.bfloat16)


def normed(values, gain):
    wide = values.astype(jnp.float32)
    factor = lax.rsqrt(jnp.mean(wide * wide, axis=-1, keepdims=True) + 1e-06)
    return (wide * factor * gain).astype(jnp.bfloat16)


def project(values, weight):
    flat = values.reshape(-1, values.shape[-1])
    result = jnp.dot(flat, weight, preferred_element_type=jnp.float32).astype(jnp.bfloat16)
    return result.reshape(values.shape[:-1] + (weight.shape[1],))


def heads_of(values):
    return values.reshape(values.shape[:-1] + (HEADS, values.shape[-1] // HEADS))


def softmax_attend(query, keys, vals, score_form, value_form, total_form):
    scale = query.shape[-1] ** (-0.5)
    scores = jnp.einsum(score_form, query, keys, preferred_element_type=jnp.float32) * scale
    weights = jnp.exp(scores - jnp.max(scores, axis=-1, keepdims=True))
    totals = jnp.sum(weights, axis=-1)
    summed = jnp.einsum(
        value_form, weights.astype(jnp.bfloat16), vals, preferred_element_type=jnp.float32
    )
    return summed / jnp.einsum(total_form, totals)[..., None]


def shards(
    latents,
    gain_one,
    query_one,
    key_one,
    value_one,
    out_one,
    gain_two,
    query_two,
    key_two,
    value_two,
    out_two,
):
    frames, places, width = latents.shape
    n_pos = lax.axis_size("pos")
    n_frame = lax.axis_size("frame")
    per = frames // n_pos
    got, zero = spatial_exchange(latents.reshape(n_pos, per, places, width), n_pos, n_frame, 1)
    got = spatial_attend(
        got, zero, gain_one, query_one, key_one, value_one, out_one,
        min(512, n_pos * places), n_frame, n_pos, 2,
    )
    all_places = n_pos * places
    run = all_places // (n_pos * n_frame)
    mid_t = got.reshape(n_frame * n_pos * per, run, width)
    got = temporal_attend(mid_t, gain_two, query_two, key_two, value_two, out_two, n_frame, 3)
    return got.transpose(2, 0, 1, 3).reshape(frames, places, width)


def solution(mesh):
    return jax.shard_map(
        shards,
        mesh=mesh,
        in_specs=(P("frame", "pos", None), P(), P(), P(), P(), P(), P(), P(), P(), P(), P()),
        out_specs=P("frame", "pos", None),
        check_vma=False,
    )
```

```python
import jax
import jax.numpy as jnp
from jax import lax
from jax.experimental import pallas as pl
from jax.experimental.pallas import tpu as pltpu
from jax.sharding import PartitionSpec as P

HEADS = 4

MESH = pl.DeviceIdType.MESH


def exchange(x, names, sizes, cid):
    n = x.shape[0]

    def where(peer):
        if len(names) == 1:
            return {names[0]: peer}
        return {names[0]: peer // sizes[1], names[1]: peer % sizes[1]}

    def kernel(x_ref, o_ref, send_sem, recv_sem):
        me = lax.axis_index(names[0])
        if len(names) == 2:
            me = me * sizes[1] + lax.axis_index(names[1])
        barrier = pltpu.get_barrier_semaphore()
        for k in range(1, n):
            pl.semaphore_signal(barrier, inc=1, device_id=where((me + k) % n), device_id_type=MESH)
        pl.semaphore_wait(barrier, n - 1)
        copies = []
        for k in range(1, n):
            peer = (me + k) % n
            copy = pltpu.make_async_remote_copy(
                src_ref=x_ref.at[peer],
                dst_ref=o_ref.at[me],
                send_sem=send_sem.at[k],
                recv_sem=recv_sem.at[k],
                device_id=where(peer),
                device_id_type=MESH,
            )
            copy.start()
            copies.append(copy)
        o_ref[me] = x_ref[me]
        for copy in copies:
            copy.wait()

    return pl.pallas_call(
        kernel,
        out_shape=jax.ShapeDtypeStruct(x.shape, x.dtype),
        in_specs=[pl.BlockSpec(memory_space=pltpu.VMEM)],
        out_specs=pl.BlockSpec(memory_space=pltpu.VMEM),
        scratch_shapes=[pltpu.SemaphoreType.DMA((n,)), pltpu.SemaphoreType.DMA((n,))],
        compiler_params=pltpu.CompilerParams(collective_id=cid, has_side_effects=True),
    )(x)


def spatial_exchange(x, n_pos, n_frame, cid):
    _, per, places, width = x.shape

    def kernel(x_ref, o_ref, z_ref, send_sem, recv_sem, fsend_sem, frecv_sem, zsend_sem, zrecv_sem, local_sem):
        fi = lax.axis_index("frame")
        pi = lax.axis_index("pos")
        barrier = pltpu.get_barrier_semaphore()
        for k in range(1, n_pos):
            pl.semaphore_signal(barrier, inc=1, device_id={"pos": (pi + k) % n_pos}, device_id_type=MESH)
        for g in range(1, n_frame):
            pl.semaphore_signal(barrier, inc=1, device_id={"frame": (fi + g) % n_frame}, device_id_type=MESH)
        pl.semaphore_wait(barrier, n_pos - 1 + n_frame - 1)
        def spread(g):
            return pltpu.make_async_remote_copy(
                src_ref=x_ref.at[0, 0],
                dst_ref=z_ref.at[pi],
                send_sem=fsend_sem.at[g],
                recv_sem=frecv_sem,
                device_id={"frame": g},
                device_id_type=MESH,
            )

        @pl.when(fi == 0)
        def _():
            for g in range(1, n_frame):
                spread(g).start()

        copies = []
        for k in range(1, n_pos):
            peer = (pi + k) % n_pos
            copy = pltpu.make_async_remote_copy(
                src_ref=x_ref.at[peer],
                dst_ref=o_ref.at[pi],
                send_sem=send_sem.at[k],
                recv_sem=recv_sem.at[k],
                device_id={"pos": peer},
                device_id_type=MESH,
            )
            copy.start()
            copies.append(copy)

        @pl.when(fi == 0)
        def _():
            local = pltpu.make_async_copy(x_ref.at[0, 0], z_ref.at[pi], local_sem)
            local.start()
            local.wait()

        @pl.when(fi != 0)
        def _():
            spread(1).wait_recv()

        for k in range(1, n_pos):
            peer = (pi + k) % n_pos
            copy = pltpu.make_async_remote_copy(
                src_ref=z_ref.at[pi],
                dst_ref=z_ref.at[pi],
                send_sem=zsend_sem.at[k],
                recv_sem=zrecv_sem.at[k],
                device_id={"pos": peer},
                device_id_type=MESH,
            )
            copy.start()
            copies.append(copy)

        @pl.when(fi == 0)
        def _():
            for g in range(1, n_frame):
                spread(g).wait_send()

        for copy in copies:
            copy.wait()
        o_ref[pi] = x_ref[pi]

    return pl.pallas_call(
        kernel,
        out_shape=(
            jax.ShapeDtypeStruct(x.shape, x.dtype),
            jax.ShapeDtypeStruct((n_pos, places, width), x.dtype),
        ),
        in_specs=[pl.BlockSpec(memory_space=pltpu.VMEM)],
        out_specs=(pl.BlockSpec(memory_space=pltpu.VMEM), pl.BlockSpec(memory_space=pltpu.VMEM)),
        scratch_shapes=[
            pltpu.SemaphoreType.DMA((n_pos,)),
            pltpu.SemaphoreType.DMA((n_pos,)),
            pltpu.SemaphoreType.DMA((n_frame,)),
            pltpu.SemaphoreType.DMA,
            pltpu.SemaphoreType.DMA((n_pos,)),
            pltpu.SemaphoreType.DMA((n_pos,)),
            pltpu.SemaphoreType.DMA,
        ],
        compiler_params=pltpu.CompilerParams(collective_id=cid, has_side_effects=True),
    )(x)


def spatial_attend(got_in, zero, gain, wq, wk, wv, out_w, rows, n_frame, n_pos, cid):
    _, frames, slab, width = got_in.shape
    places = n_pos * slab
    depth = width // HEADS
    scale = depth ** (-0.5)
    n_dev = n_frame * n_pos
    run = places // n_dev
    chunks = rows // run
    n_tiles = places // rows
    per_tile = rows // slab

    def kernel(x_ref, z_ref, g_ref, wq_ref, wkt_ref, wvt_ref, w_ref, o_ref,
               q_ref, kt_ref, vt_ref, k0t_ref, v0t_ref, made, got, send_sem, recv_sem):
        t = pl.program_id(0)
        fi = lax.axis_index("frame")
        pi = lax.axis_index("pos")
        me = fi * n_pos + pi
        barrier = pltpu.get_barrier_semaphore()
        contract = (((1,), (1,)), ((), ()))

        def normed_rows(values):
            wide = values.reshape(places, width).astype(jnp.float32)
            factor = lax.rsqrt(jnp.mean(wide * wide, axis=-1, keepdims=True) + 1e-06)
            return (wide * factor * g_ref[...]).astype(jnp.bfloat16)

        def channels_first(weight_t, values):
            return lax.dot_general(weight_t, values, contract, preferred_element_type=jnp.float32).astype(jnp.bfloat16)

        @pl.when(t == 0)
        def _():
            for k in range(1, n_dev):
                peer = (me + k) % n_dev
                pl.semaphore_signal(
                    barrier, inc=1, device_id={"frame": peer // n_pos, "pos": peer % n_pos}, device_id_type=MESH
                )
            wkt = wkt_ref[...].T
            wvt = wvt_ref[...].T
            for f in range(frames):
                normed_one = normed_rows(x_ref[:, f])
                q_ref[f] = jnp.dot(normed_one, wq_ref[...], preferred_element_type=jnp.float32).astype(jnp.bfloat16)
                kt_ref[f] = channels_first(wkt, normed_one)
                vt_ref[f] = channels_first(wvt, normed_one)
            normed_zero = normed_rows(z_ref[...])
            k0t_ref[...] = channels_first(wkt, normed_zero)
            v0t_ref[...] = channels_first(wvt, normed_zero)

        tt = (t + fi + pi) % n_tiles
        base = tt * chunks
        these = pl.ds(pl.multiple_of(tt * rows, rows), rows)
        for f in range(frames):
            acc = x_ref[pl.ds(tt * per_tile, per_tile), f].reshape(rows, width).astype(jnp.float32)
            for h in range(HEADS):
                part = pl.ds(h * depth, depth)
                qh = q_ref[f, these, part]
                own = jnp.dot(qh, kt_ref[f, part, :], preferred_element_type=jnp.float32) * scale
                first = jnp.dot(qh, k0t_ref[part, :], preferred_element_type=jnp.float32) * scale
                high = jnp.maximum(
                    jnp.max(own, axis=-1, keepdims=True), jnp.max(first, axis=-1, keepdims=True)
                )
                own = jnp.exp(own - high)
                first = jnp.exp(first - high)
                totals = jnp.sum(own, axis=-1, keepdims=True) + jnp.sum(first, axis=-1, keepdims=True)
                summed = lax.dot_general(
                    own.astype(jnp.bfloat16), vt_ref[f, part, :], contract, preferred_element_type=jnp.float32
                ) + lax.dot_general(
                    first.astype(jnp.bfloat16), v0t_ref[part, :], contract, preferred_element_type=jnp.float32
                )
                attended = (summed / totals).astype(jnp.bfloat16)
                acc = acc + jnp.dot(attended, w_ref[part, :], preferred_element_type=jnp.float32)
            made[pl.ds(base, chunks), f] = acc.reshape(chunks, run, width).astype(made.dtype)

        @pl.when(t == 0)
        def _():
            pl.semaphore_wait(barrier, n_dev - 1)

        for i in range(chunks):
            gf = i % n_frame
            gp = (base + i) // n_frame

            @pl.when((gf == fi) & (gp == pi))
            def _():
                got[me] = made[base + i]

            @pl.when((gf != fi) | (gp != pi))
            def _():
                pltpu.make_async_remote_copy(
                    src_ref=made.at[base + i],
                    dst_ref=got.at[me],
                    send_sem=send_sem,
                    recv_sem=recv_sem,
                    device_id={"frame": gf, "pos": gp},
                    device_id_type=MESH,
                ).start()

        @pl.when(t == n_tiles - 1)
        def _():
            others = pltpu.make_async_copy(got.at[pl.ds(0, n_dev - 1)], got.at[pl.ds(1, n_dev - 1)], recv_sem)
            others.wait()
            sent = pltpu.make_async_copy(got.at[pl.ds(0, n_dev - 1)], got.at[pl.ds(1, n_dev - 1)], send_sem)
            sent.wait()
            o_ref[...] = got[...]

    fixed = lambda t: (0, 0)
    dtype = got_in.dtype
    return pl.pallas_call(
        kernel,
        out_shape=jax.ShapeDtypeStruct((n_dev, frames, run, width), dtype),
        grid=(n_tiles,),
        in_specs=[
            pl.BlockSpec(memory_space=pltpu.VMEM),
            pl.BlockSpec(memory_space=pltpu.VMEM),
            pl.BlockSpec((1, width), fixed),
            pl.BlockSpec((width, width), fixed),
            pl.BlockSpec((width, width), fixed),
            pl.BlockSpec((width, width), fixed),
            pl.BlockSpec((width, width), fixed),
        ],
        out_specs=pl.BlockSpec(memory_space=pltpu.VMEM),
        scratch_shapes=[
            pltpu.VMEM((frames, places, width), dtype),
            pltpu.VMEM((frames, width, places), dtype),
            pltpu.VMEM((frames, width, places), dtype),
            pltpu.VMEM((width, places), dtype),
            pltpu.VMEM((width, places), dtype),
            pltpu.VMEM((n_dev, frames, run, width), dtype),
            pltpu.VMEM((n_dev, frames, run, width), dtype),
            pltpu.SemaphoreType.DMA,
            pltpu.SemaphoreType.DMA,
        ],
        compiler_params=pltpu.CompilerParams(collective_id=cid, has_side_effects=True),
    )(got_in, zero, gain.reshape(1, width), wq, wk, wv, out_w)


def temporal_attend(x, gain, wq, wk, wv, out_w, n_frame, cid):
    every, run, width = x.shape
    depth = width // HEADS
    scale = depth ** (-0.5)
    frames = every // n_frame
    rows = every * run
    lanes = width // 128

    def kernel(x_ref, g_ref, wq_ref, wk_ref, wv_ref, w_ref, o_ref, xs, qs, ks, vs, made, got, send_sem, recv_sem):
        fi = lax.axis_index("frame")
        barrier = pltpu.get_barrier_semaphore()
        for k in range(1, n_frame):
            pl.semaphore_signal(barrier, inc=1, device_id={"frame": (fi + k) % n_frame}, device_id_type=MESH)

        wide = x_ref[...].astype(jnp.float32).reshape(rows, width)
        factor = lax.rsqrt(jnp.mean(wide * wide, axis=-1, keepdims=True) + 1e-06)
        normed_two = (wide * factor * g_ref[...]).astype(jnp.bfloat16)
        def keep(ref, values):
            for c in range(lanes):
                ref[c] = values[:, c * 128 : (c + 1) * 128]

        def gather(ref, p):
            place = pl.ds(p, every, stride=run)
            return jnp.concatenate([ref[c, place, :] for c in range(lanes)], axis=-1)

        keep(xs, wide)
        for ref, weight in ((qs, wq_ref), (ks, wk_ref), (vs, wv_ref)):
            projected = jnp.dot(normed_two, weight[...], preferred_element_type=jnp.float32)
            keep(ref, projected.astype(jnp.bfloat16).astype(jnp.float32))

        for p in range(run):
            q = gather(qs, p).astype(jnp.bfloat16)
            k = gather(ks, p).astype(jnp.bfloat16)
            v = gather(vs, p).astype(jnp.bfloat16)
            acc = gather(xs, p)
            for h in range(HEADS):
                part = slice(h * depth, (h + 1) * depth)
                contract = (((1,), (1,)), ((), ()))
                scores = lax.dot_general(q[:, part], k[:, part], contract, preferred_element_type=jnp.float32) * scale
                weights = jnp.exp(scores - jnp.max(scores, axis=-1, keepdims=True))
                totals = jnp.sum(weights, axis=-1, keepdims=True)
                summed = jnp.dot(weights.astype(jnp.bfloat16), v[:, part], preferred_element_type=jnp.float32)
                attended = (summed / totals).astype(jnp.bfloat16)
                acc = acc + jnp.dot(attended, w_ref[part, :], preferred_element_type=jnp.float32)
            made[p] = acc.astype(made.dtype)
            if p == 0:
                pl.semaphore_wait(barrier, n_frame - 1)
            for k in range(1, n_frame):
                g = (fi + k) % n_frame
                pltpu.make_async_remote_copy(
                    src_ref=made.at[p, pl.ds(pl.multiple_of(g * frames, frames), frames)],
                    dst_ref=got.at[fi, p],
                    send_sem=send_sem,
                    recv_sem=recv_sem,
                    device_id={"frame": g},
                    device_id_type=MESH,
                ).start()
            got[fi, p] = made[p, pl.ds(pl.multiple_of(fi * frames, frames), frames)]

        others = pltpu.make_async_copy(got.at[pl.ds(0, n_frame - 1)], got.at[pl.ds(1, n_frame - 1)], recv_sem)
        others.wait()
        sent = pltpu.make_async_copy(got.at[pl.ds(0, n_frame - 1)], got.at[pl.ds(1, n_frame - 1)], send_sem)
        sent.wait()
        o_ref[...] = got[...]

    vmem = pl.BlockSpec(memory_space=pltpu.VMEM)
    return pl.pallas_call(
        kernel,
        out_shape=jax.ShapeDtypeStruct((n_frame, run, frames, width), x.dtype),
        in_specs=[vmem] * 6,
        out_specs=vmem,
        scratch_shapes=[
            pltpu.VMEM((lanes, rows, 128), jnp.float32),
            pltpu.VMEM((lanes, rows, 128), jnp.float32),
            pltpu.VMEM((lanes, rows, 128), jnp.float32),
            pltpu.VMEM((lanes, rows, 128), jnp.float32),
            pltpu.VMEM((run, every, width), x.dtype),
            pltpu.VMEM((n_frame, run, frames, width), x.dtype),
            pltpu.SemaphoreType.DMA,
            pltpu.SemaphoreType.DMA,
        ],
        compiler_params=pltpu.CompilerParams(collective_id=cid, has_side_effects=True),
    )(x, gain.reshape(1, width), wq, wk, wv, out_w)


def transposed(values, weight):
    result = jnp.einsum("...rc,cd->...dr", values, weight, preferred_element_type=jnp.float32)
    return result.astype(jnp.bfloat16)


def normed(values, gain):
    wide = values.astype(jnp.float32)
    factor = lax.rsqrt(jnp.mean(wide * wide, axis=-1, keepdims=True) + 1e-06)
    return (wide * factor * gain).astype(jnp.bfloat16)


def project(values, weight):
    flat = values.reshape(-1, values.shape[-1])
    result = jnp.dot(flat, weight, preferred_element_type=jnp.float32).astype(jnp.bfloat16)
    return result.reshape(values.shape[:-1] + (weight.shape[1],))


def heads_of(values):
    return values.reshape(values.shape[:-1] + (HEADS, values.shape[-1] // HEADS))


def softmax_attend(query, keys, vals, score_form, value_form, total_form):
    scale = query.shape[-1] ** (-0.5)
    scores = jnp.einsum(score_form, query, keys, preferred_element_type=jnp.float32) * scale
    weights = jnp.exp(scores - jnp.max(scores, axis=-1, keepdims=True))
    totals = jnp.sum(weights, axis=-1)
    summed = jnp.einsum(
        value_form, weights.astype(jnp.bfloat16), vals, preferred_element_type=jnp.float32
    )
    return summed / jnp.einsum(total_form, totals)[..., None]


def shards(
    latents,
    gain_one,
    query_one,
    key_one,
    value_one,
    out_one,
    gain_two,
    query_two,
    key_two,
    value_two,
    out_two,
):
    frames, places, width = latents.shape
    n_pos = lax.axis_size("pos")
    n_frame = lax.axis_size("frame")
    per = frames // n_pos
    got, zero = spatial_exchange(latents.reshape(n_pos, per, places, width), n_pos, n_frame, 1)
    got = spatial_attend(
        got, zero, gain_one, query_one, key_one, value_one, out_one,
        min(512, n_pos * places), n_frame, n_pos, 2,
    )
    all_places = n_pos * places
    run = all_places // (n_pos * n_frame)
    mid_t = got.reshape(n_frame * n_pos * per, run, width)
    got = temporal_attend(mid_t, gain_two, query_two, key_two, value_two, out_two, n_frame, 3)
    return got.transpose(2, 0, 1, 3).reshape(frames, places, width)


def solution(mesh):
    return jax.shard_map(
        shards,
        mesh=mesh,
        in_specs=(P("frame", "pos", None), P(), P(), P(), P(), P(), P(), P(), P(), P(), P()),
        out_specs=P("frame", "pos", None),
        check_vma=False,
    )
```

```python
import jax
import jax.numpy as jnp
from jax import lax
from jax.experimental import pallas as pl
from jax.experimental.pallas import tpu as pltpu
from jax.sharding import PartitionSpec as P

HEADS = 4

MESH = pl.DeviceIdType.MESH


def exchange(x, names, sizes, cid):
    n = x.shape[0]

    def where(peer):
        if len(names) == 1:
            return {names[0]: peer}
        return {names[0]: peer // sizes[1], names[1]: peer % sizes[1]}

    def kernel(x_ref, o_ref, send_sem, recv_sem):
        me = lax.axis_index(names[0])
        if len(names) == 2:
            me = me * sizes[1] + lax.axis_index(names[1])
        barrier = pltpu.get_barrier_semaphore()
        for k in range(1, n):
            pl.semaphore_signal(barrier, inc=1, device_id=where((me + k) % n), device_id_type=MESH)
        pl.semaphore_wait(barrier, n - 1)
        copies = []
        for k in range(1, n):
            peer = (me + k) % n
            copy = pltpu.make_async_remote_copy(
                src_ref=x_ref.at[peer],
                dst_ref=o_ref.at[me],
                send_sem=send_sem.at[k],
                recv_sem=recv_sem.at[k],
                device_id=where(peer),
                device_id_type=MESH,
            )
            copy.start()
            copies.append(copy)
        o_ref[me] = x_ref[me]
        for copy in copies:
            copy.wait()

    return pl.pallas_call(
        kernel,
        out_shape=jax.ShapeDtypeStruct(x.shape, x.dtype),
        in_specs=[pl.BlockSpec(memory_space=pltpu.VMEM)],
        out_specs=pl.BlockSpec(memory_space=pltpu.VMEM),
        scratch_shapes=[pltpu.SemaphoreType.DMA((n,)), pltpu.SemaphoreType.DMA((n,))],
        compiler_params=pltpu.CompilerParams(collective_id=cid, has_side_effects=True),
    )(x)


def spatial_exchange(x, n_pos, n_frame, cid):
    _, per, places, width = x.shape

    def kernel(x_ref, o_ref, z_ref, send_sem, recv_sem, fsend_sem, frecv_sem, zsend_sem, zrecv_sem, local_sem):
        fi = lax.axis_index("frame")
        pi = lax.axis_index("pos")
        barrier = pltpu.get_barrier_semaphore()
        for k in range(1, n_pos):
            pl.semaphore_signal(barrier, inc=1, device_id={"pos": (pi + k) % n_pos}, device_id_type=MESH)
        for g in range(1, n_frame):
            pl.semaphore_signal(barrier, inc=1, device_id={"frame": (fi + g) % n_frame}, device_id_type=MESH)
        pl.semaphore_wait(barrier, n_pos - 1 + n_frame - 1)
        def spread(g):
            return pltpu.make_async_remote_copy(
                src_ref=x_ref.at[0, 0],
                dst_ref=z_ref.at[pi],
                send_sem=fsend_sem.at[g],
                recv_sem=frecv_sem,
                device_id={"frame": g},
                device_id_type=MESH,
            )

        @pl.when(fi == 0)
        def _():
            for g in range(1, n_frame):
                spread(g).start()

        copies = []
        for k in range(1, n_pos):
            peer = (pi + k) % n_pos
            copy = pltpu.make_async_remote_copy(
                src_ref=x_ref.at[peer],
                dst_ref=o_ref.at[pi],
                send_sem=send_sem.at[k],
                recv_sem=recv_sem.at[k],
                device_id={"pos": peer},
                device_id_type=MESH,
            )
            copy.start()
            copies.append(copy)

        @pl.when(fi == 0)
        def _():
            local = pltpu.make_async_copy(x_ref.at[0, 0], z_ref.at[pi], local_sem)
            local.start()
            local.wait()

        @pl.when(fi != 0)
        def _():
            spread(1).wait_recv()

        for k in range(1, n_pos):
            peer = (pi + k) % n_pos
            copy = pltpu.make_async_remote_copy(
                src_ref=z_ref.at[pi],
                dst_ref=z_ref.at[pi],
                send_sem=zsend_sem.at[k],
                recv_sem=zrecv_sem.at[k],
                device_id={"pos": peer},
                device_id_type=MESH,
            )
            copy.start()
            copies.append(copy)

        @pl.when(fi == 0)
        def _():
            for g in range(1, n_frame):
                spread(g).wait_send()

        for copy in copies:
            copy.wait()
        o_ref[pi] = x_ref[pi]

    return pl.pallas_call(
        kernel,
        out_shape=(
            jax.ShapeDtypeStruct(x.shape, x.dtype),
            jax.ShapeDtypeStruct((n_pos, places, width), x.dtype),
        ),
        in_specs=[pl.BlockSpec(memory_space=pltpu.VMEM)],
        out_specs=(pl.BlockSpec(memory_space=pltpu.VMEM), pl.BlockSpec(memory_space=pltpu.VMEM)),
        scratch_shapes=[
            pltpu.SemaphoreType.DMA((n_pos,)),
            pltpu.SemaphoreType.DMA((n_pos,)),
            pltpu.SemaphoreType.DMA((n_frame,)),
            pltpu.SemaphoreType.DMA,
            pltpu.SemaphoreType.DMA((n_pos,)),
            pltpu.SemaphoreType.DMA((n_pos,)),
            pltpu.SemaphoreType.DMA,
        ],
        compiler_params=pltpu.CompilerParams(collective_id=cid, has_side_effects=True),
    )(x)


def spatial_attend(got_in, zero, gain, wq, wk, wv, out_w, rows, n_frame, n_pos, cid):
    _, frames, slab, width = got_in.shape
    places = n_pos * slab
    depth = width // HEADS
    scale = depth ** (-0.5)
    n_dev = n_frame * n_pos
    run = places // n_dev
    chunks = rows // run
    n_tiles = places // rows
    per_tile = rows // slab

    def kernel(x_ref, z_ref, g_ref, wq_ref, wkt_ref, wvt_ref, w_ref, o_ref,
               q_ref, kt_ref, vt_ref, made, got, send_sem, recv_sem):
        t = pl.program_id(0)
        fi = lax.axis_index("frame")
        pi = lax.axis_index("pos")
        me = fi * n_pos + pi
        barrier = pltpu.get_barrier_semaphore()
        contract = (((1,), (1,)), ((), ()))

        def normed_rows(values):
            wide = values.reshape(places, width).astype(jnp.float32)
            factor = lax.rsqrt(jnp.mean(wide * wide, axis=-1, keepdims=True) + 1e-06)
            return (wide * factor * g_ref[...]).astype(jnp.bfloat16)

        def channels_first(weight_t, values):
            return lax.dot_general(weight_t, values, contract, preferred_element_type=jnp.float32).astype(jnp.bfloat16)

        @pl.when(t == 0)
        def _():
            for k in range(1, n_dev):
                peer = (me + k) % n_dev
                pl.semaphore_signal(
                    barrier, inc=1, device_id={"frame": peer // n_pos, "pos": peer % n_pos}, device_id_type=MESH
                )
            wkt = wkt_ref[...].T
            wvt = wvt_ref[...].T
            normed_zero = normed_rows(z_ref[...])
            k_zero = channels_first(wkt, normed_zero)
            v_zero = channels_first(wvt, normed_zero)
            for f in range(frames):
                normed_one = normed_rows(x_ref[:, f])
                q_ref[f] = jnp.dot(normed_one, wq_ref[...], preferred_element_type=jnp.float32).astype(jnp.bfloat16)
                kt_ref[f, :, pl.ds(0, places)] = channels_first(wkt, normed_one)
                vt_ref[f, :, pl.ds(0, places)] = channels_first(wvt, normed_one)
                kt_ref[f, :, pl.ds(places, places)] = k_zero
                vt_ref[f, :, pl.ds(places, places)] = v_zero

        tt = (t + fi + pi) % n_tiles
        base = tt * chunks
        these = pl.ds(pl.multiple_of(tt * rows, rows), rows)
        for f in range(frames):
            acc = x_ref[pl.ds(tt * per_tile, per_tile), f].reshape(rows, width).astype(jnp.float32)
            for h in range(HEADS):
                part = pl.ds(h * depth, depth)
                qh = q_ref[f, these, part]
                scores = jnp.dot(qh, kt_ref[f, part, :], preferred_element_type=jnp.float32) * scale
                weights = jnp.exp(scores - jnp.max(scores, axis=-1, keepdims=True))
                totals = jnp.sum(weights, axis=-1, keepdims=True)
                summed = lax.dot_general(
                    weights.astype(jnp.bfloat16), vt_ref[f, part, :], contract, preferred_element_type=jnp.float32
                )
                attended = (summed / totals).astype(jnp.bfloat16)
                acc = acc + jnp.dot(attended, w_ref[part, :], preferred_element_type=jnp.float32)
            made[pl.ds(base, chunks), f] = acc.reshape(chunks, run, width).astype(made.dtype)

        @pl.when(t == 0)
        def _():
            pl.semaphore_wait(barrier, n_dev - 1)

        for i in range(chunks):
            gf = i % n_frame
            gp = (base + i) // n_frame

            @pl.when((gf == fi) & (gp == pi))
            def _():
                got[me] = made[base + i]

            @pl.when((gf != fi) | (gp != pi))
            def _():
                pltpu.make_async_remote_copy(
                    src_ref=made.at[base + i],
                    dst_ref=got.at[me],
                    send_sem=send_sem,
                    recv_sem=recv_sem,
                    device_id={"frame": gf, "pos": gp},
                    device_id_type=MESH,
                ).start()

        @pl.when(t == n_tiles - 1)
        def _():
            others = pltpu.make_async_copy(got.at[pl.ds(0, n_dev - 1)], got.at[pl.ds(1, n_dev - 1)], recv_sem)
            others.wait()
            sent = pltpu.make_async_copy(got.at[pl.ds(0, n_dev - 1)], got.at[pl.ds(1, n_dev - 1)], send_sem)
            sent.wait()
            o_ref[...] = got[...]

    fixed = lambda t: (0, 0)
    dtype = got_in.dtype
    return pl.pallas_call(
        kernel,
        out_shape=jax.ShapeDtypeStruct((n_dev, frames, run, width), dtype),
        grid=(n_tiles,),
        in_specs=[
            pl.BlockSpec(memory_space=pltpu.VMEM),
            pl.BlockSpec(memory_space=pltpu.VMEM),
            pl.BlockSpec((1, width), fixed),
            pl.BlockSpec((width, width), fixed),
            pl.BlockSpec((width, width), fixed),
            pl.BlockSpec((width, width), fixed),
            pl.BlockSpec((width, width), fixed),
        ],
        out_specs=pl.BlockSpec(memory_space=pltpu.VMEM),
        scratch_shapes=[
            pltpu.VMEM((frames, places, width), dtype),
            pltpu.VMEM((frames, width, 2 * places), dtype),
            pltpu.VMEM((frames, width, 2 * places), dtype),
            pltpu.VMEM((n_dev, frames, run, width), dtype),
            pltpu.VMEM((n_dev, frames, run, width), dtype),
            pltpu.SemaphoreType.DMA,
            pltpu.SemaphoreType.DMA,
        ],
        compiler_params=pltpu.CompilerParams(collective_id=cid, has_side_effects=True),
    )(got_in, zero, gain.reshape(1, width), wq, wk, wv, out_w)


def temporal_attend(x, gain, wq, wk, wv, out_w, n_frame, cid):
    every, run, width = x.shape
    depth = width // HEADS
    scale = depth ** (-0.5)
    frames = every // n_frame
    rows = every * run
    lanes = width // 128

    def kernel(x_ref, g_ref, wq_ref, wk_ref, wv_ref, w_ref, o_ref, xs, qs, ks, vs, made, got, send_sem, recv_sem):
        fi = lax.axis_index("frame")
        barrier = pltpu.get_barrier_semaphore()
        for k in range(1, n_frame):
            pl.semaphore_signal(barrier, inc=1, device_id={"frame": (fi + k) % n_frame}, device_id_type=MESH)

        wide = x_ref[...].astype(jnp.float32).reshape(rows, width)
        factor = lax.rsqrt(jnp.mean(wide * wide, axis=-1, keepdims=True) + 1e-06)
        normed_two = (wide * factor * g_ref[...]).astype(jnp.bfloat16)
        def keep(ref, values):
            for c in range(lanes):
                ref[c] = values[:, c * 128 : (c + 1) * 128]

        def gather(ref, p):
            place = pl.ds(p, every, stride=run)
            return jnp.concatenate([ref[c, place, :] for c in range(lanes)], axis=-1)

        keep(xs, wide)
        for ref, weight in ((qs, wq_ref), (ks, wk_ref), (vs, wv_ref)):
            projected = jnp.dot(normed_two, weight[...], preferred_element_type=jnp.float32)
            keep(ref, projected.astype(jnp.bfloat16).astype(jnp.float32))

        for p in range(run):
            q = gather(qs, p).astype(jnp.bfloat16)
            k = gather(ks, p).astype(jnp.bfloat16)
            v = gather(vs, p).astype(jnp.bfloat16)
            acc = gather(xs, p)
            for h in range(HEADS):
                part = slice(h * depth, (h + 1) * depth)
                contract = (((1,), (1,)), ((), ()))
                scores = lax.dot_general(q[:, part], k[:, part], contract, preferred_element_type=jnp.float32) * scale
                weights = jnp.exp(scores - jnp.max(scores, axis=-1, keepdims=True))
                totals = jnp.sum(weights, axis=-1, keepdims=True)
                summed = jnp.dot(weights.astype(jnp.bfloat16), v[:, part], preferred_element_type=jnp.float32)
                attended = (summed / totals).astype(jnp.bfloat16)
                acc = acc + jnp.dot(attended, w_ref[part, :], preferred_element_type=jnp.float32)
            made[p] = acc.astype(made.dtype)
            if p == 0:
                pl.semaphore_wait(barrier, n_frame - 1)
            for g in range(n_frame):
                @pl.when(g == fi)
                def _():
                    got[fi, p] = made[p, pl.ds(g * frames, frames)]

                @pl.when(g != fi)
                def _():
                    pltpu.make_async_remote_copy(
                        src_ref=made.at[p, pl.ds(g * frames, frames)],
                        dst_ref=got.at[fi, p],
                        send_sem=send_sem,
                        recv_sem=recv_sem,
                        device_id={"frame": g},
                        device_id_type=MESH,
                    ).start()

        others = pltpu.make_async_copy(got.at[pl.ds(0, n_frame - 1)], got.at[pl.ds(1, n_frame - 1)], recv_sem)
        others.wait()
        sent = pltpu.make_async_copy(got.at[pl.ds(0, n_frame - 1)], got.at[pl.ds(1, n_frame - 1)], send_sem)
        sent.wait()
        o_ref[...] = got[...]

    vmem = pl.BlockSpec(memory_space=pltpu.VMEM)
    return pl.pallas_call(
        kernel,
        out_shape=jax.ShapeDtypeStruct((n_frame, run, frames, width), x.dtype),
        in_specs=[vmem] * 6,
        out_specs=vmem,
        scratch_shapes=[
            pltpu.VMEM((lanes, rows, 128), jnp.float32),
            pltpu.VMEM((lanes, rows, 128), jnp.float32),
            pltpu.VMEM((lanes, rows, 128), jnp.float32),
            pltpu.VMEM((lanes, rows, 128), jnp.float32),
            pltpu.VMEM((run, every, width), x.dtype),
            pltpu.VMEM((n_frame, run, frames, width), x.dtype),
            pltpu.SemaphoreType.DMA,
            pltpu.SemaphoreType.DMA,
        ],
        compiler_params=pltpu.CompilerParams(collective_id=cid, has_side_effects=True),
    )(x, gain.reshape(1, width), wq, wk, wv, out_w)


def transposed(values, weight):
    result = jnp.einsum("...rc,cd->...dr", values, weight, preferred_element_type=jnp.float32)
    return result.astype(jnp.bfloat16)


def normed(values, gain):
    wide = values.astype(jnp.float32)
    factor = lax.rsqrt(jnp.mean(wide * wide, axis=-1, keepdims=True) + 1e-06)
    return (wide * factor * gain).astype(jnp.bfloat16)


def project(values, weight):
    flat = values.reshape(-1, values.shape[-1])
    result = jnp.dot(flat, weight, preferred_element_type=jnp.float32).astype(jnp.bfloat16)
    return result.reshape(values.shape[:-1] + (weight.shape[1],))


def heads_of(values):
    return values.reshape(values.shape[:-1] + (HEADS, values.shape[-1] // HEADS))


def softmax_attend(query, keys, vals, score_form, value_form, total_form):
    scale = query.shape[-1] ** (-0.5)
    scores = jnp.einsum(score_form, query, keys, preferred_element_type=jnp.float32) * scale
    weights = jnp.exp(scores - jnp.max(scores, axis=-1, keepdims=True))
    totals = jnp.sum(weights, axis=-1)
    summed = jnp.einsum(
        value_form, weights.astype(jnp.bfloat16), vals, preferred_element_type=jnp.float32
    )
    return summed / jnp.einsum(total_form, totals)[..., None]


def shards(
    latents,
    gain_one,
    query_one,
    key_one,
    value_one,
    out_one,
    gain_two,
    query_two,
    key_two,
    value_two,
    out_two,
):
    frames, places, width = latents.shape
    n_pos = lax.axis_size("pos")
    n_frame = lax.axis_size("frame")
    per = frames // n_pos
    got, zero = spatial_exchange(latents.reshape(n_pos, per, places, width), n_pos, n_frame, 1)
    got = spatial_attend(
        got, zero, gain_one, query_one, key_one, value_one, out_one,
        min(512, n_pos * places), n_frame, n_pos, 2,
    )
    all_places = n_pos * places
    run = all_places // (n_pos * n_frame)
    mid_t = got.reshape(n_frame * n_pos * per, run, width)
    got = temporal_attend(mid_t, gain_two, query_two, key_two, value_two, out_two, n_frame, 3)
    return got.transpose(2, 0, 1, 3).reshape(frames, places, width)


def solution(mesh):
    return jax.shard_map(
        shards,
        mesh=mesh,
        in_specs=(P("frame", "pos", None), P(), P(), P(), P(), P(), P(), P(), P(), P(), P()),
        out_specs=P("frame", "pos", None),
        check_vma=False,
    )
```

```python
import jax
import jax.numpy as jnp
from jax import lax
from jax.experimental import pallas as pl
from jax.experimental.pallas import tpu as pltpu
from jax.sharding import PartitionSpec as P

HEADS = 4

MESH = pl.DeviceIdType.MESH


def exchange(x, names, sizes, cid):
    n = x.shape[0]

    def where(peer):
        if len(names) == 1:
            return {names[0]: peer}
        return {names[0]: peer // sizes[1], names[1]: peer % sizes[1]}

    def kernel(x_ref, o_ref, send_sem, recv_sem):
        me = lax.axis_index(names[0])
        if len(names) == 2:
            me = me * sizes[1] + lax.axis_index(names[1])
        barrier = pltpu.get_barrier_semaphore()
        for k in range(1, n):
            pl.semaphore_signal(barrier, inc=1, device_id=where((me + k) % n), device_id_type=MESH)
        pl.semaphore_wait(barrier, n - 1)
        copies = []
        for k in range(1, n):
            peer = (me + k) % n
            copy = pltpu.make_async_remote_copy(
                src_ref=x_ref.at[peer],
                dst_ref=o_ref.at[me],
                send_sem=send_sem.at[k],
                recv_sem=recv_sem.at[k],
                device_id=where(peer),
                device_id_type=MESH,
            )
            copy.start()
            copies.append(copy)
        o_ref[me] = x_ref[me]
        for copy in copies:
            copy.wait()

    return pl.pallas_call(
        kernel,
        out_shape=jax.ShapeDtypeStruct(x.shape, x.dtype),
        in_specs=[pl.BlockSpec(memory_space=pltpu.VMEM)],
        out_specs=pl.BlockSpec(memory_space=pltpu.VMEM),
        scratch_shapes=[pltpu.SemaphoreType.DMA((n,)), pltpu.SemaphoreType.DMA((n,))],
        compiler_params=pltpu.CompilerParams(collective_id=cid, has_side_effects=True),
    )(x)


def spatial_exchange(x, n_pos, n_frame, cid):
    _, per, places, width = x.shape

    def kernel(x_ref, o_ref, z_ref, send_sem, recv_sem, fsend_sem, frecv_sem, zsend_sem, zrecv_sem, local_sem):
        fi = lax.axis_index("frame")
        pi = lax.axis_index("pos")
        barrier = pltpu.get_barrier_semaphore()
        for k in range(1, n_pos):
            pl.semaphore_signal(barrier, inc=1, device_id={"pos": (pi + k) % n_pos}, device_id_type=MESH)
        for g in range(1, n_frame):
            pl.semaphore_signal(barrier, inc=1, device_id={"frame": (fi + g) % n_frame}, device_id_type=MESH)
        pl.semaphore_wait(barrier, n_pos - 1 + n_frame - 1)
        def spread(g):
            return pltpu.make_async_remote_copy(
                src_ref=x_ref.at[0, 0],
                dst_ref=z_ref.at[pi],
                send_sem=fsend_sem.at[g],
                recv_sem=frecv_sem,
                device_id={"frame": g},
                device_id_type=MESH,
            )

        def forward(k):
            return pltpu.make_async_remote_copy(
                src_ref=z_ref.at[pi],
                dst_ref=z_ref.at[pi],
                send_sem=zsend_sem.at[k],
                recv_sem=zrecv_sem.at[k],
                device_id={"pos": (pi + k) % n_pos},
                device_id_type=MESH,
            )

        @pl.when(fi == 0)
        def _():
            for g in range(1, n_frame):
                spread(g).start()
            local = pltpu.make_async_copy(x_ref.at[0, 0], z_ref.at[pi], local_sem)
            local.start()
            local.wait()
            for k in range(1, n_pos):
                forward(k).start()

        copies = []
        for k in range(1, n_pos):
            peer = (pi + k) % n_pos
            copy = pltpu.make_async_remote_copy(
                src_ref=x_ref.at[peer],
                dst_ref=o_ref.at[pi],
                send_sem=send_sem.at[k],
                recv_sem=recv_sem.at[k],
                device_id={"pos": peer},
                device_id_type=MESH,
            )
            copy.start()
            copies.append(copy)

        @pl.when(fi != 0)
        def _():
            spread(1).wait_recv()
            for k in range(1, n_pos):
                forward(k).start()

        copies += [forward(k) for k in range(1, n_pos)]

        @pl.when(fi == 0)
        def _():
            for g in range(1, n_frame):
                spread(g).wait_send()

        for copy in copies:
            copy.wait()
        o_ref[pi] = x_ref[pi]

    return pl.pallas_call(
        kernel,
        out_shape=(
            jax.ShapeDtypeStruct(x.shape, x.dtype),
            jax.ShapeDtypeStruct((n_pos, places, width), x.dtype),
        ),
        in_specs=[pl.BlockSpec(memory_space=pltpu.VMEM)],
        out_specs=(pl.BlockSpec(memory_space=pltpu.VMEM), pl.BlockSpec(memory_space=pltpu.VMEM)),
        scratch_shapes=[
            pltpu.SemaphoreType.DMA((n_pos,)),
            pltpu.SemaphoreType.DMA((n_pos,)),
            pltpu.SemaphoreType.DMA((n_frame,)),
            pltpu.SemaphoreType.DMA,
            pltpu.SemaphoreType.DMA((n_pos,)),
            pltpu.SemaphoreType.DMA((n_pos,)),
            pltpu.SemaphoreType.DMA,
        ],
        compiler_params=pltpu.CompilerParams(collective_id=cid, has_side_effects=True),
    )(x)


def spatial_attend(got_in, zero, gain, wq, wk, wv, out_w, rows, n_frame, n_pos, cid):
    _, frames, slab, width = got_in.shape
    places = n_pos * slab
    depth = width // HEADS
    scale = depth ** (-0.5)
    n_dev = n_frame * n_pos
    run = places // n_dev
    chunks = rows // run
    n_tiles = places // rows
    per_tile = rows // slab

    def kernel(x_ref, z_ref, g_ref, wq_ref, wkt_ref, wvt_ref, w_ref, o_ref,
               q_ref, kt_ref, vt_ref, made, got, send_sem, recv_sem):
        t = pl.program_id(0)
        fi = lax.axis_index("frame")
        pi = lax.axis_index("pos")
        me = fi * n_pos + pi
        barrier = pltpu.get_barrier_semaphore()
        contract = (((1,), (1,)), ((), ()))

        def normed_rows(values):
            wide = values.reshape(places, width).astype(jnp.float32)
            factor = lax.rsqrt(jnp.mean(wide * wide, axis=-1, keepdims=True) + 1e-06)
            return (wide * factor * g_ref[...]).astype(jnp.bfloat16)

        def channels_first(weight_t, values):
            return lax.dot_general(weight_t, values, contract, preferred_element_type=jnp.float32).astype(jnp.bfloat16)

        @pl.when(t == 0)
        def _():
            for k in range(1, n_dev):
                peer = (me + k) % n_dev
                pl.semaphore_signal(
                    barrier, inc=1, device_id={"frame": peer // n_pos, "pos": peer % n_pos}, device_id_type=MESH
                )
            wkt = wkt_ref[...].T
            wvt = wvt_ref[...].T
            normed_zero = normed_rows(z_ref[...])
            k_zero = channels_first(wkt, normed_zero)
            v_zero = channels_first(wvt, normed_zero)
            for f in range(frames):
                normed_one = normed_rows(x_ref[:, f])
                q_ref[f] = jnp.dot(normed_one, wq_ref[...], preferred_element_type=jnp.float32).astype(jnp.bfloat16)
                kt_ref[f, :, pl.ds(0, places)] = channels_first(wkt, normed_one)
                vt_ref[f, :, pl.ds(0, places)] = channels_first(wvt, normed_one)
                kt_ref[f, :, pl.ds(places, places)] = k_zero
                vt_ref[f, :, pl.ds(places, places)] = v_zero

        tt = (t + fi + pi) % n_tiles
        base = tt * chunks
        these = pl.ds(pl.multiple_of(tt * rows, rows), rows)
        for f in range(frames):
            acc = x_ref[pl.ds(tt * per_tile, per_tile), f].reshape(rows, width).astype(jnp.float32)
            for h in range(HEADS):
                part = pl.ds(h * depth, depth)
                qh = q_ref[f, these, part]
                scores = jnp.dot(qh, kt_ref[f, part, :], preferred_element_type=jnp.float32) * scale
                weights = jnp.exp(scores - jnp.max(scores, axis=-1, keepdims=True))
                totals = jnp.sum(weights, axis=-1, keepdims=True)
                summed = lax.dot_general(
                    weights.astype(jnp.bfloat16), vt_ref[f, part, :], contract, preferred_element_type=jnp.float32
                )
                attended = (summed / totals).astype(jnp.bfloat16)
                acc = acc + jnp.dot(attended, w_ref[part, :], preferred_element_type=jnp.float32)
            made[pl.ds(base, chunks), f] = acc.reshape(chunks, run, width).astype(made.dtype)

        @pl.when(t == 0)
        def _():
            pl.semaphore_wait(barrier, n_dev - 1)

        for i in range(chunks):
            gf = i % n_frame
            gp = (base + i) // n_frame

            @pl.when((gf == fi) & (gp == pi))
            def _():
                got[me] = made[base + i]

            @pl.when((gf != fi) | (gp != pi))
            def _():
                pltpu.make_async_remote_copy(
                    src_ref=made.at[base + i],
                    dst_ref=got.at[me],
                    send_sem=send_sem,
                    recv_sem=recv_sem,
                    device_id={"frame": gf, "pos": gp},
                    device_id_type=MESH,
                ).start()

        @pl.when(t == n_tiles - 1)
        def _():
            others = pltpu.make_async_copy(got.at[pl.ds(0, n_dev - 1)], got.at[pl.ds(1, n_dev - 1)], recv_sem)
            others.wait()
            sent = pltpu.make_async_copy(got.at[pl.ds(0, n_dev - 1)], got.at[pl.ds(1, n_dev - 1)], send_sem)
            sent.wait()
            o_ref[...] = got[...]

    fixed = lambda t: (0, 0)
    dtype = got_in.dtype
    return pl.pallas_call(
        kernel,
        out_shape=jax.ShapeDtypeStruct((n_dev, frames, run, width), dtype),
        grid=(n_tiles,),
        in_specs=[
            pl.BlockSpec(memory_space=pltpu.VMEM),
            pl.BlockSpec(memory_space=pltpu.VMEM),
            pl.BlockSpec((1, width), fixed),
            pl.BlockSpec((width, width), fixed),
            pl.BlockSpec((width, width), fixed),
            pl.BlockSpec((width, width), fixed),
            pl.BlockSpec((width, width), fixed),
        ],
        out_specs=pl.BlockSpec(memory_space=pltpu.VMEM),
        scratch_shapes=[
            pltpu.VMEM((frames, places, width), dtype),
            pltpu.VMEM((frames, width, 2 * places), dtype),
            pltpu.VMEM((frames, width, 2 * places), dtype),
            pltpu.VMEM((n_dev, frames, run, width), dtype),
            pltpu.VMEM((n_dev, frames, run, width), dtype),
            pltpu.SemaphoreType.DMA,
            pltpu.SemaphoreType.DMA,
        ],
        compiler_params=pltpu.CompilerParams(collective_id=cid, has_side_effects=True),
    )(got_in, zero, gain.reshape(1, width), wq, wk, wv, out_w)


def temporal_attend(x, gain, wq, wk, wv, out_w, n_frame, cid):
    every, run, width = x.shape
    depth = width // HEADS
    scale = depth ** (-0.5)
    frames = every // n_frame
    rows = every * run
    lanes = width // 128

    def kernel(x_ref, g_ref, wq_ref, wk_ref, wv_ref, w_ref, o_ref, xs, qs, ks, vs, made, got, send_sem, recv_sem):
        fi = lax.axis_index("frame")
        barrier = pltpu.get_barrier_semaphore()
        for k in range(1, n_frame):
            pl.semaphore_signal(barrier, inc=1, device_id={"frame": (fi + k) % n_frame}, device_id_type=MESH)

        wide = x_ref[...].astype(jnp.float32).reshape(rows, width)
        factor = lax.rsqrt(jnp.mean(wide * wide, axis=-1, keepdims=True) + 1e-06)
        normed_two = (wide * factor * g_ref[...]).astype(jnp.bfloat16)
        def keep(ref, values):
            for c in range(lanes):
                ref[c] = values[:, c * 128 : (c + 1) * 128]

        def gather(ref, p):
            place = pl.ds(p, every, stride=run)
            return jnp.concatenate([ref[c, place, :] for c in range(lanes)], axis=-1)

        keep(xs, wide)
        for ref, weight in ((qs, wq_ref), (ks, wk_ref), (vs, wv_ref)):
            projected = jnp.dot(normed_two, weight[...], preferred_element_type=jnp.float32)
            keep(ref, projected.astype(jnp.bfloat16).astype(jnp.float32))

        for p in range(run):
            q = gather(qs, p).astype(jnp.bfloat16)
            k = gather(ks, p).astype(jnp.bfloat16)
            v = gather(vs, p).astype(jnp.bfloat16)
            acc = gather(xs, p)
            for h in range(HEADS):
                part = slice(h * depth, (h + 1) * depth)
                contract = (((1,), (1,)), ((), ()))
                scores = lax.dot_general(q[:, part], k[:, part], contract, preferred_element_type=jnp.float32) * scale
                weights = jnp.exp(scores - jnp.max(scores, axis=-1, keepdims=True))
                totals = jnp.sum(weights, axis=-1, keepdims=True)
                summed = jnp.dot(weights.astype(jnp.bfloat16), v[:, part], preferred_element_type=jnp.float32)
                attended = (summed / totals).astype(jnp.bfloat16)
                acc = acc + jnp.dot(attended, w_ref[part, :], preferred_element_type=jnp.float32)
            made[p] = acc.astype(made.dtype)
            if p == 0:
                pl.semaphore_wait(barrier, n_frame - 1)
            for g in range(n_frame):
                @pl.when(g == fi)
                def _():
                    got[fi, p] = made[p, pl.ds(g * frames, frames)]

                @pl.when(g != fi)
                def _():
                    pltpu.make_async_remote_copy(
                        src_ref=made.at[p, pl.ds(g * frames, frames)],
                        dst_ref=got.at[fi, p],
                        send_sem=send_sem,
                        recv_sem=recv_sem,
                        device_id={"frame": g},
                        device_id_type=MESH,
                    ).start()

        others = pltpu.make_async_copy(got.at[pl.ds(0, n_frame - 1)], got.at[pl.ds(1, n_frame - 1)], recv_sem)
        others.wait()
        sent = pltpu.make_async_copy(got.at[pl.ds(0, n_frame - 1)], got.at[pl.ds(1, n_frame - 1)], send_sem)
        sent.wait()
        o_ref[...] = got[...]

    vmem = pl.BlockSpec(memory_space=pltpu.VMEM)
    return pl.pallas_call(
        kernel,
        out_shape=jax.ShapeDtypeStruct((n_frame, run, frames, width), x.dtype),
        in_specs=[vmem] * 6,
        out_specs=vmem,
        scratch_shapes=[
            pltpu.VMEM((lanes, rows, 128), jnp.float32),
            pltpu.VMEM((lanes, rows, 128), jnp.float32),
            pltpu.VMEM((lanes, rows, 128), jnp.float32),
            pltpu.VMEM((lanes, rows, 128), jnp.float32),
            pltpu.VMEM((run, every, width), x.dtype),
            pltpu.VMEM((n_frame, run, frames, width), x.dtype),
            pltpu.SemaphoreType.DMA,
            pltpu.SemaphoreType.DMA,
        ],
        compiler_params=pltpu.CompilerParams(collective_id=cid, has_side_effects=True),
    )(x, gain.reshape(1, width), wq, wk, wv, out_w)


def transposed(values, weight):
    result = jnp.einsum("...rc,cd->...dr", values, weight, preferred_element_type=jnp.float32)
    return result.astype(jnp.bfloat16)


def normed(values, gain):
    wide = values.astype(jnp.float32)
    factor = lax.rsqrt(jnp.mean(wide * wide, axis=-1, keepdims=True) + 1e-06)
    return (wide * factor * gain).astype(jnp.bfloat16)


def project(values, weight):
    flat = values.reshape(-1, values.shape[-1])
    result = jnp.dot(flat, weight, preferred_element_type=jnp.float32).astype(jnp.bfloat16)
    return result.reshape(values.shape[:-1] + (weight.shape[1],))


def heads_of(values):
    return values.reshape(values.shape[:-1] + (HEADS, values.shape[-1] // HEADS))


def softmax_attend(query, keys, vals, score_form, value_form, total_form):
    scale = query.shape[-1] ** (-0.5)
    scores = jnp.einsum(score_form, query, keys, preferred_element_type=jnp.float32) * scale
    weights = jnp.exp(scores - jnp.max(scores, axis=-1, keepdims=True))
    totals = jnp.sum(weights, axis=-1)
    summed = jnp.einsum(
        value_form, weights.astype(jnp.bfloat16), vals, preferred_element_type=jnp.float32
    )
    return summed / jnp.einsum(total_form, totals)[..., None]


def shards(
    latents,
    gain_one,
    query_one,
    key_one,
    value_one,
    out_one,
    gain_two,
    query_two,
    key_two,
    value_two,
    out_two,
):
    frames, places, width = latents.shape
    n_pos = lax.axis_size("pos")
    n_frame = lax.axis_size("frame")
    per = frames // n_pos
    got, zero = spatial_exchange(latents.reshape(n_pos, per, places, width), n_pos, n_frame, 1)
    got = spatial_attend(
        got, zero, gain_one, query_one, key_one, value_one, out_one,
        min(512, n_pos * places), n_frame, n_pos, 2,
    )
    all_places = n_pos * places
    run = all_places // (n_pos * n_frame)
    mid_t = got.reshape(n_frame * n_pos * per, run, width)
    got = temporal_attend(mid_t, gain_two, query_two, key_two, value_two, out_two, n_frame, 3)
    return got.transpose(2, 0, 1, 3).reshape(frames, places, width)


def solution(mesh):
    return jax.shard_map(
        shards,
        mesh=mesh,
        in_specs=(P("frame", "pos", None), P(), P(), P(), P(), P(), P(), P(), P(), P(), P()),
        out_specs=P("frame", "pos", None),
        check_vma=False,
    )
```

```python
import jax
import jax.numpy as jnp
from jax import lax
from jax.experimental import pallas as pl
from jax.experimental.pallas import tpu as pltpu
from jax.sharding import PartitionSpec as P

HEADS = 4

MESH = pl.DeviceIdType.MESH


def exchange(x, names, sizes, cid):
    n = x.shape[0]

    def where(peer):
        if len(names) == 1:
            return {names[0]: peer}
        return {names[0]: peer // sizes[1], names[1]: peer % sizes[1]}

    def kernel(x_ref, o_ref, send_sem, recv_sem):
        me = lax.axis_index(names[0])
        if len(names) == 2:
            me = me * sizes[1] + lax.axis_index(names[1])
        barrier = pltpu.get_barrier_semaphore()
        for k in range(1, n):
            pl.semaphore_signal(barrier, inc=1, device_id=where((me + k) % n), device_id_type=MESH)
        pl.semaphore_wait(barrier, n - 1)
        copies = []
        for k in range(1, n):
            peer = (me + k) % n
            copy = pltpu.make_async_remote_copy(
                src_ref=x_ref.at[peer],
                dst_ref=o_ref.at[me],
                send_sem=send_sem.at[k],
                recv_sem=recv_sem.at[k],
                device_id=where(peer),
                device_id_type=MESH,
            )
            copy.start()
            copies.append(copy)
        o_ref[me] = x_ref[me]
        for copy in copies:
            copy.wait()

    return pl.pallas_call(
        kernel,
        out_shape=jax.ShapeDtypeStruct(x.shape, x.dtype),
        in_specs=[pl.BlockSpec(memory_space=pltpu.VMEM)],
        out_specs=pl.BlockSpec(memory_space=pltpu.VMEM),
        scratch_shapes=[pltpu.SemaphoreType.DMA((n,)), pltpu.SemaphoreType.DMA((n,))],
        compiler_params=pltpu.CompilerParams(collective_id=cid, has_side_effects=True),
    )(x)


def spatial_exchange(x, n_pos, n_frame, cid):
    _, per, places, width = x.shape

    def kernel(x_ref, o_ref, z_ref, send_sem, recv_sem, fsend_sem, frecv_sem, zsend_sem, zrecv_sem, local_sem):
        fi = lax.axis_index("frame")
        pi = lax.axis_index("pos")
        barrier = pltpu.get_barrier_semaphore()
        for k in range(1, n_pos):
            pl.semaphore_signal(barrier, inc=1, device_id={"pos": (pi + k) % n_pos}, device_id_type=MESH)
        for g in range(1, n_frame):
            pl.semaphore_signal(barrier, inc=1, device_id={"frame": (fi + g) % n_frame}, device_id_type=MESH)
        pl.semaphore_wait(barrier, n_pos - 1 + n_frame - 1)
        def spread(g):
            return pltpu.make_async_remote_copy(
                src_ref=x_ref.at[0, 0],
                dst_ref=z_ref.at[pi],
                send_sem=fsend_sem.at[g],
                recv_sem=frecv_sem,
                device_id={"frame": g},
                device_id_type=MESH,
            )

        @pl.when(fi == 0)
        def _():
            for g in range(1, n_frame):
                spread(g).start()

        copies = []
        for k in range(1, n_pos):
            peer = (pi + k) % n_pos
            copy = pltpu.make_async_remote_copy(
                src_ref=x_ref.at[peer],
                dst_ref=o_ref.at[pi],
                send_sem=send_sem.at[k],
                recv_sem=recv_sem.at[k],
                device_id={"pos": peer},
                device_id_type=MESH,
            )
            copy.start()
            copies.append(copy)

        @pl.when(fi == 0)
        def _():
            local = pltpu.make_async_copy(x_ref.at[0, 0], z_ref.at[pi], local_sem)
            local.start()
            local.wait()

        @pl.when(fi != 0)
        def _():
            spread(1).wait_recv()

        for k in range(1, n_pos):
            peer = (pi + k) % n_pos
            copy = pltpu.make_async_remote_copy(
                src_ref=z_ref.at[pi],
                dst_ref=z_ref.at[pi],
                send_sem=zsend_sem.at[k],
                recv_sem=zrecv_sem.at[k],
                device_id={"pos": peer},
                device_id_type=MESH,
            )
            copy.start()
            copies.append(copy)

        @pl.when(fi == 0)
        def _():
            for g in range(1, n_frame):
                spread(g).wait_send()

        for copy in copies:
            copy.wait()
        o_ref[pi] = x_ref[pi]

    return pl.pallas_call(
        kernel,
        out_shape=(
            jax.ShapeDtypeStruct(x.shape, x.dtype),
            jax.ShapeDtypeStruct((n_pos, places, width), x.dtype),
        ),
        in_specs=[pl.BlockSpec(memory_space=pltpu.VMEM)],
        out_specs=(pl.BlockSpec(memory_space=pltpu.VMEM), pl.BlockSpec(memory_space=pltpu.VMEM)),
        scratch_shapes=[
            pltpu.SemaphoreType.DMA((n_pos,)),
            pltpu.SemaphoreType.DMA((n_pos,)),
            pltpu.SemaphoreType.DMA((n_frame,)),
            pltpu.SemaphoreType.DMA,
            pltpu.SemaphoreType.DMA((n_pos,)),
            pltpu.SemaphoreType.DMA((n_pos,)),
            pltpu.SemaphoreType.DMA,
        ],
        compiler_params=pltpu.CompilerParams(collective_id=cid, has_side_effects=True),
    )(x)


def spatial_attend(got_in, zero, gain, wq, wk, wv, out_w, rows, n_frame, n_pos, cid):
    _, frames, slab, width = got_in.shape
    places = n_pos * slab
    depth = width // HEADS
    scale = depth ** (-0.5)
    n_dev = n_frame * n_pos
    run = places // n_dev
    chunks = rows // run
    n_tiles = places // rows
    per_tile = rows // slab

    def kernel(x_ref, z_ref, g_ref, wq_ref, wkt_ref, wvt_ref, w_ref, o_ref,
               q_ref, kt_ref, vt_ref, made, got, send_sem, recv_sem):
        t = pl.program_id(0)
        fi = lax.axis_index("frame")
        pi = lax.axis_index("pos")
        me = fi * n_pos + pi
        barrier = pltpu.get_barrier_semaphore()
        contract = (((1,), (1,)), ((), ()))

        def normed_rows(values):
            wide = values.reshape(places, width).astype(jnp.float32)
            factor = lax.rsqrt(jnp.mean(wide * wide, axis=-1, keepdims=True) + 1e-06)
            return (wide * factor * g_ref[...]).astype(jnp.bfloat16)

        def channels_first(weight_t, values):
            return lax.dot_general(weight_t, values, contract, preferred_element_type=jnp.float32).astype(jnp.bfloat16)

        @pl.when(t == 0)
        def _():
            for k in range(1, n_dev):
                peer = (me + k) % n_dev
                pl.semaphore_signal(
                    barrier, inc=1, device_id={"frame": peer // n_pos, "pos": peer % n_pos}, device_id_type=MESH
                )
            wkt = wkt_ref[...].T
            wvt = wvt_ref[...].T
            normed_zero = normed_rows(z_ref[...])
            k_zero = channels_first(wkt, normed_zero)
            v_zero = channels_first(wvt, normed_zero)
            for f in range(frames):
                normed_one = normed_rows(x_ref[:, f])
                q_ref[f] = jnp.dot(normed_one, wq_ref[...], preferred_element_type=jnp.float32).astype(jnp.bfloat16)
                kt_ref[f, :, pl.ds(0, places)] = channels_first(wkt, normed_one)
                vt_ref[f, :, pl.ds(0, places)] = channels_first(wvt, normed_one)
                kt_ref[f, :, pl.ds(places, places)] = k_zero
                vt_ref[f, :, pl.ds(places, places)] = v_zero

        tt = (t + fi + pi) % n_tiles
        base = tt * chunks
        these = pl.ds(pl.multiple_of(tt * rows, rows), rows)
        for f in range(frames):
            acc = x_ref[pl.ds(tt * per_tile, per_tile), f].reshape(rows, width).astype(jnp.float32)
            for h in range(HEADS):
                part = pl.ds(h * depth, depth)
                qh = q_ref[f, these, part]
                scores = jnp.dot(qh, kt_ref[f, part, :], preferred_element_type=jnp.float32) * scale
                weights = jnp.exp(scores - jnp.max(scores, axis=-1, keepdims=True))
                totals = jnp.sum(weights, axis=-1, keepdims=True)
                summed = lax.dot_general(
                    weights.astype(jnp.bfloat16), vt_ref[f, part, :], contract, preferred_element_type=jnp.float32
                )
                attended = (summed / totals).astype(jnp.bfloat16)
                acc = acc + jnp.dot(attended, w_ref[part, :], preferred_element_type=jnp.float32)
            made[pl.ds(base, chunks), f] = acc.reshape(chunks, run, width).astype(made.dtype)

        @pl.when(t == 0)
        def _():
            pl.semaphore_wait(barrier, n_dev - 1)

        for i in range(chunks):
            gf = i % n_frame
            gp = (base + i) // n_frame

            @pl.when((gf == fi) & (gp == pi))
            def _():
                got[me] = made[base + i]

            @pl.when((gf != fi) | (gp != pi))
            def _():
                pltpu.make_async_remote_copy(
                    src_ref=made.at[base + i],
                    dst_ref=got.at[me],
                    send_sem=send_sem,
                    recv_sem=recv_sem,
                    device_id={"frame": gf, "pos": gp},
                    device_id_type=MESH,
                ).start()

        @pl.when(t == n_tiles - 1)
        def _():
            others = pltpu.make_async_copy(got.at[pl.ds(0, n_dev - 1)], got.at[pl.ds(1, n_dev - 1)], recv_sem)
            others.wait()
            sent = pltpu.make_async_copy(got.at[pl.ds(0, n_dev - 1)], got.at[pl.ds(1, n_dev - 1)], send_sem)
            sent.wait()
            o_ref[...] = got[...]

    fixed = lambda t: (0, 0)
    dtype = got_in.dtype
    return pl.pallas_call(
        kernel,
        out_shape=jax.ShapeDtypeStruct((n_dev, frames, run, width), dtype),
        grid=(n_tiles,),
        in_specs=[
            pl.BlockSpec(memory_space=pltpu.VMEM),
            pl.BlockSpec(memory_space=pltpu.VMEM),
            pl.BlockSpec((1, width), fixed),
            pl.BlockSpec((width, width), fixed),
            pl.BlockSpec((width, width), fixed),
            pl.BlockSpec((width, width), fixed),
            pl.BlockSpec((width, width), fixed),
        ],
        out_specs=pl.BlockSpec(memory_space=pltpu.VMEM),
        scratch_shapes=[
            pltpu.VMEM((frames, places, width), dtype),
            pltpu.VMEM((frames, width, 2 * places), dtype),
            pltpu.VMEM((frames, width, 2 * places), dtype),
            pltpu.VMEM((n_dev, frames, run, width), dtype),
            pltpu.VMEM((n_dev, frames, run, width), dtype),
            pltpu.SemaphoreType.DMA,
            pltpu.SemaphoreType.DMA,
        ],
        compiler_params=pltpu.CompilerParams(collective_id=cid, has_side_effects=True),
    )(got_in, zero, gain.reshape(1, width), wq, wk, wv, out_w)


def temporal_attend(x, gain, wq, wk, wv, out_w, n_frame, cid):
    every, run, width = x.shape
    depth = width // HEADS
    scale = depth ** (-0.5)
    frames = every // n_frame
    rows = every * run
    lanes = width // 128

    def kernel(x_ref, g_ref, wq_ref, wk_ref, wv_ref, w_ref, o_ref, xs, qs, ks, vs, made, got, send_sem, recv_sem):
        fi = lax.axis_index("frame")
        barrier = pltpu.get_barrier_semaphore()
        for k in range(1, n_frame):
            pl.semaphore_signal(barrier, inc=1, device_id={"frame": (fi + k) % n_frame}, device_id_type=MESH)

        wide = x_ref[...].astype(jnp.float32).reshape(rows, width)
        factor = lax.rsqrt(jnp.mean(wide * wide, axis=-1, keepdims=True) + 1e-06)
        normed_two = (wide * factor * g_ref[...]).astype(jnp.bfloat16)
        def keep(ref, values):
            for c in range(lanes):
                ref[c] = values[:, c * 128 : (c + 1) * 128]

        def gather(ref, p):
            place = pl.ds(p, every, stride=run)
            return jnp.concatenate([ref[c, place, :] for c in range(lanes)], axis=-1)

        keep(xs, wide)
        for ref, weight in ((qs, wq_ref), (ks, wk_ref), (vs, wv_ref)):
            projected = jnp.dot(normed_two, weight[...], preferred_element_type=jnp.float32)
            keep(ref, projected.astype(jnp.bfloat16).astype(jnp.float32))

        for p in range(run):
            q = gather(qs, p).astype(jnp.bfloat16)
            k = gather(ks, p).astype(jnp.bfloat16)
            v = gather(vs, p).astype(jnp.bfloat16)
            acc = gather(xs, p)
            for h in range(HEADS):
                part = slice(h * depth, (h + 1) * depth)
                contract = (((1,), (1,)), ((), ()))
                scores = lax.dot_general(q[:, part], k[:, part], contract, preferred_element_type=jnp.float32) * scale
                weights = jnp.exp(scores - jnp.max(scores, axis=-1, keepdims=True))
                totals = jnp.sum(weights, axis=-1, keepdims=True)
                summed = jnp.dot(weights.astype(jnp.bfloat16), v[:, part], preferred_element_type=jnp.float32)
                attended = (summed / totals).astype(jnp.bfloat16)
                acc = acc + jnp.dot(attended, w_ref[part, :], preferred_element_type=jnp.float32)
            made[p] = acc.astype(made.dtype)
            if p == 0:
                pl.semaphore_wait(barrier, n_frame - 1)
            for g in range(n_frame):
                @pl.when(g == fi)
                def _():
                    got[fi, p] = made[p, pl.ds(g * frames, frames)]

                @pl.when(g != fi)
                def _():
                    pltpu.make_async_remote_copy(
                        src_ref=made.at[p, pl.ds(g * frames, frames)],
                        dst_ref=got.at[fi, p],
                        send_sem=send_sem,
                        recv_sem=recv_sem,
                        device_id={"frame": g},
                        device_id_type=MESH,
                    ).start()

        others = pltpu.make_async_copy(got.at[pl.ds(0, n_frame - 1)], got.at[pl.ds(1, n_frame - 1)], recv_sem)
        others.wait()
        sent = pltpu.make_async_copy(got.at[pl.ds(0, n_frame - 1)], got.at[pl.ds(1, n_frame - 1)], send_sem)
        sent.wait()
        o_ref[...] = got[...]

    vmem = pl.BlockSpec(memory_space=pltpu.VMEM)
    return pl.pallas_call(
        kernel,
        out_shape=jax.ShapeDtypeStruct((n_frame, run, frames, width), x.dtype),
        in_specs=[vmem] * 6,
        out_specs=vmem,
        scratch_shapes=[
            pltpu.VMEM((lanes, rows, 128), jnp.float32),
            pltpu.VMEM((lanes, rows, 128), jnp.float32),
            pltpu.VMEM((lanes, rows, 128), jnp.float32),
            pltpu.VMEM((lanes, rows, 128), jnp.float32),
            pltpu.VMEM((run, every, width), x.dtype),
            pltpu.VMEM((n_frame, run, frames, width), x.dtype),
            pltpu.SemaphoreType.DMA,
            pltpu.SemaphoreType.DMA,
        ],
        compiler_params=pltpu.CompilerParams(collective_id=cid, has_side_effects=True),
    )(x, gain.reshape(1, width), wq, wk, wv, out_w)


def transposed(values, weight):
    result = jnp.einsum("...rc,cd->...dr", values, weight, preferred_element_type=jnp.float32)
    return result.astype(jnp.bfloat16)


def normed(values, gain):
    wide = values.astype(jnp.float32)
    factor = lax.rsqrt(jnp.mean(wide * wide, axis=-1, keepdims=True) + 1e-06)
    return (wide * factor * gain).astype(jnp.bfloat16)


def project(values, weight):
    flat = values.reshape(-1, values.shape[-1])
    result = jnp.dot(flat, weight, preferred_element_type=jnp.float32).astype(jnp.bfloat16)
    return result.reshape(values.shape[:-1] + (weight.shape[1],))


def heads_of(values):
    return values.reshape(values.shape[:-1] + (HEADS, values.shape[-1] // HEADS))


def softmax_attend(query, keys, vals, score_form, value_form, total_form):
    scale = query.shape[-1] ** (-0.5)
    scores = jnp.einsum(score_form, query, keys, preferred_element_type=jnp.float32) * scale
    weights = jnp.exp(scores - jnp.max(scores, axis=-1, keepdims=True))
    totals = jnp.sum(weights, axis=-1)
    summed = jnp.einsum(
        value_form, weights.astype(jnp.bfloat16), vals, preferred_element_type=jnp.float32
    )
    return summed / jnp.einsum(total_form, totals)[..., None]


def shards(
    latents,
    gain_one,
    query_one,
    key_one,
    value_one,
    out_one,
    gain_two,
    query_two,
    key_two,
    value_two,
    out_two,
):
    frames, places, width = latents.shape
    n_pos = lax.axis_size("pos")
    n_frame = lax.axis_size("frame")
    per = frames // n_pos
    got, zero = spatial_exchange(latents.reshape(n_pos, per, places, width), n_pos, n_frame, 1)
    got = spatial_attend(
        got, zero, gain_one, query_one, key_one, value_one, out_one,
        min(256, n_pos * places), n_frame, n_pos, 2,
    )
    all_places = n_pos * places
    run = all_places // (n_pos * n_frame)
    mid_t = got.reshape(n_frame * n_pos * per, run, width)
    got = temporal_attend(mid_t, gain_two, query_two, key_two, value_two, out_two, n_frame, 3)
    return got.transpose(2, 0, 1, 3).reshape(frames, places, width)


def solution(mesh):
    return jax.shard_map(
        shards,
        mesh=mesh,
        in_specs=(P("frame", "pos", None), P(), P(), P(), P(), P(), P(), P(), P(), P(), P()),
        out_specs=P("frame", "pos", None),
        check_vma=False,
    )
```
